512 devices in a mesh: tm: 32 (over z, x), frac: 16 (over y, core).
Axes of the slice: x: 4, y: 8, z: 8, core: 2. Of those that a mesh axis runs over, the one named last changes fastest.
Arguments:
- pressure0: float32 [64, 32, 128], P('frac'), may hold values from -6 to 6
- storage: float32 [64, 32, 128], P('frac'), may hold values from 0.1 to 1
- perm_base: float32 [64, 32, 128], P('frac'), may hold values from 0.2 to 5
- leakoff: float32 [64, 32, 128], P('frac'), may hold values from 0.5 to 2
- sources: float32 [32, 64, 32, 128], P('tm', 'frac'), may hold values from -6 to 6
- export_cells: int32 [4096], P('frac'), may hold values from 0 to 16383
- inter_local: int32 [16384], P('frac'), may hold values from 0 to 16383
- trace_source: int32 [16384], P('frac'), may hold values from 0 to 4095, as said below
- inter_trans: float32 [16384], P('frac'), may hold values from 0.5 to 4
- inter_count: int32 [16], P('frac'), may hold values from 1 to 1024, 8192 in all
Outputs:
- slice_pressure: float32 [32, 64, 32, 128], P('tm', 'frac')
The draws below stay inside these ranges and needn't reach their ends.
Inputs may be any that keep to these rules, and one draw needn't show every extreme that they name: An entry of frac index d names a slot of another frac index: trace_source // 256 differs from d. `inter_count`: the live entries of a frac index are its first ones; the largest count is 1024.
All inputs are finite; a program needn't handle non-finite values. No bound on the sum of `inter_count` on one device may be relied on, other than what follows from the above.
Results may differ from the reference program's by a relative error of at most 0.00002.
Values sent between devices are 32-bit elements; how exact they have to be, the bound alone decides.
A program may use at most 64 MiB of HBM per device.

```python
import math
import jax
import jax.numpy as jnp
import numpy as np
from jax import lax

F_DEV = 4
FROWS = 32
FCOLS = 128
FINE_STEPS = 4
SWEEPS = 8
COARSE_SWEEPS = 2
ITERS = 2
NE = 256
NI = 1024
CELLS_DEV = 16384
FRACS = 64
SLICES = 32
N_FRAC = 16


def draw_trace_source(key, part):
    total = N_FRAC * NI
    owner_key = jax.random.fold_in(key, 11)
    slot_key = jax.random.fold_in(key, 23)
    entry_index = jnp.arange(total, dtype=jnp.int32)
    home = entry_index // NI
    offset = jax.random.randint(owner_key, (total,), 1, N_FRAC, dtype=jnp.int32)
    owner = (home + offset) % N_FRAC
    within = jax.random.randint(slot_key, (total,), 0, NE, dtype=jnp.int32)
    return (owner * NE + within).astype(jnp.int32)


def with_ends(values, rng, least, top_value):
    index_at = [jax.random.randint(jax.random.fold_in(rng, axis), (), 0, length) for axis, length in enumerate(values.shape)]
    main_axis = values.shape.index(max(values.shape))
    neighbour = index_at[:main_axis] + [(index_at[main_axis] + 1) % values.shape[main_axis]] + index_at[main_axis + 1:]
    return values.at[tuple(index_at)].set(least).at[tuple(neighbour)].set(top_value)


def level_of(rng, extent, split, low, top_value):
    loudness, own = 1.0, jax.random.fold_in(rng, 6)
    for dim, shards_of in split:
        heights = jnp.exp(jax.random.uniform(jax.random.fold_in(own, dim), (shards_of,), jnp.float32, low / len(split), top_value / len(split)))
        loudness = loudness * jnp.repeat(heights, extent[dim] // shards_of).reshape([-1 if axis == dim else 1 for axis in range(len(extent))])
    return loudness


def length_profile(amount, total, limit, lean):
    portions = [(1 << 20) // math.isqrt(rank ** lean) + 1 for rank in range(2, amount + 1)]
    rest, holding = total - limit - (amount - 1), [1] * (amount - 1)
    while rest > 0:
        movable = [i for i in range(amount - 1) if holding[i] < limit]
        pool, remaining = sum([portions[i] for i in movable]), rest
        for i in movable:
            more = min(limit - holding[i], max(1, remaining * portions[i] // pool), rest)
            holding[i] = holding[i] + more
            rest = rest - more
    return np.array([limit] + holding)


def uneven(stream_key, number_of, total, limit, skew):
    if number_of == 2:
        one = jax.random.randint(stream_key, (), max(1, total - limit), min(limit, total - 1) + 1)
        return jnp.stack([one, total - one])
    tallies = jnp.asarray(length_profile(number_of, total, limit, skew), jnp.int32)
    pairs = (number_of - 1) // 2
    source_of, sink = tallies[1:1 + 2 * pairs:2], tallies[2:2 + 2 * pairs:2]
    margin = jnp.minimum(source_of - 1, limit - sink)
    passed = jax.random.randint(jax.random.fold_in(stream_key, 1), (pairs,), 0, 1 << 20) % (margin + 1)
    tallies = tallies.at[1:1 + 2 * pairs:2].set(source_of - passed).at[2:2 + 2 * pairs:2].set(sink + passed)
    return tallies[jax.random.permutation(jax.random.fold_in(stream_key, 2), number_of)]


def bell_draw(rng, extent, scale, reach, cuts=(), held_as=jnp.bfloat16):
    values = scale * jax.random.normal(rng, extent, jnp.float32)
    if cuts:
        values = values * level_of(rng, extent, cuts, -0.22, 0.18)
    return jnp.clip(values, -reach, reach).astype(held_as)


def setup_inputs(seed: int = 0) -> dict:
    key_list = jax.random.split(jax.random.key(seed), 11)
    return {
        "pressure0": bell_draw(key_list[0], (FRACS, FROWS, FCOLS), 1.0, 6.0, ((0, 16),), jnp.float32),
        "storage": jnp.clip(jnp.exp(math.log(1.0) - 2.3025851 * jax.random.uniform(key_list[1], (FRACS, FROWS, FCOLS), jnp.float32) ** level_of(key_list[1], (FRACS, FROWS, FCOLS), ((0, 16),), -0.2, 0.2)), 0.1, 1.0),
        "perm_base": jnp.clip(jnp.exp(math.log(5.0) - 3.218876 * jax.random.uniform(key_list[2], (FRACS, FROWS, FCOLS), jnp.float32) ** level_of(key_list[2], (FRACS, FROWS, FCOLS), ((0, 16),), -0.2, 0.2)), 0.2, 5.0),
        "leakoff": jnp.clip(jnp.exp(math.log(2.0) - 1.3862944 * jax.random.uniform(key_list[3], (FRACS, FROWS, FCOLS), jnp.float32) ** level_of(key_list[3], (FRACS, FROWS, FCOLS), ((0, 16),), -0.2, 0.2)), 0.5, 2.0),
        "sources": bell_draw(key_list[4], (SLICES, FRACS, FROWS, FCOLS), 1.0, 6.0, ((0, 32), (1, 16)), jnp.float32),
        "export_cells": with_ends(jax.random.randint(key_list[5], (N_FRAC * NE,), 0, CELLS_DEV), jax.random.fold_in(key_list[5], 1), 0, CELLS_DEV - 1).astype(jnp.int32),
        "inter_local": with_ends(jax.random.randint(key_list[6], (N_FRAC * NI,), 0, CELLS_DEV), jax.random.fold_in(key_list[6], 1), 0, CELLS_DEV - 1).astype(jnp.int32),
        "trace_source": draw_trace_source(jax.random.fold_in(key_list[10], 71), 0),
        "inter_trans": jnp.clip(jnp.exp(math.log(4.0) - 2.0794415 * jax.random.uniform(key_list[8], (N_FRAC * NI,), jnp.float32) ** level_of(key_list[8], (N_FRAC * NI,), ((0, 16),), -0.2, 0.2)), 0.5, 4.0),
        "inter_count": uneven(key_list[9], N_FRAC, N_FRAC * NI // 2, NI, 2).astype(jnp.int32),
    }


stress_factor = 0.15
fine_size = 0.25


def next_rows(array):
    return jnp.concatenate([array[:, 1:, :], jnp.zeros_like(array[:, :1, :])], axis=1)


def prev_rows(array):
    return jnp.concatenate([jnp.zeros_like(array[:, :1, :]), array[:, :-1, :]], axis=1)


def next_cols(array):
    return jnp.concatenate([array[:, :, 1:], jnp.zeros_like(array[:, :, :1])], axis=2)


def prev_cols(array):
    return jnp.concatenate([jnp.zeros_like(array[:, :, :1]), array[:, :, :-1]], axis=2)


def implicit(pressure, slice_source, step_size, sweeps, fields, couple):
    storage, perm_base, leakoff, tisum = fields
    permeability = perm_base * jnp.exp(stress_factor * pressure)
    row_index = lax.broadcasted_iota(jnp.int32, pressure.shape, 1)
    col_index = lax.broadcasted_iota(jnp.int32, pressure.shape, 2)
    face_rows = jnp.where(row_index < pressure.shape[1] - 1, 0.5 * (permeability + next_rows(permeability)), 0.0)
    face_cols = jnp.where(col_index < pressure.shape[2] - 1, 0.5 * (permeability + next_cols(permeability)), 0.0)
    storage_rate = storage / step_size
    diagonal_total = storage_rate + leakoff + face_rows + prev_rows(face_rows) + face_cols + prev_cols(face_cols)
    right_side = storage_rate * pressure + slice_source
    if couple is not None:
        diagonal_total = diagonal_total + tisum
        right_side = right_side + couple(pressure)

    def sweep(sweep_index, current):
        beside = face_rows * next_rows(current) + prev_rows(face_rows * current)
        beside = beside + face_cols * next_cols(current) + prev_cols(face_cols * current)
        return (right_side + beside) / diagonal_total

    return lax.fori_loop(0, sweeps, sweep, pressure)


def reference(pressure0, storage, perm_base, leakoff, sources, export_cells, inter_local, trace_source, inter_trans, inter_count):
    cells = F_DEV * FROWS * FCOLS
    slot_index = jnp.arange(N_FRAC * NE, dtype=jnp.int32)
    export_global = (slot_index // NE) * cells + export_cells
    remote_cell = export_global[trace_source]
    entry_index = jnp.arange(N_FRAC * NI, dtype=jnp.int32)
    local_cell = (entry_index // NI) * cells + inter_local
    live_entry = (entry_index % NI) < inter_count[entry_index // NI]
    weights = jnp.where(live_entry, inter_trans, jnp.zeros_like(inter_trans))
    tisum = jnp.zeros((FRACS * FROWS * FCOLS,), inter_trans.dtype).at[local_cell].add(weights).reshape(pressure0.shape)
    fields = (storage, perm_base, leakoff, tisum)

    def couple(current):
        flat_field = current.reshape(-1)
        remote_values = flat_field[remote_cell]
        return jnp.zeros_like(flat_field).at[local_cell].add(weights * remote_values).reshape(current.shape)

    def coarse(pressure, slice_source):
        return implicit(pressure, slice_source, fine_size * FINE_STEPS, COARSE_SWEEPS, fields, None)

    def fine(pressure, slice_source):
        for step_number in range(FINE_STEPS):
            pressure = implicit(pressure, slice_source, fine_size, SWEEPS, fields, couple)
        return pressure

    def chain(deltas):
        def advance(current, inputs):
            slice_source, correction = inputs
            following = coarse(current, slice_source) + correction
            return following, following

        final_state, states = lax.scan(advance, pressure0, (sources[:-1], deltas))
        return jnp.concatenate([pressure0[None], states], axis=0)

    states = chain(jnp.zeros_like(sources[:-1]))
    for iteration in range(ITERS):
        fine_ends = lax.map(lambda pair: fine(pair[0], pair[1]), (states[:-1], sources[:-1]))
        coarse_ends = lax.map(lambda pair: coarse(pair[0], pair[1]), (states[:-1], sources[:-1]))
        states = chain(fine_ends - coarse_ends)
    return states
```

```python
import functools

import jax
import jax.numpy as jnp
from jax import lax
from jax.experimental import pallas as pl
from jax.experimental.pallas import tpu as pltpu
from jax.sharding import PartitionSpec as P

FINE_STEPS = 4
SWEEPS = 8
COARSE_SWEEPS = 2
ITERS = 2
GROUP = 4

stress_factor = 0.15
fine_size = 0.25


def next_rows(v):
    return jnp.concatenate(
        [v[..., 1:, :, :], pltpu.roll(v[..., :1, :, :], 7, v.ndim - 2)], axis=v.ndim - 3
    )


def prev_rows(v):
    return jnp.concatenate(
        [pltpu.roll(v[..., 3:, :, :], 1, v.ndim - 2), v[..., :3, :, :]], axis=v.ndim - 3
    )


def next_cols(v):
    return pltpu.roll(v, 127, v.ndim - 1)


def prev_cols(v):
    return pltpu.roll(v, 1, v.ndim - 1)


def faces(pressure, perm):
    conductivity = perm * jnp.exp(stress_factor * pressure)
    shape = pressure.shape
    block = lax.broadcasted_iota(jnp.int32, shape, len(shape) - 3)
    sub = lax.broadcasted_iota(jnp.int32, shape, len(shape) - 2)
    lane = lax.broadcasted_iota(jnp.int32, shape, len(shape) - 1)
    row_half = jnp.where((block == 3) & (sub == 7), 0.0, 0.5)
    col_half = jnp.where(lane == 127, 0.0, 0.5)
    face_r = row_half * (conductivity + next_rows(conductivity))
    face_c = col_half * (conductivity + next_cols(conductivity))
    return face_r, prev_rows(face_r), face_c, prev_cols(face_c)


def sweep(v, base, weights):
    down, up, right, left = weights
    return base + (down * next_rows(v) + up * prev_rows(v)) + (
        right * next_cols(v) + left * prev_cols(v)
    )


def coarse(pressure, source, store, perm, leak):
    parts = faces(pressure, perm)
    inverse = 1.0 / (store + leak + (parts[0] + parts[1]) + (parts[2] + parts[3]))
    base = (store * pressure + source) * inverse
    weights = [part * inverse for part in parts]
    v = pressure
    for _ in range(COARSE_SWEEPS):
        v = sweep(v, base, weights)
    return v


def pick(table, lanes):
    return jnp.take_along_axis(table, lanes, axis=1, mode="promise_in_bounds")


def kernel(
    planes,
    peers,
    count_ref,
    pressure_ref,
    storage_ref,
    perm_ref,
    leak_ref,
    source_ref,
    export_ref,
    local_ref,
    trace_ref,
    trans_ref,
    out_ref,
    start,
    store,
    perm,
    leak,
    tisum,
    own_source,
    source_in,
    u_out,
    u_in,
    f_out,
    f_in,
    edge_in,
    edge_out,
    coarse_old,
    shared,
    field,
    row_hot,
    lane_hot,
    export_lane,
    export_code,
    trace_lane,
    trace_row,
    weight,
    source_send,
    source_recv,
    u_send,
    u_recv,
    f_send,
    f_recv,
    edge_send,
    edge_recv,
    share_send,
    share_recv,
):
    slice_index = lax.axis_index("tm")
    me = lax.axis_index("frac")
    plane = slice_index // GROUP
    column = slice_index % GROUP
    others = sorted(range(1, peers), key=lambda d: -min(d, peers - d))

    barrier = pltpu.get_barrier_semaphore()
    for d in others:
        pl.semaphore_signal(
            barrier, inc=1, device_id={"tm": slice_index, "frac": (me + d) % peers}
        )
    for d in range(1, GROUP):
        pl.semaphore_signal(
            barrier,
            inc=1,
            device_id={"tm": plane * GROUP + (column + d) % GROUP, "frac": me},
        )

    for d in (1, planes - 1):
        pl.semaphore_signal(
            barrier,
            inc=1,
            device_id={"tm": (plane + d) % planes * GROUP + column, "frac": me},
        )

    for f in range(GROUP):
        for r in range(4):
            rows = pl.ds(f * 32 + r, 8, stride=4)
            start[f, r] = pressure_ref[rows, :]
            store[f, r] = storage_ref[rows, :]
            perm[f, r] = perm_ref[rows, :]
            leak[f, r] = leak_ref[rows, :]
            own_source[f, r] = source_ref[rows, :]

    sub8 = lax.broadcasted_iota(jnp.int32, (8, 128), 0)
    lane8 = lax.broadcasted_iota(jnp.int32, (8, 128), 1)
    for g in range(2):
        cell = jnp.broadcast_to(export_ref[g : g + 1, :], (8, 128))
        row = (cell >> 7) & 31
        export_lane[g] = cell & 127
        export_code[g] = jnp.where((row >> 2) == sub8, (cell >> 12) * 4 + (row & 3), -1)
    slot = trace_ref[...]
    trace_lane[...] = slot & 127
    trace_row[...] = slot >> 7
    live = (sub8 * 128 + lane8) < count_ref[0]
    weight[...] = jnp.where(live, trans_ref[...], 0.0)
    cell = local_ref[...]
    cell_row = (cell >> 7) & 31
    code = (cell >> 12) * 32 + (cell_row & 3) * 8 + (cell_row >> 2)
    cell_lane = cell & 127
    number = lax.broadcasted_iota(jnp.int32, (128, 128), 0)
    for t in range(8):
        rows_t = jnp.broadcast_to(code[t : t + 1, :], (128, 128))
        row_hot[t] = jnp.where(rows_t == number, 1.0, 0.0).astype(jnp.bfloat16)
        lanes_t = jnp.broadcast_to(cell_lane[t : t + 1, :], (128, 128))
        hot = jnp.where(lanes_t == number, 1.0, 0.0)
        lane_hot[t * 128 : (t + 1) * 128, :] = hot.T.astype(jnp.bfloat16)

    def scatter(parts):
        total = jnp.zeros((128 * len(parts), 128), jnp.float32)
        for p in range(4):
            stacked = []
            for part in parts:
                pieces = []
                for t in (2 * p, 2 * p + 1):
                    line = jnp.broadcast_to(part[t : t + 1, :], (16, 128)).astype(jnp.bfloat16)
                    block = row_hot[t].reshape(8, 16, 128) * line[None]
                    pieces.append(block.reshape(128, 128))
                stacked.append(jnp.concatenate(pieces, axis=1))
            left = jnp.concatenate(stacked, axis=0)
            right = lane_hot[p * 256 : (p + 1) * 256, :]
            total = total + jnp.dot(left, right, preferred_element_type=jnp.float32)
        result = total[:128]
        for n in range(1, len(parts)):
            result = result + total[n * 128 : (n + 1) * 128]
        return result.reshape(GROUP, 4, 8, 128)

    def terms(value, number_of):
        parts = []
        for _ in range(number_of):
            part = value.astype(jnp.bfloat16).astype(jnp.float32)
            parts.append(part)
            value = value - part
        return parts

    tisum[...] = scatter(terms(weight[...], 3))

    pl.semaphore_wait(barrier, peers - 1 + GROUP - 1 + 2)

    def source_copy(target):
        return pltpu.make_async_remote_copy(
            src_ref=own_source.at[target],
            dst_ref=source_in.at[column],
            send_sem=source_send.at[target],
            recv_sem=source_recv.at[column],
            device_id={"tm": plane * GROUP + target, "frac": me},
        )

    def source_arrival(origin):
        return pltpu.make_async_remote_copy(
            src_ref=own_source.at[origin],
            dst_ref=source_in.at[origin],
            send_sem=source_send.at[origin],
            recv_sem=source_recv.at[origin],
            device_id={"tm": plane * GROUP + origin, "frac": me},
        )

    def u_copy(k, target):
        return pltpu.make_async_remote_copy(
            src_ref=u_out.at[k, target],
            dst_ref=u_in.at[k, column],
            send_sem=u_send.at[k, target],
            recv_sem=u_recv.at[k, column],
            device_id={"tm": plane * GROUP + target, "frac": me},
        )

    def u_arrival(k, origin):
        return pltpu.make_async_remote_copy(
            src_ref=u_out.at[k, origin],
            dst_ref=u_in.at[k, origin],
            send_sem=u_send.at[k, origin],
            recv_sem=u_recv.at[k, origin],
            device_id={"tm": plane * GROUP + origin, "frac": me},
        )

    def f_copy(k, target):
        return pltpu.make_async_remote_copy(
            src_ref=f_out.at[k, target],
            dst_ref=f_in.at[k, column],
            send_sem=f_send.at[k, target],
            recv_sem=f_recv.at[k, column],
            device_id={"tm": plane * GROUP + target, "frac": me},
        )

    def f_arrival(k, origin):
        return pltpu.make_async_remote_copy(
            src_ref=f_out.at[k, origin],
            dst_ref=f_in.at[k, origin],
            send_sem=f_send.at[k, origin],
            recv_sem=f_recv.at[k, origin],
            device_id={"tm": plane * GROUP + origin, "frac": me},
        )

    def edge_copy(k, target):
        return pltpu.make_async_remote_copy(
            src_ref=edge_out.at[k],
            dst_ref=edge_in.at[k],
            send_sem=edge_send.at[k],
            recv_sem=edge_recv.at[k],
            device_id={"tm": target, "frac": me},
        )

    def share_copy(m, target):
        return pltpu.make_async_remote_copy(
            src_ref=shared.at[m, me],
            dst_ref=shared.at[m, me],
            send_sem=share_send.at[m],
            recv_sem=share_recv.at[m],
            device_id={"tm": slice_index, "frac": target},
        )

    def share_all(m):
        return pltpu.make_async_remote_copy(
            src_ref=shared.at[m, pl.ds(0, peers - 1)],
            dst_ref=shared.at[m, pl.ds(0, peers - 1)],
            send_sem=share_send.at[m],
            recv_sem=share_recv.at[m],
            device_id={"tm": slice_index, "frac": (me + 1) % peers},
        )

    for d in range(1, GROUP):
        source_copy((column + d) % GROUP).start()
    source_in[column] = own_source[column]

    def chain(k, first):
        @pl.when(plane > 0)
        def _():
            edge_copy(k, slice_index - GROUP).wait_recv()

        @pl.when(plane == 0)
        def _():
            edge_in[k] = start[column]

        u = edge_in[k]
        for j in range(GROUP):
            u_out[k, j] = u

            @pl.when(column != j)
            def _():
                u_copy(k, j).start()
                if first:
                    source_arrival(j).wait_recv()
                else:
                    f_arrival(k - 1, j).wait_recv()

            following = coarse(u, source_in[j], store[column], perm[column], leak[column])
            if first:
                u = following
            else:
                u = following + (f_in[k - 1, j] - coarse_old[j])
            coarse_old[j] = following
        edge_out[k] = u

        @pl.when(plane < planes - 1)
        def _():
            edge_copy(k, slice_index + GROUP).start()

        u_in[k, column] = u_out[k, column]
        for d in range(1, GROUP):
            u_arrival(k, (column + d) % GROUP).wait_recv()

    def fine(k):
        field[...] = u_in[k]

        def step(t, carry):
            m = k * FINE_STEPS + t
            q = field[...]
            for g in range(2):
                lanes, codes = export_lane[g], export_code[g]
                found = jnp.zeros((8, 128), jnp.float32)
                for n in range(4 * GROUP):
                    found = jnp.where(codes == n, pick(q[n // 4, n % 4], lanes), found)
                shared[m, me, g : g + 1, :] = jnp.sum(found, axis=0, keepdims=True)
            for d in others:
                share_copy(m, (me + d) % peers).start()

            parts = faces(q, perm[...])
            rate = store[...] * (1.0 / fine_size)
            total = rate + leak[...] + tisum[...] + (parts[0] + parts[1]) + (parts[2] + parts[3])
            inverse = 1.0 / total
            base = (rate * q + own_source[...]) * inverse
            weights = [part * inverse for part in parts]

            share_all(m).wait_recv()
            rows = trace_row[...]
            lanes = trace_lane[...]
            value = jnp.zeros((8, 128), jnp.float32)
            for n in range(2 * peers):
                line = jnp.broadcast_to(shared[m, n // 2, n % 2 : n % 2 + 1, :], (8, 128))
                value = jnp.where(rows == n, pick(line, lanes), value)
            base = base + scatter(terms(weight[...] * value, 2)) * inverse
            v = q
            for _ in range(SWEEPS):
                v = sweep(v, base, weights)
            field[...] = v
            return carry

        lax.fori_loop(0, FINE_STEPS, step, 0)
        f_out[k] = field[...]
        for d in range(1, GROUP):
            f_copy(k, (column + d) % GROUP).start()
        f_in[k, column] = f_out[k, column]

    chain(0, True)

    def iteration(k, carry):
        fine(k)
        chain(k + 1, False)
        return carry

    lax.fori_loop(0, ITERS, iteration, 0)

    for f in range(GROUP):
        for r in range(4):
            out_ref[pl.ds(f * 32 + r, 8, stride=4), :] = u_in[ITERS, f, r]

    for d in range(1, GROUP):
        other = (column + d) % GROUP
        source_copy(other).wait_send()
        for k in range(ITERS + 1):
            u_copy(k, other).wait_send()
        for k in range(ITERS):
            f_copy(k, other).wait_send()

    @pl.when(plane < planes - 1)
    def _():
        for k in range(ITERS + 1):
            edge_copy(k, slice_index + GROUP).wait_send()

    for m in range(ITERS * FINE_STEPS):
        share_all(m).wait_send()


def body(
    pressure0,
    storage,
    perm_base,
    leakoff,
    sources,
    export_cells,
    inter_local,
    trace_source,
    inter_trans,
    inter_count,
):
    planes = lax.axis_size("tm") // GROUP
    peers = lax.axis_size("frac")
    flat = lambda a: a.reshape(128, 128)
    vmem = pl.BlockSpec(memory_space=pltpu.VMEM)
    f32 = jnp.float32
    block = (4, 8, 128)
    whole = (GROUP,) + block
    shares = ITERS * FINE_STEPS
    out = pl.pallas_call(
        functools.partial(kernel, planes, peers),
        out_shape=jax.ShapeDtypeStruct((128, 128), f32),
        in_specs=[pl.BlockSpec(memory_space=pltpu.SMEM)] + [vmem] * 9,
        out_specs=vmem,
        scratch_shapes=[
            pltpu.VMEM(whole, f32),
            pltpu.VMEM(whole, f32),
            pltpu.VMEM(whole, f32),
            pltpu.VMEM(whole, f32),
            pltpu.VMEM(whole, f32),
            pltpu.VMEM(whole, f32),
            pltpu.VMEM(whole, f32),
            pltpu.VMEM((ITERS + 1,) + whole, f32),
            pltpu.VMEM((ITERS + 1,) + whole, f32),
            pltpu.VMEM((ITERS,) + whole, f32),
            pltpu.VMEM((ITERS,) + whole, f32),
            pltpu.VMEM((ITERS + 1,) + block, f32),
            pltpu.VMEM((ITERS + 1,) + block, f32),
            pltpu.VMEM(whole, f32),
            pltpu.VMEM((shares, peers, 2, 128), f32),
            pltpu.VMEM(whole, f32),
            pltpu.VMEM((8, 128, 128), jnp.bfloat16),
            pltpu.VMEM((1024, 128), jnp.bfloat16),
            pltpu.VMEM((2, 8, 128), jnp.int32),
            pltpu.VMEM((2, 8, 128), jnp.int32),
            pltpu.VMEM((8, 128), jnp.int32),
            pltpu.VMEM((8, 128), jnp.int32),
            pltpu.VMEM((8, 128), f32),
            pltpu.SemaphoreType.DMA((GROUP,)),
            pltpu.SemaphoreType.DMA((GROUP,)),
            pltpu.SemaphoreType.DMA((ITERS + 1, GROUP)),
            pltpu.SemaphoreType.DMA((ITERS + 1, GROUP)),
            pltpu.SemaphoreType.DMA((ITERS, GROUP)),
            pltpu.SemaphoreType.DMA((ITERS, GROUP)),
            pltpu.SemaphoreType.DMA((ITERS + 1,)),
            pltpu.SemaphoreType.DMA((ITERS + 1,)),
            pltpu.SemaphoreType.DMA((shares,)),
            pltpu.SemaphoreType.DMA((shares,)),
        ],
        compiler_params=pltpu.CompilerParams(collective_id=0, has_side_effects=True),
        name="parareal",
    )(
        inter_count,
        flat(pressure0),
        flat(storage),
        flat(perm_base),
        flat(leakoff),
        flat(sources),
        export_cells.reshape(2, 128),
        inter_local.reshape(8, 128),
        trace_source.reshape(8, 128),
        inter_trans.reshape(8, 128),
    )
    return out.reshape(sources.shape)


def solution(mesh):
    placed = (
        P("frac", None, None),
        P("frac", None, None),
        P("frac", None, None),
        P("frac", None, None),
        P("tm", "frac", None, None),
        P("frac"),
        P("frac"),
        P("frac"),
        P("frac"),
        P("frac"),
    )
    return jax.shard_map(
        body, mesh=mesh, in_specs=placed, out_specs=P("tm", "frac", None, None), check_vma=False
    )
```

```python
import functools

import jax
import jax.numpy as jnp
from jax import lax
from jax.experimental import pallas as pl
from jax.experimental.pallas import tpu as pltpu
from jax.sharding import PartitionSpec as P

FINE_STEPS = 4
SWEEPS = 8
COARSE_SWEEPS = 2
ITERS = 2
GROUP = 4

stress_factor = 0.15
fine_size = 0.25


def next_rows(v):
    return jnp.concatenate(
        [v[..., 1:, :, :], pltpu.roll(v[..., :1, :, :], 7, v.ndim - 2)], axis=v.ndim - 3
    )


def prev_rows(v):
    return jnp.concatenate(
        [pltpu.roll(v[..., 3:, :, :], 1, v.ndim - 2), v[..., :3, :, :]], axis=v.ndim - 3
    )


def next_cols(v):
    return pltpu.roll(v, 127, v.ndim - 1)


def prev_cols(v):
    return pltpu.roll(v, 1, v.ndim - 1)


def faces(pressure, perm):
    conductivity = perm * jnp.exp(stress_factor * pressure)
    shape = pressure.shape
    block = lax.broadcasted_iota(jnp.int32, shape, len(shape) - 3)
    sub = lax.broadcasted_iota(jnp.int32, shape, len(shape) - 2)
    lane = lax.broadcasted_iota(jnp.int32, shape, len(shape) - 1)
    row_half = jnp.where((block == 3) & (sub == 7), 0.0, 0.5)
    col_half = jnp.where(lane == 127, 0.0, 0.5)
    face_r = row_half * (conductivity + next_rows(conductivity))
    face_c = col_half * (conductivity + next_cols(conductivity))
    return face_r, prev_rows(face_r), face_c, prev_cols(face_c)


def sweep(v, base, weights):
    down, up, right, left = weights
    return base + (down * next_rows(v) + up * prev_rows(v)) + (
        right * next_cols(v) + left * prev_cols(v)
    )


def coarse(pressure, source, store, perm, leak):
    parts = faces(pressure, perm)
    inverse = 1.0 / (store + leak + (parts[0] + parts[1]) + (parts[2] + parts[3]))
    base = (store * pressure + source) * inverse
    weights = [part * inverse for part in parts]
    v = pressure
    for _ in range(COARSE_SWEEPS):
        v = sweep(v, base, weights)
    return v


def pick(table, lanes):
    return jnp.take_along_axis(table, lanes, axis=1, mode="promise_in_bounds")


def kernel(
    planes,
    peers,
    count_ref,
    pressure_hbm,
    storage_hbm,
    perm_hbm,
    leak_hbm,
    source_hbm,
    export_hbm,
    local_hbm,
    trace_hbm,
    trans_hbm,
    out_ref,
    pressure_ref,
    storage_ref,
    perm_ref,
    leak_ref,
    source_ref,
    export_ref,
    local_ref,
    trace_ref,
    trans_ref,
    start,
    store,
    perm,
    leak,
    tisum,
    own_source,
    source_in,
    u_out,
    u_in,
    f_out,
    f_in,
    edge_in,
    edge_out,
    coarse_old,
    shared,
    field,
    row_hot,
    lane_hot,
    export_lane,
    export_code,
    trace_lane,
    trace_row,
    weight,
    fetched,
    source_send,
    source_recv,
    u_send,
    u_recv,
    f_send,
    f_recv,
    edge_send,
    edge_recv,
    share_send,
    share_recv,
):
    slice_index = lax.axis_index("tm")
    me = lax.axis_index("frac")
    plane = slice_index // GROUP
    column = slice_index % GROUP
    others = sorted(range(1, peers), key=lambda d: -min(d, peers - d))

    barrier = pltpu.get_barrier_semaphore()
    for d in others:
        pl.semaphore_signal(
            barrier, inc=1, device_id={"tm": slice_index, "frac": (me + d) % peers}
        )
    for d in range(1, GROUP):
        pl.semaphore_signal(
            barrier,
            inc=1,
            device_id={"tm": plane * GROUP + (column + d) % GROUP, "frac": me},
        )

    for d in (1, 2, planes - 2, planes - 1):
        pl.semaphore_signal(
            barrier,
            inc=1,
            device_id={"tm": (plane + d) % planes * GROUP + column, "frac": me},
        )
    for d in range(1, GROUP):
        for p in (1, planes - 1):
            pl.semaphore_signal(
                barrier,
                inc=1,
                device_id={
                    "tm": (plane + p) % planes * GROUP + (column + d) % GROUP,
                    "frac": me,
                },
            )

    pairs = (
        (source_hbm, source_ref),
        (pressure_hbm, pressure_ref),
        (storage_hbm, storage_ref),
        (perm_hbm, perm_ref),
        (leak_hbm, leak_ref),
        (export_hbm, export_ref),
        (local_hbm, local_ref),
        (trace_hbm, trace_ref),
        (trans_hbm, trans_ref),
    )
    fetches = [
        pltpu.make_async_copy(origin, target, fetched.at[n])
        for n, (origin, target) in enumerate(pairs)
    ]
    for fetch in fetches:
        fetch.start()
    for fetch in fetches:
        fetch.wait()

    for f in range(GROUP):
        for r in range(4):
            rows = pl.ds(f * 32 + r, 8, stride=4)
            start[f, r] = pressure_ref[rows, :]
            store[f, r] = storage_ref[rows, :]
            perm[f, r] = perm_ref[rows, :]
            leak[f, r] = leak_ref[rows, :]
            own_source[f, r] = source_ref[rows, :]

    sub8 = lax.broadcasted_iota(jnp.int32, (8, 128), 0)
    lane8 = lax.broadcasted_iota(jnp.int32, (8, 128), 1)
    for g in range(2):
        cell = jnp.broadcast_to(export_ref[g : g + 1, :], (8, 128))
        row = (cell >> 7) & 31
        export_lane[g] = cell & 127
        export_code[g] = jnp.where((row >> 2) == sub8, (cell >> 12) * 4 + (row & 3), -1)
    slot = trace_ref[...]
    trace_lane[...] = slot & 127
    trace_row[...] = slot >> 7
    live = (sub8 * 128 + lane8) < count_ref[0]
    weight[...] = jnp.where(live, trans_ref[...], 0.0)
    cell = local_ref[...]
    cell_row = (cell >> 7) & 31
    code = (cell >> 12) * 32 + (cell_row & 3) * 8 + (cell_row >> 2)
    cell_lane = cell & 127
    number = lax.broadcasted_iota(jnp.int32, (128, 128), 0)
    for t in range(8):
        rows_t = jnp.broadcast_to(code[t : t + 1, :], (128, 128))
        row_hot[t] = jnp.where(rows_t == number, 1.0, 0.0).astype(jnp.bfloat16)
        lanes_t = jnp.broadcast_to(cell_lane[t : t + 1, :], (128, 128))
        hot = jnp.where(lanes_t == number, 1.0, 0.0)
        lane_hot[t * 128 : (t + 1) * 128, :] = hot.T.astype(jnp.bfloat16)

    def scatter(parts):
        total = jnp.zeros((128 * len(parts), 128), jnp.float32)
        for p in range(4):
            stacked = []
            for part in parts:
                pieces = []
                for t in (2 * p, 2 * p + 1):
                    line = jnp.broadcast_to(part[t : t + 1, :], (16, 128)).astype(jnp.bfloat16)
                    block = row_hot[t].reshape(8, 16, 128) * line[None]
                    pieces.append(block.reshape(128, 128))
                stacked.append(jnp.concatenate(pieces, axis=1))
            left = jnp.concatenate(stacked, axis=0)
            right = lane_hot[p * 256 : (p + 1) * 256, :]
            total = total + jnp.dot(left, right, preferred_element_type=jnp.float32)
        result = total[:128]
        for n in range(1, len(parts)):
            result = result + total[n * 128 : (n + 1) * 128]
        return result.reshape(GROUP, 4, 8, 128)

    def terms(value, number_of):
        parts = []
        for _ in range(number_of):
            part = value.astype(jnp.bfloat16).astype(jnp.float32)
            parts.append(part)
            value = value - part
        return parts

    tisum[...] = scatter(terms(weight[...], 3))

    pl.semaphore_wait(barrier, peers - 1 + GROUP - 1 + 4 + 2 * (GROUP - 1))

    def source_copy(ahead, target):
        slot = (1 - ahead) * GROUP + column
        return pltpu.make_async_remote_copy(
            src_ref=own_source.at[target],
            dst_ref=source_in.at[slot],
            send_sem=source_send.at[ahead, target],
            recv_sem=source_recv.at[slot],
            device_id={"tm": (plane + ahead) * GROUP + target, "frac": me},
        )

    def source_arrival(slot):
        return pltpu.make_async_remote_copy(
            src_ref=own_source.at[0],
            dst_ref=source_in.at[slot],
            send_sem=source_send.at[0, 0],
            recv_sem=source_recv.at[slot],
            device_id={"tm": plane * GROUP + (column + 1) % GROUP, "frac": me},
        )

    def u_copy(k, target):
        return pltpu.make_async_remote_copy(
            src_ref=u_out.at[k, target],
            dst_ref=u_in.at[k, column],
            send_sem=u_send.at[k, target],
            recv_sem=u_recv.at[k, column],
            device_id={"tm": plane * GROUP + target, "frac": me},
        )

    def u_arrival(k, origin):
        return pltpu.make_async_remote_copy(
            src_ref=u_out.at[k, origin],
            dst_ref=u_in.at[k, origin],
            send_sem=u_send.at[k, origin],
            recv_sem=u_recv.at[k, origin],
            device_id={"tm": plane * GROUP + origin, "frac": me},
        )

    def f_copy(k, ahead, target):
        slot = (1 - ahead) * GROUP + column
        return pltpu.make_async_remote_copy(
            src_ref=f_out.at[k, target],
            dst_ref=f_in.at[k, slot],
            send_sem=f_send.at[k, ahead, target],
            recv_sem=f_recv.at[k, slot],
            device_id={"tm": (plane + ahead) * GROUP + target, "frac": me},
        )

    def f_arrival(k, slot):
        return pltpu.make_async_remote_copy(
            src_ref=f_out.at[k, 0],
            dst_ref=f_in.at[k, slot],
            send_sem=f_send.at[k, 0, 0],
            recv_sem=f_recv.at[k, slot],
            device_id={"tm": plane * GROUP + (column + 1) % GROUP, "frac": me},
        )

    def edge_copy(k, target):
        return pltpu.make_async_remote_copy(
            src_ref=edge_out.at[k],
            dst_ref=edge_in.at[k],
            send_sem=edge_send.at[k],
            recv_sem=edge_recv.at[k],
            device_id={"tm": target, "frac": me},
        )

    def share_copy(m, target):
        return pltpu.make_async_remote_copy(
            src_ref=shared.at[m, me],
            dst_ref=shared.at[m, me],
            send_sem=share_send.at[m],
            recv_sem=share_recv.at[m],
            device_id={"tm": slice_index, "frac": target},
        )

    def share_all(m):
        return pltpu.make_async_remote_copy(
            src_ref=shared.at[m, pl.ds(0, peers - 1)],
            dst_ref=shared.at[m, pl.ds(0, peers - 1)],
            send_sem=share_send.at[m],
            recv_sem=share_recv.at[m],
            device_id={"tm": slice_index, "frac": (me + 1) % peers},
        )

    @pl.when(plane < planes - 1)
    def _():
        for d in (2, 1, 3, 0):
            source_copy(1, (column + d) % GROUP).start()

    for d in (2, 1, 3):
        source_copy(0, (column + d) % GROUP).start()
    source_in[GROUP + column] = own_source[column]

    def advance(k, first, slot, u):
        following = coarse(u, source_in[slot], store[column], perm[column], leak[column])
        if first:
            u = following
        else:
            u = following + (f_in[k - 1, slot] - coarse_old[slot])
        coarse_old[slot] = following
        return u

    def arrival(k, first, slot):
        if first:
            source_arrival(slot).wait_recv()
        else:
            f_arrival(k - 1, slot).wait_recv()

    def chain(k, first):
        @pl.when(plane > 1)
        def _():
            edge_copy(k, slice_index - 2 * GROUP).wait_recv()

        @pl.when(plane <= 1)
        def _():
            edge_in[k] = start[column]

        @pl.when(plane > 0)
        def _():
            u = edge_in[k]
            for j in range(GROUP):
                arrival(k, first, j)
                u = advance(k, first, j, u)
            edge_in[k] = u

        u = edge_in[k]
        for j in range(GROUP):
            u_out[k, j] = u

            @pl.when(column != j)
            def _():
                u_copy(k, j).start()
                arrival(k, first, GROUP + j)

            u = advance(k, first, GROUP + j, u)
        edge_out[k] = u

        @pl.when(plane < planes - 2)
        def _():
            edge_copy(k, slice_index + 2 * GROUP).start()

        u_in[k, column] = u_out[k, column]
        for d in range(1, GROUP):
            u_arrival(k, (column + d) % GROUP).wait_recv()

    def fine(k):
        field[...] = u_in[k]

        def step(t, carry):
            m = k * FINE_STEPS + t
            q = field[...]
            for g in range(2):
                lanes, codes = export_lane[g], export_code[g]
                found = jnp.zeros((8, 128), jnp.float32)
                for n in range(4 * GROUP):
                    found = jnp.where(codes == n, pick(q[n // 4, n % 4], lanes), found)
                shared[m, me, g : g + 1, :] = jnp.sum(found, axis=0, keepdims=True)
            for d in others:
                share_copy(m, (me + d) % peers).start()

            parts = faces(q, perm[...])
            rate = store[...] * (1.0 / fine_size)
            total = rate + leak[...] + tisum[...] + (parts[0] + parts[1]) + (parts[2] + parts[3])
            inverse = 1.0 / total
            base = (rate * q + own_source[...]) * inverse
            weights = [part * inverse for part in parts]

            share_all(m).wait_recv()
            rows = trace_row[...]
            lanes = trace_lane[...]
            value = jnp.zeros((8, 128), jnp.float32)
            for n in range(2 * peers):
                line = jnp.broadcast_to(shared[m, n // 2, n % 2 : n % 2 + 1, :], (8, 128))
                value = jnp.where(rows == n, pick(line, lanes), value)
            base = base + scatter(terms(weight[...] * value, 2)) * inverse
            v = q
            for _ in range(SWEEPS):
                v = sweep(v, base, weights)
            field[...] = v
            return carry

        lax.fori_loop(0, FINE_STEPS, step, 0)
        f_out[k] = field[...]

        @pl.when(plane < planes - 1)
        def _():
            for d in (2, 1, 3, 0):
                f_copy(k, 1, (column + d) % GROUP).start()

        for d in (2, 1, 3):
            f_copy(k, 0, (column + d) % GROUP).start()
        f_in[k, GROUP + column] = f_out[k, column]

    chain(0, True)

    def iteration(k, carry):
        fine(k)
        chain(k + 1, False)
        return carry

    lax.fori_loop(0, ITERS, iteration, 0)

    for f in range(GROUP):
        for r in range(4):
            out_ref[pl.ds(f * 32 + r, 8, stride=4), :] = u_in[ITERS, f, r]

    for d in range(1, GROUP):
        other = (column + d) % GROUP
        source_copy(0, other).wait_send()
        for k in range(ITERS + 1):
            u_copy(k, other).wait_send()
        for k in range(ITERS):
            f_copy(k, 0, other).wait_send()

    @pl.when(plane < planes - 1)
    def _():
        for f in range(GROUP):
            source_copy(1, f).wait_send()
            for k in range(ITERS):
                f_copy(k, 1, f).wait_send()

    @pl.when(plane < planes - 2)
    def _():
        for k in range(ITERS + 1):
            edge_copy(k, slice_index + 2 * GROUP).wait_send()

    for m in range(ITERS * FINE_STEPS):
        share_all(m).wait_send()


def body(
    pressure0,
    storage,
    perm_base,
    leakoff,
    sources,
    export_cells,
    inter_local,
    trace_source,
    inter_trans,
    inter_count,
):
    planes = lax.axis_size("tm") // GROUP
    peers = lax.axis_size("frac")
    flat = lambda a: a.reshape(128, 128)
    vmem = pl.BlockSpec(memory_space=pltpu.VMEM)
    f32 = jnp.float32
    block = (4, 8, 128)
    whole = (GROUP,) + block
    shares = ITERS * FINE_STEPS
    slots = 2 * GROUP
    out = pl.pallas_call(
        functools.partial(kernel, planes, peers),
        out_shape=jax.ShapeDtypeStruct((128, 128), f32),
        in_specs=[pl.BlockSpec(memory_space=pltpu.SMEM)]
        + [pl.BlockSpec(memory_space=pl.ANY)] * 9,
        out_specs=vmem,
        scratch_shapes=[
            pltpu.VMEM((128, 128), f32),
            pltpu.VMEM((128, 128), f32),
            pltpu.VMEM((128, 128), f32),
            pltpu.VMEM((128, 128), f32),
            pltpu.VMEM((128, 128), f32),
            pltpu.VMEM((2, 128), jnp.int32),
            pltpu.VMEM((8, 128), jnp.int32),
            pltpu.VMEM((8, 128), jnp.int32),
            pltpu.VMEM((8, 128), f32),
            pltpu.VMEM(whole, f32),
            pltpu.VMEM(whole, f32),
            pltpu.VMEM(whole, f32),
            pltpu.VMEM(whole, f32),
            pltpu.VMEM(whole, f32),
            pltpu.VMEM(whole, f32),
            pltpu.VMEM((slots,) + block, f32),
            pltpu.VMEM((ITERS + 1,) + whole, f32),
            pltpu.VMEM((ITERS + 1,) + whole, f32),
            pltpu.VMEM((ITERS,) + whole, f32),
            pltpu.VMEM((ITERS, slots) + block, f32),
            pltpu.VMEM((ITERS + 1,) + block, f32),
            pltpu.VMEM((ITERS + 1,) + block, f32),
            pltpu.VMEM((slots,) + block, f32),
            pltpu.VMEM((shares, peers, 2, 128), f32),
            pltpu.VMEM(whole, f32),
            pltpu.VMEM((8, 128, 128), jnp.bfloat16),
            pltpu.VMEM((1024, 128), jnp.bfloat16),
            pltpu.VMEM((2, 8, 128), jnp.int32),
            pltpu.VMEM((2, 8, 128), jnp.int32),
            pltpu.VMEM((8, 128), jnp.int32),
            pltpu.VMEM((8, 128), jnp.int32),
            pltpu.VMEM((8, 128), f32),
            pltpu.SemaphoreType.DMA((9,)),
            pltpu.SemaphoreType.DMA((2, GROUP)),
            pltpu.SemaphoreType.DMA((slots,)),
            pltpu.SemaphoreType.DMA((ITERS + 1, GROUP)),
            pltpu.SemaphoreType.DMA((ITERS + 1, GROUP)),
            pltpu.SemaphoreType.DMA((ITERS, 2, GROUP)),
            pltpu.SemaphoreType.DMA((ITERS, slots)),
            pltpu.SemaphoreType.DMA((ITERS + 1,)),
            pltpu.SemaphoreType.DMA((ITERS + 1,)),
            pltpu.SemaphoreType.DMA((shares,)),
            pltpu.SemaphoreType.DMA((shares,)),
        ],
        compiler_params=pltpu.CompilerParams(
            collective_id=0, has_side_effects=True
        ),
        name="parareal",
    )(
        inter_count,
        flat(pressure0),
        flat(storage),
        flat(perm_base),
        flat(leakoff),
        flat(sources),
        export_cells.reshape(2, 128),
        inter_local.reshape(8, 128),
        trace_source.reshape(8, 128),
        inter_trans.reshape(8, 128),
    )
    return out.reshape(sources.shape)


def solution(mesh):
    placed = (
        P("frac", None, None),
        P("frac", None, None),
        P("frac", None, None),
        P("frac", None, None),
        P("tm", "frac", None, None),
        P("frac"),
        P("frac"),
        P("frac"),
        P("frac"),
        P("frac"),
    )
    return jax.shard_map(
        body, mesh=mesh, in_specs=placed, out_specs=P("tm", "frac", None, None), check_vma=False
    )
```

```python
import functools

import jax
import jax.numpy as jnp
from jax import lax
from jax.experimental import pallas as pl
from jax.experimental.pallas import tpu as pltpu
from jax.sharding import PartitionSpec as P

FINE_STEPS = 4
SWEEPS = 8
COARSE_SWEEPS = 2
ITERS = 2
GROUP = 4

stress_factor = 0.15
fine_size = 0.25


def next_rows(v):
    return jnp.concatenate(
        [v[..., 1:, :, :], pltpu.roll(v[..., :1, :, :], 7, v.ndim - 2)], axis=v.ndim - 3
    )


def prev_rows(v):
    return jnp.concatenate(
        [pltpu.roll(v[..., 3:, :, :], 1, v.ndim - 2), v[..., :3, :, :]], axis=v.ndim - 3
    )


def next_cols(v):
    return pltpu.roll(v, 127, v.ndim - 1)


def prev_cols(v):
    return pltpu.roll(v, 1, v.ndim - 1)


def faces(pressure, perm):
    conductivity = perm * jnp.exp(stress_factor * pressure)
    shape = pressure.shape
    block = lax.broadcasted_iota(jnp.int32, shape, len(shape) - 3)
    sub = lax.broadcasted_iota(jnp.int32, shape, len(shape) - 2)
    lane = lax.broadcasted_iota(jnp.int32, shape, len(shape) - 1)
    row_half = jnp.where((block == 3) & (sub == 7), 0.0, 0.5)
    col_half = jnp.where(lane == 127, 0.0, 0.5)
    face_r = row_half * (conductivity + next_rows(conductivity))
    face_c = col_half * (conductivity + next_cols(conductivity))
    return face_r, prev_rows(face_r), face_c, prev_cols(face_c)


def sweep(v, base, weights):
    down, up, right, left = weights
    return base + (down * next_rows(v) + up * prev_rows(v)) + (
        right * next_cols(v) + left * prev_cols(v)
    )


def coarse(pressure, source, store, perm, leak):
    parts = faces(pressure, perm)
    inverse = 1.0 / (store + leak + (parts[0] + parts[1]) + (parts[2] + parts[3]))
    base = (store * pressure + source) * inverse
    weights = [part * inverse for part in parts]
    v = pressure
    for _ in range(COARSE_SWEEPS):
        v = sweep(v, base, weights)
    return v


def pick(table, lanes):
    return jnp.take_along_axis(table, lanes, axis=1, mode="promise_in_bounds")


def kernel(
    planes,
    peers,
    count_ref,
    pressure_hbm,
    storage_hbm,
    perm_hbm,
    leak_hbm,
    source_hbm,
    export_hbm,
    local_hbm,
    trace_hbm,
    trans_hbm,
    out_ref,
    pressure_ref,
    storage_ref,
    perm_ref,
    leak_ref,
    source_ref,
    export_ref,
    local_ref,
    trace_ref,
    trans_ref,
    start,
    store,
    perm,
    leak,
    tisum,
    own_source,
    source_in,
    u_out,
    u_in,
    f_out,
    f_in,
    edge_in,
    edge_out,
    coarse_old,
    first_out,
    first_in,
    shared,
    gathered,
    field,
    row_hot,
    lane_hot,
    export_lane,
    export_code,
    trace_lane,
    trace_row,
    weight,
    fetched,
    source_send,
    source_recv,
    u_send,
    u_recv,
    f_send,
    f_recv,
    edge_send,
    edge_recv,
    first_send,
    first_recv,
    share_send,
    share_recv,
):
    slice_index = lax.axis_index("tm")
    me = lax.axis_index("frac")
    plane = slice_index // GROUP
    column = slice_index % GROUP
    others = sorted(range(1, peers), key=lambda d: -min(d, peers - d))

    barrier = pltpu.get_barrier_semaphore()
    for d in others:
        pl.semaphore_signal(
            barrier, inc=1, device_id={"tm": slice_index, "frac": (me + d) % peers}
        )
    for d in range(1, GROUP):
        pl.semaphore_signal(
            barrier,
            inc=1,
            device_id={"tm": plane * GROUP + (column + d) % GROUP, "frac": me},
        )

    for d in (1, 2, planes - 2, planes - 1):
        pl.semaphore_signal(
            barrier,
            inc=1,
            device_id={"tm": (plane + d) % planes * GROUP + column, "frac": me},
        )
    for d in range(1, GROUP):
        for p in (1, planes - 1):
            pl.semaphore_signal(
                barrier,
                inc=1,
                device_id={
                    "tm": (plane + p) % planes * GROUP + (column + d) % GROUP,
                    "frac": me,
                },
            )

    pairs = (
        (source_hbm, source_ref),
        (pressure_hbm, pressure_ref),
        (storage_hbm, storage_ref),
        (perm_hbm, perm_ref),
        (leak_hbm, leak_ref),
        (export_hbm, export_ref),
        (local_hbm, local_ref),
        (trace_hbm, trace_ref),
        (trans_hbm, trans_ref),
    )
    fetches = [
        pltpu.make_async_copy(origin, target, fetched.at[n])
        for n, (origin, target) in enumerate(pairs)
    ]
    for fetch in fetches:
        fetch.start()
    for fetch in fetches:
        fetch.wait()

    for f in range(GROUP):
        for r in range(4):
            rows = pl.ds(f * 32 + r, 8, stride=4)
            start[f, r] = pressure_ref[rows, :]
            store[f, r] = storage_ref[rows, :]
            perm[f, r] = perm_ref[rows, :]
            leak[f, r] = leak_ref[rows, :]
            own_source[f, r] = source_ref[rows, :]

    sub8 = lax.broadcasted_iota(jnp.int32, (8, 128), 0)
    lane8 = lax.broadcasted_iota(jnp.int32, (8, 128), 1)
    for g in range(2):
        cell = jnp.broadcast_to(export_ref[g : g + 1, :], (8, 128))
        row = (cell >> 7) & 31
        export_lane[g] = cell & 127
        export_code[g] = jnp.where((row >> 2) == sub8, (cell >> 12) * 4 + (row & 3), -1)
    slot = trace_ref[...]
    trace_lane[...] = slot & 127
    trace_row[...] = slot >> 7
    live = (sub8 * 128 + lane8) < count_ref[0]
    weight[...] = jnp.where(live, trans_ref[...], 0.0)
    cell = local_ref[...]
    cell_row = (cell >> 7) & 31
    code = (cell >> 12) * 32 + (cell_row & 3) * 8 + (cell_row >> 2)
    cell_lane = cell & 127
    number = lax.broadcasted_iota(jnp.int32, (128, 128), 0)
    for t in range(8):
        rows_t = jnp.broadcast_to(code[t : t + 1, :], (128, 128))
        row_hot[t] = jnp.where(rows_t == number, 1.0, 0.0).astype(jnp.bfloat16)
        lanes_t = jnp.broadcast_to(cell_lane[t : t + 1, :], (128, 128))
        hot = jnp.where(lanes_t == number, 1.0, 0.0)
        lane_hot[t * 128 : (t + 1) * 128, :] = hot.T.astype(jnp.bfloat16)

    def scatter(parts):
        total = jnp.zeros((128 * len(parts), 128), jnp.float32)
        for p in range(4):
            stacked = []
            for part in parts:
                pieces = []
                for t in (2 * p, 2 * p + 1):
                    line = jnp.broadcast_to(part[t : t + 1, :], (16, 128)).astype(jnp.bfloat16)
                    block = row_hot[t].reshape(8, 16, 128) * line[None]
                    pieces.append(block.reshape(128, 128))
                stacked.append(jnp.concatenate(pieces, axis=1))
            left = jnp.concatenate(stacked, axis=0)
            right = lane_hot[p * 256 : (p + 1) * 256, :]
            total = total + jnp.dot(left, right, preferred_element_type=jnp.float32)
        result = total[:128]
        for n in range(1, len(parts)):
            result = result + total[n * 128 : (n + 1) * 128]
        return result.reshape(GROUP, 4, 8, 128)

    def terms(value, number_of):
        parts = []
        for _ in range(number_of):
            part = value.astype(jnp.bfloat16).astype(jnp.float32)
            parts.append(part)
            value = value - part
        return parts

    tisum[...] = scatter(terms(weight[...], 3))

    pl.semaphore_wait(barrier, peers - 1 + GROUP - 1 + 4 + 2 * (GROUP - 1))

    def source_copy(ahead, target):
        slot = (1 - ahead) * GROUP + column
        return pltpu.make_async_remote_copy(
            src_ref=own_source.at[target],
            dst_ref=source_in.at[slot],
            send_sem=source_send.at[ahead, target],
            recv_sem=source_recv.at[slot],
            device_id={"tm": (plane + ahead) * GROUP + target, "frac": me},
        )

    def source_arrival(slot):
        return pltpu.make_async_remote_copy(
            src_ref=own_source.at[0],
            dst_ref=source_in.at[slot],
            send_sem=source_send.at[0, 0],
            recv_sem=source_recv.at[slot],
            device_id={"tm": plane * GROUP + (column + 1) % GROUP, "frac": me},
        )

    def u_copy(k, target):
        return pltpu.make_async_remote_copy(
            src_ref=u_out.at[k, target],
            dst_ref=u_in.at[k, column],
            send_sem=u_send.at[k, target],
            recv_sem=u_recv.at[k, column],
            device_id={"tm": plane * GROUP + target, "frac": me},
        )

    def u_arrival(k, origin):
        return pltpu.make_async_remote_copy(
            src_ref=u_out.at[k, origin],
            dst_ref=u_in.at[k, origin],
            send_sem=u_send.at[k, origin],
            recv_sem=u_recv.at[k, origin],
            device_id={"tm": plane * GROUP + origin, "frac": me},
        )

    def f_copy(k, ahead, target):
        slot = (1 - ahead) * GROUP + column
        return pltpu.make_async_remote_copy(
            src_ref=f_out.at[k, target],
            dst_ref=f_in.at[k, slot],
            send_sem=f_send.at[k, ahead, target],
            recv_sem=f_recv.at[k, slot],
            device_id={"tm": (plane + ahead) * GROUP + target, "frac": me},
        )

    def f_arrival(k, slot):
        return pltpu.make_async_remote_copy(
            src_ref=f_out.at[k, 0],
            dst_ref=f_in.at[k, slot],
            send_sem=f_send.at[k, 0, 0],
            recv_sem=f_recv.at[k, slot],
            device_id={"tm": plane * GROUP + (column + 1) % GROUP, "frac": me},
        )

    def edge_copy(k, target):
        return pltpu.make_async_remote_copy(
            src_ref=edge_out.at[k],
            dst_ref=edge_in.at[k],
            send_sem=edge_send.at[k],
            recv_sem=edge_recv.at[k],
            device_id={"tm": target, "frac": me},
        )

    def first_copy(k, target, peer):
        return pltpu.make_async_remote_copy(
            src_ref=first_out.at[k, target],
            dst_ref=first_in.at[k, column * peers + me],
            send_sem=first_send.at[k],
            recv_sem=first_recv.at[k],
            device_id={"tm": plane * GROUP + target, "frac": peer},
        )

    def first_all(k):
        return pltpu.make_async_remote_copy(
            src_ref=first_in.at[k, pl.ds(0, GROUP * peers - 1)],
            dst_ref=first_in.at[k, pl.ds(0, GROUP * peers - 1)],
            send_sem=first_send.at[k],
            recv_sem=first_recv.at[k],
            device_id={"tm": slice_index, "frac": (me + 1) % peers},
        )

    def share_copy(m, target):
        return pltpu.make_async_remote_copy(
            src_ref=shared.at[m, me],
            dst_ref=shared.at[m, me],
            send_sem=share_send.at[m],
            recv_sem=share_recv.at[m],
            device_id={"tm": slice_index, "frac": target},
        )

    def share_all(m):
        return pltpu.make_async_remote_copy(
            src_ref=shared.at[m, pl.ds(0, peers - 1)],
            dst_ref=shared.at[m, pl.ds(0, peers - 1)],
            send_sem=share_send.at[m],
            recv_sem=share_recv.at[m],
            device_id={"tm": slice_index, "frac": (me + 1) % peers},
        )

    @pl.when(plane < planes - 1)
    def _():
        for d in (2, 1, 3, 0):
            source_copy(1, (column + d) % GROUP).start()

    for d in (2, 1, 3):
        source_copy(0, (column + d) % GROUP).start()
    source_in[GROUP + column] = own_source[column]

    def exports(blocks, offset, g):
        lanes, codes = export_lane[g], export_code[g] - offset
        found = jnp.zeros((8, 128), jnp.float32)
        for n in range(4 * blocks.shape[0]):
            found = jnp.where(codes == n, pick(blocks[n // 4, n % 4], lanes), found)
        return jnp.sum(found, axis=0, keepdims=True)

    def announce(k):
        for j in range(GROUP):
            u = u_out[k, j][None]
            for g in range(2):
                first_out[k, j, g : g + 1, :] = exports(u, 4 * column, g)

        def send(i, carry):
            d = (peers // 2 + (1 - 2 * (i % 2)) * ((i + 1) // 2)) % peers
            for j in range(GROUP):

                @pl.when((d != 0) | (column != j))
                def _():
                    first_copy(k, j, (me + d) % peers).start()

            return carry

        lax.fori_loop(0, peers, send, 0)
        first_in[k, column * peers + me] = first_out[k, column]

    def advance(k, first, slot, u):
        following = coarse(u, source_in[slot], store[column], perm[column], leak[column])
        if first:
            u = following
        else:
            u = following + (f_in[k - 1, slot] - coarse_old[slot])
        coarse_old[slot] = following
        return u

    def arrival(k, first, slot):
        if first:
            source_arrival(slot).wait_recv()
        else:
            f_arrival(k - 1, slot).wait_recv()

    def chain(k, first):
        @pl.when(plane > 1)
        def _():
            edge_copy(k, slice_index - 2 * GROUP).wait_recv()

        @pl.when(plane <= 1)
        def _():
            edge_in[k] = start[column]

        @pl.when(plane > 0)
        def _():
            u = edge_in[k]
            for j in range(GROUP):
                arrival(k, first, j)
                u = advance(k, first, j, u)
            edge_in[k] = u

        u = edge_in[k]
        for j in range(GROUP):
            u_out[k, j] = u

            @pl.when(column != j)
            def _():
                u_copy(k, j).start()
                arrival(k, first, GROUP + j)

            u = advance(k, first, GROUP + j, u)
        edge_out[k] = u

        @pl.when(plane < planes - 2)
        def _():
            edge_copy(k, slice_index + 2 * GROUP).start()

        if first:
            announce(k)
        else:

            @pl.when(k < ITERS)
            def _():
                announce(k)

        u_in[k, column] = u_out[k, column]
        for d in range(1, GROUP):
            u_arrival(k, (column + d) % GROUP).wait_recv()

    def fine(k):
        field[...] = u_in[k]

        def step(t, carry):
            m = k * (FINE_STEPS - 1) + t - 1
            q = field[...]

            @pl.when(t > 0)
            def _():
                for g in range(2):
                    shared[m, me, g : g + 1, :] = exports(q, 0, g)
                for d in others:
                    share_copy(m, (me + d) % peers).start()

            parts = faces(q, perm[...])
            rate = store[...] * (1.0 / fine_size)
            total = rate + leak[...] + tisum[...] + (parts[0] + parts[1]) + (parts[2] + parts[3])
            inverse = 1.0 / total
            base = (rate * q + own_source[...]) * inverse
            weights = [part * inverse for part in parts]

            @pl.when(t > 0)
            def _():
                share_all(m).wait_recv()
                gathered[...] = shared[m]

            @pl.when(t == 0)
            def _():
                first_all(k).wait_recv()
                total = first_in[k, 0:peers]
                for f in range(1, GROUP):
                    total = total + first_in[k, f * peers : (f + 1) * peers]
                gathered[...] = total

            rows = trace_row[...]
            lanes = trace_lane[...]
            value = jnp.zeros((8, 128), jnp.float32)
            for n in range(2 * peers):
                line = jnp.broadcast_to(gathered[n // 2, n % 2 : n % 2 + 1, :], (8, 128))
                value = jnp.where(rows == n, pick(line, lanes), value)
            base = base + scatter(terms(weight[...] * value, 2)) * inverse
            v = q
            for _ in range(SWEEPS):
                v = sweep(v, base, weights)
            field[...] = v
            return carry

        lax.fori_loop(0, FINE_STEPS, step, 0)
        f_out[k] = field[...]

        @pl.when(plane < planes - 1)
        def _():
            for d in (2, 1, 3, 0):
                f_copy(k, 1, (column + d) % GROUP).start()

        for d in (2, 1, 3):
            f_copy(k, 0, (column + d) % GROUP).start()
        f_in[k, GROUP + column] = f_out[k, column]

    chain(0, True)

    def iteration(k, carry):
        fine(k)
        chain(k + 1, False)
        return carry

    lax.fori_loop(0, ITERS, iteration, 0)

    for f in range(GROUP):
        for r in range(4):
            out_ref[pl.ds(f * 32 + r, 8, stride=4), :] = u_in[ITERS, f, r]

    for d in range(1, GROUP):
        other = (column + d) % GROUP
        source_copy(0, other).wait_send()
        for k in range(ITERS + 1):
            u_copy(k, other).wait_send()
        for k in range(ITERS):
            f_copy(k, 0, other).wait_send()

    @pl.when(plane < planes - 1)
    def _():
        for f in range(GROUP):
            source_copy(1, f).wait_send()
            for k in range(ITERS):
                f_copy(k, 1, f).wait_send()

    @pl.when(plane < planes - 2)
    def _():
        for k in range(ITERS + 1):
            edge_copy(k, slice_index + 2 * GROUP).wait_send()

    for k in range(ITERS):
        first_all(k).wait_send()
    for m in range(ITERS * (FINE_STEPS - 1)):
        share_all(m).wait_send()


def body(
    pressure0,
    storage,
    perm_base,
    leakoff,
    sources,
    export_cells,
    inter_local,
    trace_source,
    inter_trans,
    inter_count,
):
    planes = lax.axis_size("tm") // GROUP
    peers = lax.axis_size("frac")
    flat = lambda a: a.reshape(128, 128)
    vmem = pl.BlockSpec(memory_space=pltpu.VMEM)
    f32 = jnp.float32
    block = (4, 8, 128)
    whole = (GROUP,) + block
    shares = ITERS * (FINE_STEPS - 1)
    slots = 2 * GROUP
    out = pl.pallas_call(
        functools.partial(kernel, planes, peers),
        out_shape=jax.ShapeDtypeStruct((128, 128), f32),
        in_specs=[pl.BlockSpec(memory_space=pltpu.SMEM)]
        + [pl.BlockSpec(memory_space=pl.ANY)] * 9,
        out_specs=vmem,
        scratch_shapes=[
            pltpu.VMEM((128, 128), f32),
            pltpu.VMEM((128, 128), f32),
            pltpu.VMEM((128, 128), f32),
            pltpu.VMEM((128, 128), f32),
            pltpu.VMEM((128, 128), f32),
            pltpu.VMEM((2, 128), jnp.int32),
            pltpu.VMEM((8, 128), jnp.int32),
            pltpu.VMEM((8, 128), jnp.int32),
            pltpu.VMEM((8, 128), f32),
            pltpu.VMEM(whole, f32),
            pltpu.VMEM(whole, f32),
            pltpu.VMEM(whole, f32),
            pltpu.VMEM(whole, f32),
            pltpu.VMEM(whole, f32),
            pltpu.VMEM(whole, f32),
            pltpu.VMEM((slots,) + block, f32),
            pltpu.VMEM((ITERS + 1,) + whole, f32),
            pltpu.VMEM((ITERS + 1,) + whole, f32),
            pltpu.VMEM((ITERS,) + whole, f32),
            pltpu.VMEM((ITERS, slots) + block, f32),
            pltpu.VMEM((ITERS + 1,) + block, f32),
            pltpu.VMEM((ITERS + 1,) + block, f32),
            pltpu.VMEM((slots,) + block, f32),
            pltpu.VMEM((ITERS, GROUP, 2, 128), f32),
            pltpu.VMEM((ITERS, GROUP * peers, 2, 128), f32),
            pltpu.VMEM((shares, peers, 2, 128), f32),
            pltpu.VMEM((peers, 2, 128), f32),
            pltpu.VMEM(whole, f32),
            pltpu.VMEM((8, 128, 128), jnp.bfloat16),
            pltpu.VMEM((1024, 128), jnp.bfloat16),
            pltpu.VMEM((2, 8, 128), jnp.int32),
            pltpu.VMEM((2, 8, 128), jnp.int32),
            pltpu.VMEM((8, 128), jnp.int32),
            pltpu.VMEM((8, 128), jnp.int32),
            pltpu.VMEM((8, 128), f32),
            pltpu.SemaphoreType.DMA((9,)),
            pltpu.SemaphoreType.DMA((2, GROUP)),
            pltpu.SemaphoreType.DMA((slots,)),
            pltpu.SemaphoreType.DMA((ITERS + 1, GROUP)),
            pltpu.SemaphoreType.DMA((ITERS + 1, GROUP)),
            pltpu.SemaphoreType.DMA((ITERS, 2, GROUP)),
            pltpu.SemaphoreType.DMA((ITERS, slots)),
            pltpu.SemaphoreType.DMA((ITERS + 1,)),
            pltpu.SemaphoreType.DMA((ITERS + 1,)),
            pltpu.SemaphoreType.DMA((ITERS,)),
            pltpu.SemaphoreType.DMA((ITERS,)),
            pltpu.SemaphoreType.DMA((shares,)),
            pltpu.SemaphoreType.DMA((shares,)),
        ],
        compiler_params=pltpu.CompilerParams(
            collective_id=0, has_side_effects=True
        ),
        name="parareal",
    )(
        inter_count,
        flat(pressure0),
        flat(storage),
        flat(perm_base),
        flat(leakoff),
        flat(sources),
        export_cells.reshape(2, 128),
        inter_local.reshape(8, 128),
        trace_source.reshape(8, 128),
        inter_trans.reshape(8, 128),
    )
    return out.reshape(sources.shape)


def solution(mesh):
    placed = (
        P("frac", None, None),
        P("frac", None, None),
        P("frac", None, None),
        P("frac", None, None),
        P("tm", "frac", None, None),
        P("frac"),
        P("frac"),
        P("frac"),
        P("frac"),
        P("frac"),
    )
    return jax.shard_map(
        body, mesh=mesh, in_specs=placed, out_specs=P("tm", "frac", None, None), check_vma=False
    )
```

```python
import functools

import jax
import jax.numpy as jnp
from jax import lax
from jax.experimental import pallas as pl
from jax.experimental.pallas import tpu as pltpu
from jax.sharding import PartitionSpec as P

FINE_STEPS = 4
SWEEPS = 8
COARSE_SWEEPS = 2
ITERS = 2
GROUP = 4

stress_factor = 0.15
fine_size = 0.25


def next_rows(v):
    return jnp.concatenate(
        [v[..., 1:, :, :], pltpu.roll(v[..., :1, :, :], 7, v.ndim - 2)], axis=v.ndim - 3
    )


def prev_rows(v):
    return jnp.concatenate(
        [pltpu.roll(v[..., 3:, :, :], 1, v.ndim - 2), v[..., :3, :, :]], axis=v.ndim - 3
    )


def next_cols(v):
    return pltpu.roll(v, 127, v.ndim - 1)


def prev_cols(v):
    return pltpu.roll(v, 1, v.ndim - 1)


def faces(pressure, perm):
    conductivity = perm * jnp.exp(stress_factor * pressure)
    shape = pressure.shape
    block = lax.broadcasted_iota(jnp.int32, shape, len(shape) - 3)
    sub = lax.broadcasted_iota(jnp.int32, shape, len(shape) - 2)
    lane = lax.broadcasted_iota(jnp.int32, shape, len(shape) - 1)
    row_half = jnp.where((block == 3) & (sub == 7), 0.0, 0.5)
    col_half = jnp.where(lane == 127, 0.0, 0.5)
    face_r = row_half * (conductivity + next_rows(conductivity))
    face_c = col_half * (conductivity + next_cols(conductivity))
    return face_r, prev_rows(face_r), face_c, prev_cols(face_c)


def sweep(v, base, weights):
    down, up, right, left = weights
    return base + (down * next_rows(v) + up * prev_rows(v)) + (
        right * next_cols(v) + left * prev_cols(v)
    )


def coarse(pressure, source, store, perm, leak):
    parts = faces(pressure, perm)
    inverse = 1.0 / (store + leak + (parts[0] + parts[1]) + (parts[2] + parts[3]))
    base = (store * pressure + source) * inverse
    weights = [part * inverse for part in parts]
    v = pressure
    for _ in range(COARSE_SWEEPS):
        v = sweep(v, base, weights)
    return v


def pick(table, lanes):
    return jnp.take_along_axis(table, lanes, axis=1, mode="promise_in_bounds")


def kernel(
    planes,
    peers,
    count_ref,
    pressure_hbm,
    storage_hbm,
    perm_hbm,
    leak_hbm,
    source_hbm,
    export_hbm,
    local_hbm,
    trace_hbm,
    trans_hbm,
    out_ref,
    pressure_ref,
    storage_ref,
    perm_ref,
    leak_ref,
    source_ref,
    export_ref,
    local_ref,
    trace_ref,
    trans_ref,
    start,
    store,
    perm,
    leak,
    tisum,
    own_source,
    source_in,
    u_out,
    u_in,
    f_out,
    f_in,
    edge_in,
    edge_out,
    coarse_old,
    first_out,
    first_in,
    shared,
    gathered,
    field,
    row_hot,
    lane_hot,
    export_lane,
    export_code,
    trace_lane,
    trace_row,
    weight,
    fetched,
    source_send,
    source_recv,
    u_send,
    u_recv,
    f_send,
    f_recv,
    edge_send,
    edge_recv,
    first_send,
    first_recv,
    share_send,
    share_recv,
):
    slice_index = lax.axis_index("tm")
    me = lax.axis_index("frac")
    plane = slice_index // GROUP
    column = slice_index % GROUP
    odd = plane % 2
    partner = plane + 1 - 2 * odd
    others = sorted(range(1, peers), key=lambda d: -min(d, peers - d))

    barrier = pltpu.get_barrier_semaphore()
    for d in others:
        pl.semaphore_signal(
            barrier, inc=1, device_id={"tm": slice_index, "frac": (me + d) % peers}
        )
    for d in range(1, GROUP):
        pl.semaphore_signal(
            barrier,
            inc=1,
            device_id={"tm": plane * GROUP + (column + d) % GROUP, "frac": me},
        )

    for d in (1, 2, planes - 2, planes - 1):
        pl.semaphore_signal(
            barrier,
            inc=1,
            device_id={"tm": (plane + d) % planes * GROUP + column, "frac": me},
        )
    for d in range(1, GROUP):
        pl.semaphore_signal(
            barrier,
            inc=1,
            device_id={"tm": partner * GROUP + (column + d) % GROUP, "frac": me},
        )

    pairs = (
        (source_hbm, source_ref),
        (pressure_hbm, pressure_ref),
        (storage_hbm, storage_ref),
        (perm_hbm, perm_ref),
        (leak_hbm, leak_ref),
        (export_hbm, export_ref),
        (local_hbm, local_ref),
        (trace_hbm, trace_ref),
        (trans_hbm, trans_ref),
    )
    fetches = [
        pltpu.make_async_copy(origin, target, fetched.at[n])
        for n, (origin, target) in enumerate(pairs)
    ]
    for fetch in fetches:
        fetch.start()
    for fetch in fetches:
        fetch.wait()

    for f in range(GROUP):
        for r in range(4):
            rows = pl.ds(f * 32 + r, 8, stride=4)
            start[f, r] = pressure_ref[rows, :]
            store[f, r] = storage_ref[rows, :]
            perm[f, r] = perm_ref[rows, :]
            leak[f, r] = leak_ref[rows, :]
            own_source[f, r] = source_ref[rows, :]

    sub8 = lax.broadcasted_iota(jnp.int32, (8, 128), 0)
    lane8 = lax.broadcasted_iota(jnp.int32, (8, 128), 1)
    for g in range(2):
        cell = jnp.broadcast_to(export_ref[g : g + 1, :], (8, 128))
        row = (cell >> 7) & 31
        export_lane[g] = cell & 127
        export_code[g] = jnp.where((row >> 2) == sub8, (cell >> 12) * 4 + (row & 3), -1)
    slot = trace_ref[...]
    trace_lane[...] = slot & 127
    trace_row[...] = slot >> 7
    live = (sub8 * 128 + lane8) < count_ref[0]
    weight[...] = jnp.where(live, trans_ref[...], 0.0)
    cell = local_ref[...]
    cell_row = (cell >> 7) & 31
    code = (cell >> 12) * 32 + (cell_row & 3) * 8 + (cell_row >> 2)
    cell_lane = cell & 127
    number = lax.broadcasted_iota(jnp.int32, (128, 128), 0)
    for t in range(8):
        rows_t = jnp.broadcast_to(code[t : t + 1, :], (128, 128))
        row_hot[t] = jnp.where(rows_t == number, 1.0, 0.0).astype(jnp.bfloat16)
        lanes_t = jnp.broadcast_to(cell_lane[t : t + 1, :], (128, 128))
        hot = jnp.where(lanes_t == number, 1.0, 0.0)
        lane_hot[t * 128 : (t + 1) * 128, :] = hot.T.astype(jnp.bfloat16)

    def scatter(parts):
        total = jnp.zeros((128 * len(parts), 128), jnp.float32)
        for p in range(4):
            stacked = []
            for part in parts:
                pieces = []
                for t in (2 * p, 2 * p + 1):
                    line = jnp.broadcast_to(part[t : t + 1, :], (16, 128)).astype(jnp.bfloat16)
                    block = row_hot[t].reshape(8, 16, 128) * line[None]
                    pieces.append(block.reshape(128, 128))
                stacked.append(jnp.concatenate(pieces, axis=1))
            left = jnp.concatenate(stacked, axis=0)
            right = lane_hot[p * 256 : (p + 1) * 256, :]
            total = total + jnp.dot(left, right, preferred_element_type=jnp.float32)
        result = total[:128]
        for n in range(1, len(parts)):
            result = result + total[n * 128 : (n + 1) * 128]
        return result.reshape(GROUP, 4, 8, 128)

    def terms(value, number_of):
        parts = []
        for _ in range(number_of):
            part = value.astype(jnp.bfloat16).astype(jnp.float32)
            parts.append(part)
            value = value - part
        return parts

    tisum[...] = scatter(terms(weight[...], 3))

    pl.semaphore_wait(barrier, peers - 1 + 2 * (GROUP - 1) + 4)

    def source_copy(ahead, target):
        slot = (1 - ahead) * GROUP + column
        return pltpu.make_async_remote_copy(
            src_ref=own_source.at[target],
            dst_ref=source_in.at[slot],
            send_sem=source_send.at[ahead, target],
            recv_sem=source_recv.at[slot],
            device_id={"tm": (plane + ahead) * GROUP + target, "frac": me},
        )

    def source_arrival(slot):
        return pltpu.make_async_remote_copy(
            src_ref=own_source.at[0],
            dst_ref=source_in.at[slot],
            send_sem=source_send.at[0, 0],
            recv_sem=source_recv.at[slot],
            device_id={"tm": plane * GROUP + (column + 1) % GROUP, "frac": me},
        )

    def u_copy(k, target):
        return pltpu.make_async_remote_copy(
            src_ref=u_out.at[k, target],
            dst_ref=u_in.at[k, column],
            send_sem=u_send.at[k, target],
            recv_sem=u_recv.at[k, column],
            device_id={"tm": plane * GROUP + target, "frac": me},
        )

    def u_arrival(k, origin):
        return pltpu.make_async_remote_copy(
            src_ref=u_out.at[k, origin],
            dst_ref=u_in.at[k, origin],
            send_sem=u_send.at[k, origin],
            recv_sem=u_recv.at[k, origin],
            device_id={"tm": plane * GROUP + origin, "frac": me},
        )

    def f_copy(k, ahead, target):
        slot = (1 - ahead) * GROUP + column
        return pltpu.make_async_remote_copy(
            src_ref=f_out.at[k, target],
            dst_ref=f_in.at[k, slot],
            send_sem=f_send.at[k, ahead, target],
            recv_sem=f_recv.at[k, slot],
            device_id={"tm": (plane + ahead) * GROUP + target, "frac": me},
        )

    def f_arrival(k, slot):
        return pltpu.make_async_remote_copy(
            src_ref=f_out.at[k, 0],
            dst_ref=f_in.at[k, slot],
            send_sem=f_send.at[k, 0, 0],
            recv_sem=f_recv.at[k, slot],
            device_id={"tm": plane * GROUP + (column + 1) % GROUP, "frac": me},
        )

    def edge_copy(k, ahead):
        return pltpu.make_async_remote_copy(
            src_ref=edge_out.at[k],
            dst_ref=edge_in.at[k],
            send_sem=edge_send.at[k, ahead - 1],
            recv_sem=edge_recv.at[k],
            device_id={"tm": slice_index + ahead * GROUP, "frac": me},
        )

    def edge_arrival(k):
        return pltpu.make_async_remote_copy(
            src_ref=edge_out.at[k],
            dst_ref=edge_in.at[k],
            send_sem=edge_send.at[k, 0],
            recv_sem=edge_recv.at[k],
            device_id={"tm": slice_index - GROUP, "frac": me},
        )

    def first_copy(k, target, peer):
        return pltpu.make_async_remote_copy(
            src_ref=first_out.at[k, target],
            dst_ref=first_in.at[k, column * peers + me],
            send_sem=first_send.at[k],
            recv_sem=first_recv.at[k],
            device_id={"tm": plane * GROUP + target, "frac": peer},
        )

    def first_all(k):
        return pltpu.make_async_remote_copy(
            src_ref=first_in.at[k, pl.ds(0, GROUP * peers - 1)],
            dst_ref=first_in.at[k, pl.ds(0, GROUP * peers - 1)],
            send_sem=first_send.at[k],
            recv_sem=first_recv.at[k],
            device_id={"tm": slice_index, "frac": (me + 1) % peers},
        )

    def share_copy(m, target):
        return pltpu.make_async_remote_copy(
            src_ref=shared.at[m, me],
            dst_ref=shared.at[m, me],
            send_sem=share_send.at[m],
            recv_sem=share_recv.at[m],
            device_id={"tm": slice_index, "frac": target},
        )

    def share_all(m):
        return pltpu.make_async_remote_copy(
            src_ref=shared.at[m, pl.ds(0, peers - 1)],
            dst_ref=shared.at[m, pl.ds(0, peers - 1)],
            send_sem=share_send.at[m],
            recv_sem=share_recv.at[m],
            device_id={"tm": slice_index, "frac": (me + 1) % peers},
        )

    @pl.when(odd == 0)
    def _():
        for d in (2, 1, 3, 0):
            source_copy(1, (column + d) % GROUP).start()

    for d in (2, 1, 3):
        source_copy(0, (column + d) % GROUP).start()
    source_in[GROUP + column] = own_source[column]

    def exports(blocks, offset, g):
        lanes, codes = export_lane[g], export_code[g] - offset
        found = jnp.zeros((8, 128), jnp.float32)
        for n in range(4 * blocks.shape[0]):
            found = jnp.where(codes == n, pick(blocks[n // 4, n % 4], lanes), found)
        return jnp.sum(found, axis=0, keepdims=True)

    def announce(k):
        for j in range(GROUP):
            u = u_out[k, j][None]
            for g in range(2):
                first_out[k, j, g : g + 1, :] = exports(u, 4 * column, g)

        for d in others:
            for j in range(GROUP):
                first_copy(k, j, (me + d) % peers).start()
        for d in range(1, GROUP):
            first_copy(k, (column + d) % GROUP, me).start()
        first_in[k, column * peers + me] = first_out[k, column]

    def advance(k, first, slot, u):
        following = coarse(u, source_in[slot], store[column], perm[column], leak[column])
        if first:
            u = following
        else:
            u = following + (f_in[k - 1, slot] - coarse_old[slot])
        coarse_old[slot] = following
        return u

    def arrival(k, first, slot):
        if first:
            source_arrival(slot).wait_recv()
        else:
            f_arrival(k - 1, slot).wait_recv()

    def chain(k, first):
        @pl.when(plane > 1)
        def _():
            edge_arrival(k).wait_recv()

        @pl.when(plane <= 1)
        def _():
            edge_in[k] = start[column]

        @pl.when(odd == 1)
        def _():
            u = edge_in[k]
            for j in range(GROUP):
                arrival(k, first, j)
                u = advance(k, first, j, u)
            edge_in[k] = u

        u = edge_in[k]
        for j in range(GROUP):
            u_out[k, j] = u

            @pl.when(column != j)
            def _():
                u_copy(k, j).start()
                arrival(k, first, GROUP + j)

            u = advance(k, first, GROUP + j, u)
        edge_out[k] = u

        @pl.when((odd == 1) & (plane < planes - 2))
        def _():
            edge_copy(k, 2).start()
            edge_copy(k, 1).start()

        if first:
            announce(k)
        else:

            @pl.when(k < ITERS)
            def _():
                announce(k)

        u_in[k, column] = u_out[k, column]
        for d in range(1, GROUP):
            u_arrival(k, (column + d) % GROUP).wait_recv()

    def fine(k):
        field[...] = u_in[k]

        def step(t, carry):
            m = k * (FINE_STEPS - 1) + t - 1
            q = field[...]

            @pl.when(t > 0)
            def _():
                for g in range(2):
                    shared[m, me, g : g + 1, :] = exports(q, 0, g)
                for d in others:
                    share_copy(m, (me + d) % peers).start()

            parts = faces(q, perm[...])
            rate = store[...] * (1.0 / fine_size)
            total = rate + leak[...] + tisum[...] + (parts[0] + parts[1]) + (parts[2] + parts[3])
            inverse = 1.0 / total
            base = (rate * q + own_source[...]) * inverse
            weights = [part * inverse for part in parts]

            @pl.when(t > 0)
            def _():
                share_all(m).wait_recv()
                gathered[...] = shared[m]

            @pl.when(t == 0)
            def _():
                first_all(k).wait_recv()
                total = first_in[k, 0:peers]
                for f in range(1, GROUP):
                    total = total + first_in[k, f * peers : (f + 1) * peers]
                gathered[...] = total

            rows = trace_row[...]
            lanes = trace_lane[...]
            value = jnp.zeros((8, 128), jnp.float32)
            for n in range(2 * peers):
                line = jnp.broadcast_to(gathered[n // 2, n % 2 : n % 2 + 1, :], (8, 128))
                value = jnp.where(rows == n, pick(line, lanes), value)
            base = base + scatter(terms(weight[...] * value, 2)) * inverse
            v = q
            for _ in range(SWEEPS):
                v = sweep(v, base, weights)
            field[...] = v
            return carry

        lax.fori_loop(0, FINE_STEPS, step, 0)
        f_out[k] = field[...]

        @pl.when(odd == 0)
        def _():
            for d in (2, 1, 3, 0):
                f_copy(k, 1, (column + d) % GROUP).start()

        for d in (2, 1, 3):
            f_copy(k, 0, (column + d) % GROUP).start()
        f_in[k, GROUP + column] = f_out[k, column]

    chain(0, True)

    def iteration(k, carry):
        fine(k)
        chain(k + 1, False)
        return carry

    lax.fori_loop(0, ITERS, iteration, 0)

    for f in range(GROUP):
        for r in range(4):
            out_ref[pl.ds(f * 32 + r, 8, stride=4), :] = u_in[ITERS, f, r]

    for d in range(1, GROUP):
        other = (column + d) % GROUP
        source_copy(0, other).wait_send()
        for k in range(ITERS + 1):
            u_copy(k, other).wait_send()
        for k in range(ITERS):
            f_copy(k, 0, other).wait_send()

    @pl.when(odd == 0)
    def _():
        for f in range(GROUP):
            source_copy(1, f).wait_send()
            for k in range(ITERS):
                f_copy(k, 1, f).wait_send()

    @pl.when((odd == 1) & (plane < planes - 2))
    def _():
        for k in range(ITERS + 1):
            for ahead in (1, 2):
                edge_copy(k, ahead).wait_send()

    for k in range(ITERS):
        first_all(k).wait_send()
    for m in range(ITERS * (FINE_STEPS - 1)):
        share_all(m).wait_send()


def body(
    pressure0,
    storage,
    perm_base,
    leakoff,
    sources,
    export_cells,
    inter_local,
    trace_source,
    inter_trans,
    inter_count,
):
    planes = lax.axis_size("tm") // GROUP
    peers = lax.axis_size("frac")
    flat = lambda a: a.reshape(128, 128)
    vmem = pl.BlockSpec(memory_space=pltpu.VMEM)
    f32 = jnp.float32
    block = (4, 8, 128)
    whole = (GROUP,) + block
    shares = ITERS * (FINE_STEPS - 1)
    slots = 2 * GROUP
    out = pl.pallas_call(
        functools.partial(kernel, planes, peers),
        out_shape=jax.ShapeDtypeStruct((128, 128), f32),
        in_specs=[pl.BlockSpec(memory_space=pltpu.SMEM)]
        + [pl.BlockSpec(memory_space=pl.ANY)] * 9,
        out_specs=vmem,
        scratch_shapes=[
            pltpu.VMEM((128, 128), f32),
            pltpu.VMEM((128, 128), f32),
            pltpu.VMEM((128, 128), f32),
            pltpu.VMEM((128, 128), f32),
            pltpu.VMEM((128, 128), f32),
            pltpu.VMEM((2, 128), jnp.int32),
            pltpu.VMEM((8, 128), jnp.int32),
            pltpu.VMEM((8, 128), jnp.int32),
            pltpu.VMEM((8, 128), f32),
            pltpu.VMEM(whole, f32),
            pltpu.VMEM(whole, f32),
            pltpu.VMEM(whole, f32),
            pltpu.VMEM(whole, f32),
            pltpu.VMEM(whole, f32),
            pltpu.VMEM(whole, f32),
            pltpu.VMEM((slots,) + block, f32),
            pltpu.VMEM((ITERS + 1,) + whole, f32),
            pltpu.VMEM((ITERS + 1,) + whole, f32),
            pltpu.VMEM((ITERS,) + whole, f32),
            pltpu.VMEM((ITERS, slots) + block, f32),
            pltpu.VMEM((ITERS + 1,) + block, f32),
            pltpu.VMEM((ITERS + 1,) + block, f32),
            pltpu.VMEM((slots,) + block, f32),
            pltpu.VMEM((ITERS, GROUP, 2, 128), f32),
            pltpu.VMEM((ITERS, GROUP * peers, 2, 128), f32),
            pltpu.VMEM((shares, peers, 2, 128), f32),
            pltpu.VMEM((peers, 2, 128), f32),
            pltpu.VMEM(whole, f32),
            pltpu.VMEM((8, 128, 128), jnp.bfloat16),
            pltpu.VMEM((1024, 128), jnp.bfloat16),
            pltpu.VMEM((2, 8, 128), jnp.int32),
            pltpu.VMEM((2, 8, 128), jnp.int32),
            pltpu.VMEM((8, 128), jnp.int32),
            pltpu.VMEM((8, 128), jnp.int32),
            pltpu.VMEM((8, 128), f32),
            pltpu.SemaphoreType.DMA((9,)),
            pltpu.SemaphoreType.DMA((2, GROUP)),
            pltpu.SemaphoreType.DMA((slots,)),
            pltpu.SemaphoreType.DMA((ITERS + 1, GROUP)),
            pltpu.SemaphoreType.DMA((ITERS + 1, GROUP)),
            pltpu.SemaphoreType.DMA((ITERS, 2, GROUP)),
            pltpu.SemaphoreType.DMA((ITERS, slots)),
            pltpu.SemaphoreType.DMA((ITERS + 1, 2)),
            pltpu.SemaphoreType.DMA((ITERS + 1,)),
            pltpu.SemaphoreType.DMA((ITERS,)),
            pltpu.SemaphoreType.DMA((ITERS,)),
            pltpu.SemaphoreType.DMA((shares,)),
            pltpu.SemaphoreType.DMA((shares,)),
        ],
        compiler_params=pltpu.CompilerParams(
            collective_id=0, has_side_effects=True
        ),
        name="parareal",
    )(
        inter_count,
        flat(pressure0),
        flat(storage),
        flat(perm_base),
        flat(leakoff),
        flat(sources),
        export_cells.reshape(2, 128),
        inter_local.reshape(8, 128),
        trace_source.reshape(8, 128),
        inter_trans.reshape(8, 128),
    )
    return out.reshape(sources.shape)


def solution(mesh):
    placed = (
        P("frac", None, None),
        P("frac", None, None),
        P("frac", None, None),
        P("frac", None, None),
        P("tm", "frac", None, None),
        P("frac"),
        P("frac"),
        P("frac"),
        P("frac"),
        P("frac"),
    )
    return jax.shard_map(
        body, mesh=mesh, in_specs=placed, out_specs=P("tm", "frac", None, None), check_vma=False
    )
```

```python
import functools

import jax
import jax.numpy as jnp
from jax import lax
from jax.experimental import pallas as pl
from jax.experimental.pallas import tpu as pltpu
from jax.sharding import PartitionSpec as P

FINE_STEPS = 4
SWEEPS = 8
COARSE_SWEEPS = 2
ITERS = 2
GROUP = 4

stress_factor = 0.15
fine_size = 0.25


def next_rows(v):
    return jnp.concatenate(
        [v[..., 1:, :, :], pltpu.roll(v[..., :1, :, :], 7, v.ndim - 2)], axis=v.ndim - 3
    )


def prev_rows(v):
    return jnp.concatenate(
        [pltpu.roll(v[..., 3:, :, :], 1, v.ndim - 2), v[..., :3, :, :]], axis=v.ndim - 3
    )


def next_cols(v):
    return pltpu.roll(v, 127, v.ndim - 1)


def prev_cols(v):
    return pltpu.roll(v, 1, v.ndim - 1)


def faces(pressure, perm):
    conductivity = perm * jnp.exp(stress_factor * pressure)
    shape = pressure.shape
    block = lax.broadcasted_iota(jnp.int32, shape, len(shape) - 3)
    sub = lax.broadcasted_iota(jnp.int32, shape, len(shape) - 2)
    lane = lax.broadcasted_iota(jnp.int32, shape, len(shape) - 1)
    down_half = jnp.where((block == 3) & (sub == 7), 0.0, 0.5)
    up_half = jnp.where((block == 0) & (sub == 0), 0.0, 0.5)
    right_half = jnp.where(lane == 127, 0.0, 0.5)
    left_half = jnp.where(lane == 0, 0.0, 0.5)
    return (
        down_half * (conductivity + next_rows(conductivity)),
        up_half * (conductivity + prev_rows(conductivity)),
        right_half * (conductivity + next_cols(conductivity)),
        left_half * (conductivity + prev_cols(conductivity)),
    )


def sweep(v, base, weights):
    down, up, right, left = weights
    return base + (down * next_rows(v) + up * prev_rows(v)) + (
        right * next_cols(v) + left * prev_cols(v)
    )


def coarse(pressure, source, store, perm, leak):
    parts = faces(pressure, perm)
    inverse = 1.0 / (store + leak + (parts[0] + parts[1]) + (parts[2] + parts[3]))
    base = (store * pressure + source) * inverse
    weights = [part * inverse for part in parts]
    v = pressure
    for _ in range(COARSE_SWEEPS):
        v = sweep(v, base, weights)
    return v


def pick(table, lanes):
    return jnp.take_along_axis(table, lanes, axis=1, mode="promise_in_bounds")


def kernel(
    planes,
    peers,
    count_ref,
    pressure_hbm,
    storage_hbm,
    perm_hbm,
    leak_hbm,
    source_hbm,
    export_hbm,
    local_hbm,
    trace_hbm,
    trans_hbm,
    out_ref,
    pressure_ref,
    storage_ref,
    perm_ref,
    leak_ref,
    source_ref,
    export_ref,
    local_ref,
    trace_ref,
    trans_ref,
    start,
    store,
    perm,
    leak,
    tisum,
    own_source,
    source_in,
    u_out,
    u_in,
    f_out,
    f_in,
    edge_in,
    edge_out,
    coarse_old,
    first_out,
    first_in,
    shared,
    gathered,
    field,
    row_hot,
    lane_hot,
    export_lane,
    export_code,
    trace_lane,
    trace_row,
    weight,
    fetched,
    source_send,
    source_recv,
    u_send,
    u_recv,
    f_send,
    f_recv,
    edge_send,
    edge_recv,
    first_send,
    first_recv,
    share_send,
    share_recv,
):
    slice_index = lax.axis_index("tm")
    me = lax.axis_index("frac")
    plane = slice_index // GROUP
    column = slice_index % GROUP
    odd = plane % 2
    partner = plane + 1 - 2 * odd
    others = sorted(range(1, peers), key=lambda d: -min(d, peers - d))

    barrier = pltpu.get_barrier_semaphore()
    for d in others:
        pl.semaphore_signal(
            barrier, inc=1, device_id={"tm": slice_index, "frac": (me + d) % peers}
        )
    for d in range(1, GROUP):
        pl.semaphore_signal(
            barrier,
            inc=1,
            device_id={"tm": plane * GROUP + (column + d) % GROUP, "frac": me},
        )

    for d in (1, 2, planes - 2, planes - 1):
        pl.semaphore_signal(
            barrier,
            inc=1,
            device_id={"tm": (plane + d) % planes * GROUP + column, "frac": me},
        )
    for d in range(1, GROUP):
        pl.semaphore_signal(
            barrier,
            inc=1,
            device_id={"tm": partner * GROUP + (column + d) % GROUP, "frac": me},
        )

    pairs = (
        (source_hbm, source_ref),
        (pressure_hbm, pressure_ref),
        (storage_hbm, storage_ref),
        (perm_hbm, perm_ref),
        (leak_hbm, leak_ref),
        (export_hbm, export_ref),
        (local_hbm, local_ref),
        (trace_hbm, trace_ref),
        (trans_hbm, trans_ref),
    )
    fetches = [
        pltpu.make_async_copy(origin, target, fetched.at[n])
        for n, (origin, target) in enumerate(pairs)
    ]
    for fetch in fetches:
        fetch.start()
    for fetch in fetches:
        fetch.wait()

    for f in range(GROUP):
        for r in range(4):
            rows = pl.ds(f * 32 + r, 8, stride=4)
            start[f, r] = pressure_ref[rows, :]
            store[f, r] = storage_ref[rows, :]
            perm[f, r] = perm_ref[rows, :]
            leak[f, r] = leak_ref[rows, :]
            own_source[f, r] = source_ref[rows, :]

    sub8 = lax.broadcasted_iota(jnp.int32, (8, 128), 0)
    lane8 = lax.broadcasted_iota(jnp.int32, (8, 128), 1)
    for g in range(2):
        cell = jnp.broadcast_to(export_ref[g : g + 1, :], (8, 128))
        row = (cell >> 7) & 31
        export_lane[g] = cell & 127
        export_code[g] = jnp.where((row >> 2) == sub8, (cell >> 12) * 4 + (row & 3), -1)
    slot = trace_ref[...]
    trace_lane[...] = slot & 127
    trace_row[...] = slot >> 7
    live = (sub8 * 128 + lane8) < count_ref[0]
    weight[...] = jnp.where(live, trans_ref[...], 0.0)
    cell = local_ref[...]
    cell_row = (cell >> 7) & 31
    code = (cell >> 12) * 32 + (cell_row & 3) * 8 + (cell_row >> 2)
    cell_lane = cell & 127
    number = lax.broadcasted_iota(jnp.int32, (64, 128), 0)
    column_number = lax.broadcasted_iota(jnp.int32, (256, 128), 0)
    for t in range(8):
        rows_t = jnp.broadcast_to(code[t : t + 1, :] & 63, (64, 128))
        row_hot[:, t * 128 : (t + 1) * 128] = jnp.where(rows_t == number, 1.0, 0.0).astype(
            jnp.bfloat16
        )
        columns_t = (code[t : t + 1, :] >> 6) * 128 + cell_lane[t : t + 1, :]
        hot = jnp.where(jnp.broadcast_to(columns_t, (256, 128)) == column_number, 1.0, 0.0)
        lane_hot[t * 128 : (t + 1) * 128, :] = hot.T.astype(jnp.bfloat16)

    def scatter(parts):
        rows = []
        for part in parts:
            line = jnp.concatenate([part[t : t + 1, :] for t in range(8)], axis=1)
            line = jnp.broadcast_to(line, (16, 1024)).astype(jnp.bfloat16)
            rows.append((row_hot[...].reshape(4, 16, 1024) * line[None]).reshape(64, 1024))
        left = jnp.concatenate(rows, axis=0)
        total = jnp.dot(left, lane_hot[...], preferred_element_type=jnp.float32)
        result = total[:64]
        for n in range(1, len(parts)):
            result = result + total[n * 64 : (n + 1) * 64]
        halves = [result[:, h * 128 : (h + 1) * 128].reshape(GROUP // 2, 4, 8, 128) for h in (0, 1)]
        return jnp.concatenate(halves, axis=0)

    def terms(value, number_of):
        parts = []
        for _ in range(number_of):
            part = value.astype(jnp.bfloat16).astype(jnp.float32)
            parts.append(part)
            value = value - part
        return parts

    tisum[...] = scatter(terms(weight[...], 3))

    pl.semaphore_wait(barrier, peers - 1 + 2 * (GROUP - 1) + 4)

    def source_copy(ahead, target):
        slot = (1 - ahead) * GROUP + column
        return pltpu.make_async_remote_copy(
            src_ref=own_source.at[target],
            dst_ref=source_in.at[slot],
            send_sem=source_send.at[ahead, target],
            recv_sem=source_recv.at[slot],
            device_id={"tm": (plane + ahead) * GROUP + target, "frac": me},
        )

    def source_arrival(slot):
        return pltpu.make_async_remote_copy(
            src_ref=own_source.at[0],
            dst_ref=source_in.at[slot],
            send_sem=source_send.at[0, 0],
            recv_sem=source_recv.at[slot],
            device_id={"tm": plane * GROUP + (column + 1) % GROUP, "frac": me},
        )

    def u_copy(k, target):
        return pltpu.make_async_remote_copy(
            src_ref=u_out.at[k, target],
            dst_ref=u_in.at[k, column],
            send_sem=u_send.at[k, target],
            recv_sem=u_recv.at[k, column],
            device_id={"tm": plane * GROUP + target, "frac": me},
        )

    def u_arrival(k, origin):
        return pltpu.make_async_remote_copy(
            src_ref=u_out.at[k, origin],
            dst_ref=u_in.at[k, origin],
            send_sem=u_send.at[k, origin],
            recv_sem=u_recv.at[k, origin],
            device_id={"tm": plane * GROUP + origin, "frac": me},
        )

    def f_copy(k, ahead, target):
        slot = (1 - ahead) * GROUP + column
        return pltpu.make_async_remote_copy(
            src_ref=f_out.at[k, target],
            dst_ref=f_in.at[k, slot],
            send_sem=f_send.at[k, ahead, target],
            recv_sem=f_recv.at[k, slot],
            device_id={"tm": (plane + ahead) * GROUP + target, "frac": me},
        )

    def f_arrival(k, slot):
        return pltpu.make_async_remote_copy(
            src_ref=f_out.at[k, 0],
            dst_ref=f_in.at[k, slot],
            send_sem=f_send.at[k, 0, 0],
            recv_sem=f_recv.at[k, slot],
            device_id={"tm": plane * GROUP + (column + 1) % GROUP, "frac": me},
        )

    def edge_copy(k, ahead):
        return pltpu.make_async_remote_copy(
            src_ref=edge_out.at[k],
            dst_ref=edge_in.at[k],
            send_sem=edge_send.at[k, ahead - 1],
            recv_sem=edge_recv.at[k],
            device_id={"tm": slice_index + ahead * GROUP, "frac": me},
        )

    def edge_arrival(k):
        return pltpu.make_async_remote_copy(
            src_ref=edge_out.at[k],
            dst_ref=edge_in.at[k],
            send_sem=edge_send.at[k, 0],
            recv_sem=edge_recv.at[k],
            device_id={"tm": slice_index - GROUP, "frac": me},
        )

    def first_copy(k, target, peer):
        return pltpu.make_async_remote_copy(
            src_ref=first_out.at[k, target],
            dst_ref=first_in.at[k, column * peers + me],
            send_sem=first_send.at[k],
            recv_sem=first_recv.at[k],
            device_id={"tm": plane * GROUP + target, "frac": peer},
        )

    def first_all(k):
        return pltpu.make_async_remote_copy(
            src_ref=first_in.at[k, pl.ds(0, GROUP * peers - 1)],
            dst_ref=first_in.at[k, pl.ds(0, GROUP * peers - 1)],
            send_sem=first_send.at[k],
            recv_sem=first_recv.at[k],
            device_id={"tm": slice_index, "frac": (me + 1) % peers},
        )

    def share_copy(m, target):
        return pltpu.make_async_remote_copy(
            src_ref=shared.at[m, me],
            dst_ref=shared.at[m, me],
            send_sem=share_send.at[m],
            recv_sem=share_recv.at[m],
            device_id={"tm": slice_index, "frac": target},
        )

    def share_all(m):
        return pltpu.make_async_remote_copy(
            src_ref=shared.at[m, pl.ds(0, peers - 1)],
            dst_ref=shared.at[m, pl.ds(0, peers - 1)],
            send_sem=share_send.at[m],
            recv_sem=share_recv.at[m],
            device_id={"tm": slice_index, "frac": (me + 1) % peers},
        )

    @pl.when(odd == 0)
    def _():
        for d in (2, 1, 3, 0):
            source_copy(1, (column + d) % GROUP).start()

    for d in (2, 1, 3):
        source_copy(0, (column + d) % GROUP).start()
    source_in[GROUP + column] = own_source[column]

    def exports(blocks, offset, g):
        lanes, codes = export_lane[g], export_code[g] - offset
        found = jnp.zeros((8, 128), jnp.float32)
        for n in range(4 * blocks.shape[0]):
            found = jnp.where(codes == n, pick(blocks[n // 4, n % 4], lanes), found)
        return jnp.sum(found, axis=0, keepdims=True)

    def announce(k):
        for j in range(GROUP):
            u = u_out[k, j][None]
            for g in range(2):
                first_out[k, j, g : g + 1, :] = exports(u, 4 * column, g)

        for d in others:
            for j in range(GROUP):
                first_copy(k, j, (me + d) % peers).start()
        for d in range(1, GROUP):
            first_copy(k, (column + d) % GROUP, me).start()
        first_in[k, column * peers + me] = first_out[k, column]

    def advance(k, first, slot, u):
        following = coarse(u, source_in[slot], store[column], perm[column], leak[column])
        if first:
            u = following
        else:
            u = following + (f_in[k - 1, slot] - coarse_old[slot])
        coarse_old[slot] = following
        return u

    def arrival(k, first, slot):
        if first:
            source_arrival(slot).wait_recv()
        else:
            f_arrival(k - 1, slot).wait_recv()

    def chain(k, first):
        @pl.when(plane > 1)
        def _():
            edge_arrival(k).wait_recv()

        @pl.when(plane <= 1)
        def _():
            edge_in[k] = start[column]

        @pl.when(odd == 1)
        def _():
            u = edge_in[k]
            for j in range(GROUP):
                arrival(k, first, j)
                u = advance(k, first, j, u)
            edge_in[k] = u

        u = edge_in[k]
        for j in range(GROUP):
            u_out[k, j] = u

            @pl.when(column != j)
            def _():
                u_copy(k, j).start()
                arrival(k, first, GROUP + j)

            u = advance(k, first, GROUP + j, u)
        edge_out[k] = u

        @pl.when((odd == 1) & (plane < planes - 2))
        def _():
            edge_copy(k, 2).start()
            edge_copy(k, 1).start()

        if first:
            announce(k)
        else:

            @pl.when(k < ITERS)
            def _():
                announce(k)

        u_in[k, column] = u_out[k, column]
        for d in range(1, GROUP):
            u_arrival(k, (column + d) % GROUP).wait_recv()

    def fine(k):
        field[...] = u_in[k]

        def step(t, carry):
            m = k * (FINE_STEPS - 1) + t - 1
            q = field[...]

            @pl.when(t > 0)
            def _():
                for g in range(2):
                    shared[m, me, g : g + 1, :] = exports(q, 0, g)
                for d in others:
                    share_copy(m, (me + d) % peers).start()

            parts = faces(q, perm[...])
            rate = store[...] * (1.0 / fine_size)
            total = rate + leak[...] + tisum[...] + (parts[0] + parts[1]) + (parts[2] + parts[3])
            inverse = 1.0 / total
            base = (rate * q + own_source[...]) * inverse
            weights = [part * inverse for part in parts]

            @pl.when(t > 0)
            def _():
                share_all(m).wait_recv()
                gathered[...] = shared[m]

            @pl.when(t == 0)
            def _():
                first_all(k).wait_recv()
                total = first_in[k, 0:peers]
                for f in range(1, GROUP):
                    total = total + first_in[k, f * peers : (f + 1) * peers]
                gathered[...] = total

            rows = trace_row[...]
            lanes = trace_lane[...]
            value = jnp.zeros((8, 128), jnp.float32)
            for n in range(2 * peers):
                line = jnp.broadcast_to(gathered[n // 2, n % 2 : n % 2 + 1, :], (8, 128))
                value = jnp.where(rows == n, pick(line, lanes), value)
            base = base + scatter(terms(weight[...] * value, 2)) * inverse
            v = q
            for _ in range(SWEEPS):
                v = sweep(v, base, weights)
            field[...] = v
            return carry

        lax.fori_loop(0, FINE_STEPS, step, 0)
        f_out[k] = field[...]

        @pl.when(odd == 0)
        def _():
            for d in (2, 1, 3, 0):
                f_copy(k, 1, (column + d) % GROUP).start()

        for d in (2, 1, 3):
            f_copy(k, 0, (column + d) % GROUP).start()
        f_in[k, GROUP + column] = f_out[k, column]

    chain(0, True)

    def iteration(k, carry):
        fine(k)
        chain(k + 1, False)
        return carry

    lax.fori_loop(0, ITERS, iteration, 0)

    for f in range(GROUP):
        for r in range(4):
            out_ref[pl.ds(f * 32 + r, 8, stride=4), :] = u_in[ITERS, f, r]

    for d in range(1, GROUP):
        other = (column + d) % GROUP
        source_copy(0, other).wait_send()
        for k in range(ITERS + 1):
            u_copy(k, other).wait_send()
        for k in range(ITERS):
            f_copy(k, 0, other).wait_send()

    @pl.when(odd == 0)
    def _():
        for f in range(GROUP):
            source_copy(1, f).wait_send()
            for k in range(ITERS):
                f_copy(k, 1, f).wait_send()

    @pl.when((odd == 1) & (plane < planes - 2))
    def _():
        for k in range(ITERS + 1):
            for ahead in (1, 2):
                edge_copy(k, ahead).wait_send()

    for k in range(ITERS):
        first_all(k).wait_send()
    for m in range(ITERS * (FINE_STEPS - 1)):
        share_all(m).wait_send()


def body(
    pressure0,
    storage,
    perm_base,
    leakoff,
    sources,
    export_cells,
    inter_local,
    trace_source,
    inter_trans,
    inter_count,
):
    planes = lax.axis_size("tm") // GROUP
    peers = lax.axis_size("frac")
    flat = lambda a: a.reshape(128, 128)
    vmem = pl.BlockSpec(memory_space=pltpu.VMEM)
    f32 = jnp.float32
    block = (4, 8, 128)
    whole = (GROUP,) + block
    shares = ITERS * (FINE_STEPS - 1)
    slots = 2 * GROUP
    out = pl.pallas_call(
        functools.partial(kernel, planes, peers),
        out_shape=jax.ShapeDtypeStruct((128, 128), f32),
        in_specs=[pl.BlockSpec(memory_space=pltpu.SMEM)]
        + [pl.BlockSpec(memory_space=pl.ANY)] * 9,
        out_specs=vmem,
        scratch_shapes=[
            pltpu.VMEM((128, 128), f32),
            pltpu.VMEM((128, 128), f32),
            pltpu.VMEM((128, 128), f32),
            pltpu.VMEM((128, 128), f32),
            pltpu.VMEM((128, 128), f32),
            pltpu.VMEM((2, 128), jnp.int32),
            pltpu.VMEM((8, 128), jnp.int32),
            pltpu.VMEM((8, 128), jnp.int32),
            pltpu.VMEM((8, 128), f32),
            pltpu.VMEM(whole, f32),
            pltpu.VMEM(whole, f32),
            pltpu.VMEM(whole, f32),
            pltpu.VMEM(whole, f32),
            pltpu.VMEM(whole, f32),
            pltpu.VMEM(whole, f32),
            pltpu.VMEM((slots,) + block, f32),
            pltpu.VMEM((ITERS + 1,) + whole, f32),
            pltpu.VMEM((ITERS + 1,) + whole, f32),
            pltpu.VMEM((ITERS,) + whole, f32),
            pltpu.VMEM((ITERS, slots) + block, f32),
            pltpu.VMEM((ITERS + 1,) + block, f32),
            pltpu.VMEM((ITERS + 1,) + block, f32),
            pltpu.VMEM((slots,) + block, f32),
            pltpu.VMEM((ITERS, GROUP, 2, 128), f32),
            pltpu.VMEM((ITERS, GROUP * peers, 2, 128), f32),
            pltpu.VMEM((shares, peers, 2, 128), f32),
            pltpu.VMEM((peers, 2, 128), f32),
            pltpu.VMEM(whole, f32),
            pltpu.VMEM((64, 1024), jnp.bfloat16),
            pltpu.VMEM((1024, 256), jnp.bfloat16),
            pltpu.VMEM((2, 8, 128), jnp.int32),
            pltpu.VMEM((2, 8, 128), jnp.int32),
            pltpu.VMEM((8, 128), jnp.int32),
            pltpu.VMEM((8, 128), jnp.int32),
            pltpu.VMEM((8, 128), f32),
            pltpu.SemaphoreType.DMA((9,)),
            pltpu.SemaphoreType.DMA((2, GROUP)),
            pltpu.SemaphoreType.DMA((slots,)),
            pltpu.SemaphoreType.DMA((ITERS + 1, GROUP)),
            pltpu.SemaphoreType.DMA((ITERS + 1, GROUP)),
            pltpu.SemaphoreType.DMA((ITERS, 2, GROUP)),
            pltpu.SemaphoreType.DMA((ITERS, slots)),
            pltpu.SemaphoreType.DMA((ITERS + 1, 2)),
            pltpu.SemaphoreType.DMA((ITERS + 1,)),
            pltpu.SemaphoreType.DMA((ITERS,)),
            pltpu.SemaphoreType.DMA((ITERS,)),
            pltpu.SemaphoreType.DMA((shares,)),
            pltpu.SemaphoreType.DMA((shares,)),
        ],
        compiler_params=pltpu.CompilerParams(
            collective_id=0, has_side_effects=True
        ),
        name="parareal",
    )(
        inter_count,
        flat(pressure0),
        flat(storage),
        flat(perm_base),
        flat(leakoff),
        flat(sources),
        export_cells.reshape(2, 128),
        inter_local.reshape(8, 128),
        trace_source.reshape(8, 128),
        inter_trans.reshape(8, 128),
    )
    return out.reshape(sources.shape)


def solution(mesh):
    placed = (
        P("frac", None, None),
        P("frac", None, None),
        P("frac", None, None),
        P("frac", None, None),
        P("tm", "frac", None, None),
        P("frac"),
        P("frac"),
        P("frac"),
        P("frac"),
        P("frac"),
    )
    return jax.shard_map(
        body, mesh=mesh, in_specs=placed, out_specs=P("tm", "frac", None, None), check_vma=False
    )
```

```python
import functools

import jax
import jax.numpy as jnp
from jax import lax
from jax.experimental import pallas as pl
from jax.experimental.pallas import tpu as pltpu
from jax.sharding import PartitionSpec as P

FINE_STEPS = 4
SWEEPS = 8
COARSE_SWEEPS = 2
ITERS = 2
GROUP = 4

stress_factor = 0.15
fine_size = 0.25


def next_rows(v):
    return jnp.concatenate(
        [v[..., 1:, :, :], pltpu.roll(v[..., :1, :, :], 7, v.ndim - 2)], axis=v.ndim - 3
    )


def prev_rows(v):
    return jnp.concatenate(
        [pltpu.roll(v[..., 3:, :, :], 1, v.ndim - 2), v[..., :3, :, :]], axis=v.ndim - 3
    )


def next_cols(v):
    return pltpu.roll(v, 127, v.ndim - 1)


def prev_cols(v):
    return pltpu.roll(v, 1, v.ndim - 1)


def iota(shape, axis):
    return lax.broadcasted_iota(jnp.int32, shape, len(shape) + axis)


def row_halves(shape):
    block, sub = iota(shape, -3), iota(shape, -2)
    return (
        jnp.where((block == 3) & (sub == 7), 0.0, 0.5),
        jnp.where((block == 0) & (sub == 0), 0.0, 0.5),
    )


def packed_next(v):
    return jnp.concatenate([v[:, 1:], pltpu.roll(v[:, :1], 127, v.ndim - 1)], axis=1)


def packed_prev(v):
    return jnp.concatenate([pltpu.roll(v[:, 1:], 1, v.ndim - 1), v[:, :1]], axis=1)


def packed_faces(pressure, perm):
    conductivity = perm * jnp.exp(stress_factor * pressure)
    shape = pressure.shape
    parity, place = iota(shape, -4), iota(shape, -1) & 63
    down, up = row_halves(shape)
    right = jnp.where((parity == 1) & (place == 63), 0.0, 0.5)
    left = jnp.where((parity == 0) & (place == 0), 0.0, 0.5)
    return (
        down * (conductivity + next_rows(conductivity)),
        up * (conductivity + prev_rows(conductivity)),
        right * (conductivity + packed_next(conductivity)),
        left * (conductivity + packed_prev(conductivity)),
    )


def packed_sweep(v, base, weights):
    down, up, right, left = weights
    return base + (down * next_rows(v) + up * prev_rows(v)) + (
        right * packed_next(v) + left * packed_prev(v)
    )


def coarse(pressure, source, store, perm, leak):
    conductivity = perm * jnp.exp(stress_factor * pressure)
    shape = pressure.shape
    lane = iota(shape, -1)
    down_half, up_half = row_halves(shape)
    down = down_half * (conductivity + next_rows(conductivity))
    up = up_half * (conductivity + prev_rows(conductivity))
    right = jnp.where(lane == 127, 0.0, 0.5) * (conductivity + next_cols(conductivity))
    left = jnp.where(lane == 0, 0.0, 0.5) * (conductivity + prev_cols(conductivity))
    inverse = 1.0 / (store + leak + (down + up) + (right + left))
    base = (store * pressure + source) * inverse
    down, up, right, left = down * inverse, up * inverse, right * inverse, left * inverse
    v = pressure
    for _ in range(COARSE_SWEEPS):
        v = base + (down * next_rows(v) + up * prev_rows(v)) + (
            right * next_cols(v) + left * prev_cols(v)
        )
    return v


def pick(table, lanes):
    return jnp.take_along_axis(table, lanes, axis=1, mode="promise_in_bounds")


def pack(blocks):
    lane = lax.broadcasted_iota(jnp.int32, (8, 128), 1)
    places = 2 * (lane & 63)
    pairs = []
    for p in range(GROUP // 2):
        for e in range(2):
            for r in range(4):
                low, high = pick(blocks[2 * p, r], places + e), pick(blocks[2 * p + 1, r], places + e)
                pairs.append(jnp.where(lane < 64, low, high))
    return jnp.stack(pairs).reshape(GROUP // 2, 2, 4, 8, 128)


def unpack(packed):
    lane = lax.broadcasted_iota(jnp.int32, (8, 128), 1)
    places = lane >> 1
    blocks = []
    for f in range(GROUP):
        for r in range(4):
            even, odd = [pick(packed[f // 2, e, r], places + 64 * (f % 2)) for e in range(2)]
            blocks.append(jnp.where((lane & 1) == 0, even, odd))
    return jnp.stack(blocks).reshape(GROUP, 4, 8, 128)


def kernel(
    planes,
    peers,
    count_ref,
    pressure_hbm,
    storage_hbm,
    perm_hbm,
    leak_hbm,
    source_hbm,
    export_hbm,
    local_hbm,
    trace_hbm,
    trans_hbm,
    out_ref,
    pressure_ref,
    storage_ref,
    perm_ref,
    leak_ref,
    source_ref,
    export_ref,
    local_ref,
    trace_ref,
    trans_ref,
    start,
    store,
    perm,
    leak,
    fine_store,
    fine_perm,
    fine_leak,
    fine_source,
    own_source,
    source_in,
    u_out,
    u_in,
    f_out,
    f_in,
    edge_in,
    edge_out,
    coarse_old,
    first_out,
    first_in,
    shared,
    gathered,
    field,
    row_hot,
    lane_hot,
    export_lane,
    export_code,
    fine_lane,
    fine_code,
    trace_lane,
    trace_row,
    weight,
    fetched,
    source_send,
    source_recv,
    u_send,
    u_recv,
    f_send,
    f_recv,
    edge_send,
    edge_recv,
    first_send,
    first_recv,
    share_send,
    share_recv,
):
    slice_index = lax.axis_index("tm")
    me = lax.axis_index("frac")
    plane = slice_index // GROUP
    column = slice_index % GROUP
    odd = plane % 2
    partner = plane + 1 - 2 * odd
    others = sorted(range(1, peers), key=lambda d: -min(d, peers - d))

    barrier = pltpu.get_barrier_semaphore()
    for d in others:
        pl.semaphore_signal(
            barrier, inc=1, device_id={"tm": slice_index, "frac": (me + d) % peers}
        )
    for d in range(1, GROUP):
        pl.semaphore_signal(
            barrier,
            inc=1,
            device_id={"tm": plane * GROUP + (column + d) % GROUP, "frac": me},
        )

    for d in (1, 2, planes - 2, planes - 1):
        pl.semaphore_signal(
            barrier,
            inc=1,
            device_id={"tm": (plane + d) % planes * GROUP + column, "frac": me},
        )
    for d in range(1, GROUP):
        pl.semaphore_signal(
            barrier,
            inc=1,
            device_id={"tm": partner * GROUP + (column + d) % GROUP, "frac": me},
        )

    pairs = (
        (source_hbm, source_ref),
        (pressure_hbm, pressure_ref),
        (storage_hbm, storage_ref),
        (perm_hbm, perm_ref),
        (leak_hbm, leak_ref),
        (export_hbm, export_ref),
        (local_hbm, local_ref),
        (trace_hbm, trace_ref),
        (trans_hbm, trans_ref),
    )
    fetches = [
        pltpu.make_async_copy(origin, target, fetched.at[n])
        for n, (origin, target) in enumerate(pairs)
    ]
    for fetch in fetches:
        fetch.start()
    for fetch in fetches:
        fetch.wait()

    for f in range(GROUP):
        for r in range(4):
            rows = pl.ds(f * 32 + r, 8, stride=4)
            start[f, r] = pressure_ref[rows, :]
            store[f, r] = storage_ref[rows, :]
            perm[f, r] = perm_ref[rows, :]
            leak[f, r] = leak_ref[rows, :]
            own_source[f, r] = source_ref[rows, :]

    sub8 = lax.broadcasted_iota(jnp.int32, (8, 128), 0)
    lane8 = lax.broadcasted_iota(jnp.int32, (8, 128), 1)
    for g in range(2):
        cell = jnp.broadcast_to(export_ref[g : g + 1, :], (8, 128))
        row = (cell >> 7) & 31
        export_lane[g] = cell & 127
        export_code[g] = jnp.where((row >> 2) == sub8, (cell >> 12) * 4 + (row & 3), -1)
        fine_lane[g] = ((cell >> 12) & 1) * 64 + ((cell & 127) >> 1)
        number = (cell >> 13) * 8 + (cell & 1) * 4 + (row & 3)
        fine_code[g] = jnp.where((row >> 2) == sub8, number, -1)
    slot = trace_ref[...]
    trace_lane[...] = slot & 127
    trace_row[...] = slot >> 7
    live = (sub8 * 128 + lane8) < count_ref[0]
    weight[...] = jnp.where(live, trans_ref[...], 0.0)
    cell = local_ref[...]
    cell_row = (cell >> 7) & 31
    code = (cell & 1) * 32 + (cell_row & 3) * 8 + (cell_row >> 2)
    cell_column = (cell >> 13) * 128 + ((cell >> 12) & 1) * 64 + ((cell & 127) >> 1)
    number = lax.broadcasted_iota(jnp.int32, (64, 128), 0)
    column_number = lax.broadcasted_iota(jnp.int32, (256, 128), 0)
    for t in range(8):
        rows_t = jnp.broadcast_to(code[t : t + 1, :], (64, 128))
        row_hot[:, t * 128 : (t + 1) * 128] = jnp.where(rows_t == number, 1.0, 0.0).astype(
            jnp.bfloat16
        )
        columns_t = jnp.broadcast_to(cell_column[t : t + 1, :], (256, 128))
        hot = jnp.where(columns_t == column_number, 1.0, 0.0)
        lane_hot[t * 128 : (t + 1) * 128, :] = hot.T.astype(jnp.bfloat16)

    def scatter(parts):
        rows = []
        for part in parts:
            line = jnp.concatenate([part[t : t + 1, :] for t in range(8)], axis=1)
            line = jnp.broadcast_to(line, (16, 1024)).astype(jnp.bfloat16)
            rows.append((row_hot[...].reshape(4, 16, 1024) * line[None]).reshape(64, 1024))
        left = jnp.concatenate(rows, axis=0)
        total = jnp.dot(left, lane_hot[...], preferred_element_type=jnp.float32)
        result = total[:64]
        for n in range(1, len(parts)):
            result = result + total[n * 64 : (n + 1) * 64]
        halves = [result[:, h * 128 : (h + 1) * 128].reshape(1, 2, 4, 8, 128) for h in (0, 1)]
        return jnp.concatenate(halves, axis=0)

    def terms(value, number_of):
        parts = []
        for _ in range(number_of):
            part = value.astype(jnp.bfloat16).astype(jnp.float32)
            parts.append(part)
            value = value - part
        return parts

    rate = pack(store[...]) * (1.0 / fine_size)
    fine_store[...] = rate
    fine_perm[...] = pack(perm[...])
    fine_leak[...] = rate + pack(leak[...]) + scatter(terms(weight[...], 3))
    fine_source[...] = pack(own_source[...])

    pl.semaphore_wait(barrier, peers - 1 + 2 * (GROUP - 1) + 4)

    def source_copy(ahead, target):
        slot = (1 - ahead) * GROUP + column
        return pltpu.make_async_remote_copy(
            src_ref=own_source.at[target],
            dst_ref=source_in.at[slot],
            send_sem=source_send.at[ahead, target],
            recv_sem=source_recv.at[slot],
            device_id={"tm": (plane + ahead) * GROUP + target, "frac": me},
        )

    def source_arrival(slot):
        return pltpu.make_async_remote_copy(
            src_ref=own_source.at[0],
            dst_ref=source_in.at[slot],
            send_sem=source_send.at[0, 0],
            recv_sem=source_recv.at[slot],
            device_id={"tm": plane * GROUP + (column + 1) % GROUP, "frac": me},
        )

    def u_copy(k, target):
        return pltpu.make_async_remote_copy(
            src_ref=u_out.at[k, target],
            dst_ref=u_in.at[k, column],
            send_sem=u_send.at[k, target],
            recv_sem=u_recv.at[k, column],
            device_id={"tm": plane * GROUP + target, "frac": me},
        )

    def u_arrival(k, origin):
        return pltpu.make_async_remote_copy(
            src_ref=u_out.at[k, origin],
            dst_ref=u_in.at[k, origin],
            send_sem=u_send.at[k, origin],
            recv_sem=u_recv.at[k, origin],
            device_id={"tm": plane * GROUP + origin, "frac": me},
        )

    def f_copy(k, ahead, target):
        slot = (1 - ahead) * GROUP + column
        return pltpu.make_async_remote_copy(
            src_ref=f_out.at[k, target],
            dst_ref=f_in.at[k, slot],
            send_sem=f_send.at[k, ahead, target],
            recv_sem=f_recv.at[k, slot],
            device_id={"tm": (plane + ahead) * GROUP + target, "frac": me},
        )

    def f_arrival(k, slot):
        return pltpu.make_async_remote_copy(
            src_ref=f_out.at[k, 0],
            dst_ref=f_in.at[k, slot],
            send_sem=f_send.at[k, 0, 0],
            recv_sem=f_recv.at[k, slot],
            device_id={"tm": plane * GROUP + (column + 1) % GROUP, "frac": me},
        )

    def edge_copy(k, ahead):
        return pltpu.make_async_remote_copy(
            src_ref=edge_out.at[k],
            dst_ref=edge_in.at[k],
            send_sem=edge_send.at[k, ahead - 1],
            recv_sem=edge_recv.at[k],
            device_id={"tm": slice_index + ahead * GROUP, "frac": me},
        )

    def edge_arrival(k):
        return pltpu.make_async_remote_copy(
            src_ref=edge_out.at[k],
            dst_ref=edge_in.at[k],
            send_sem=edge_send.at[k, 0],
            recv_sem=edge_recv.at[k],
            device_id={"tm": slice_index - GROUP, "frac": me},
        )

    def first_copy(k, target, peer):
        return pltpu.make_async_remote_copy(
            src_ref=first_out.at[k, target],
            dst_ref=first_in.at[k, column * peers + me],
            send_sem=first_send.at[k],
            recv_sem=first_recv.at[k],
            device_id={"tm": plane * GROUP + target, "frac": peer},
        )

    def first_all(k):
        return pltpu.make_async_remote_copy(
            src_ref=first_in.at[k, pl.ds(0, GROUP * peers - 1)],
            dst_ref=first_in.at[k, pl.ds(0, GROUP * peers - 1)],
            send_sem=first_send.at[k],
            recv_sem=first_recv.at[k],
            device_id={"tm": slice_index, "frac": (me + 1) % peers},
        )

    def share_copy(m, target):
        return pltpu.make_async_remote_copy(
            src_ref=shared.at[m, me],
            dst_ref=shared.at[m, me],
            send_sem=share_send.at[m],
            recv_sem=share_recv.at[m],
            device_id={"tm": slice_index, "frac": target},
        )

    def share_all(m):
        return pltpu.make_async_remote_copy(
            src_ref=shared.at[m, pl.ds(0, peers - 1)],
            dst_ref=shared.at[m, pl.ds(0, peers - 1)],
            send_sem=share_send.at[m],
            recv_sem=share_recv.at[m],
            device_id={"tm": slice_index, "frac": (me + 1) % peers},
        )

    @pl.when(odd == 0)
    def _():
        for d in (2, 1, 3, 0):
            source_copy(1, (column + d) % GROUP).start()

    for d in (2, 1, 3):
        source_copy(0, (column + d) % GROUP).start()
    source_in[GROUP + column] = own_source[column]

    def exports(tables, lanes, codes):
        found = jnp.zeros((8, 128), jnp.float32)
        for n, table in enumerate(tables):
            found = jnp.where(codes == n, pick(table, lanes), found)
        return jnp.sum(found, axis=0, keepdims=True)

    def announce(k):
        for j in range(GROUP):
            u = u_out[k, j]
            for g in range(2):
                first_out[k, j, g : g + 1, :] = exports(
                    [u[r] for r in range(4)], export_lane[g], export_code[g] - 4 * column
                )

        for d in others:
            for j in range(GROUP):
                first_copy(k, j, (me + d) % peers).start()
        for d in range(1, GROUP):
            first_copy(k, (column + d) % GROUP, me).start()
        first_in[k, column * peers + me] = first_out[k, column]

    def advance(k, first, slot, u):
        following = coarse(u, source_in[slot], store[column], perm[column], leak[column])
        if first:
            u = following
        else:
            u = following + (f_in[k - 1, slot] - coarse_old[slot])
        coarse_old[slot] = following
        return u

    def arrival(k, first, slot):
        if first:
            source_arrival(slot).wait_recv()
        else:
            f_arrival(k - 1, slot).wait_recv()

    def chain(k, first):
        @pl.when(plane > 1)
        def _():
            edge_arrival(k).wait_recv()

        @pl.when(plane <= 1)
        def _():
            edge_in[k] = start[column]

        @pl.when(odd == 1)
        def _():
            u = edge_in[k]
            for j in range(GROUP):
                arrival(k, first, j)
                u = advance(k, first, j, u)
            edge_in[k] = u

        u = edge_in[k]
        for j in range(GROUP):
            u_out[k, j] = u

            @pl.when(column != j)
            def _():
                u_copy(k, j).start()
                arrival(k, first, GROUP + j)

            u = advance(k, first, GROUP + j, u)
        edge_out[k] = u

        @pl.when((odd == 1) & (plane < planes - 2))
        def _():
            edge_copy(k, 2).start()
            edge_copy(k, 1).start()

        if first:
            announce(k)
        else:

            @pl.when(k < ITERS)
            def _():
                announce(k)

        u_in[k, column] = u_out[k, column]
        for d in range(1, GROUP):
            u_arrival(k, (column + d) % GROUP).wait_recv()

    def fine(k):
        field[...] = pack(u_in[k])

        def step(t, carry):
            m = k * (FINE_STEPS - 1) + t - 1
            q = field[...]

            @pl.when(t > 0)
            def _():
                for g in range(2):
                    tables = [q[n // 8, (n // 4) % 2, n % 4] for n in range(16)]
                    shared[m, me, g : g + 1, :] = exports(tables, fine_lane[g], fine_code[g])
                for d in others:
                    share_copy(m, (me + d) % peers).start()

            parts = packed_faces(q, fine_perm[...])
            total = fine_leak[...] + (parts[0] + parts[1]) + (parts[2] + parts[3])
            inverse = 1.0 / total
            base = (fine_store[...] * q + fine_source[...]) * inverse
            weights = [part * inverse for part in parts]

            @pl.when(t > 0)
            def _():
                share_all(m).wait_recv()
                gathered[...] = shared[m]

            @pl.when(t == 0)
            def _():
                first_all(k).wait_recv()
                total = first_in[k, 0:peers]
                for f in range(1, GROUP):
                    total = total + first_in[k, f * peers : (f + 1) * peers]
                gathered[...] = total

            rows = trace_row[...]
            lanes = trace_lane[...]
            value = jnp.zeros((8, 128), jnp.float32)
            for n in range(2 * peers):
                line = jnp.broadcast_to(gathered[n // 2, n % 2 : n % 2 + 1, :], (8, 128))
                value = jnp.where(rows == n, pick(line, lanes), value)
            base = base + scatter(terms(weight[...] * value, 2)) * inverse
            v = q
            for _ in range(SWEEPS):
                v = packed_sweep(v, base, weights)
            field[...] = v
            return carry

        lax.fori_loop(0, FINE_STEPS, step, 0)
        f_out[k] = unpack(field[...])

        @pl.when(odd == 0)
        def _():
            for d in (2, 1, 3, 0):
                f_copy(k, 1, (column + d) % GROUP).start()

        for d in (2, 1, 3):
            f_copy(k, 0, (column + d) % GROUP).start()
        f_in[k, GROUP + column] = f_out[k, column]

    chain(0, True)

    def iteration(k, carry):
        fine(k)
        chain(k + 1, False)
        return carry

    lax.fori_loop(0, ITERS, iteration, 0)

    for f in range(GROUP):
        for r in range(4):
            out_ref[pl.ds(f * 32 + r, 8, stride=4), :] = u_in[ITERS, f, r]

    for d in range(1, GROUP):
        other = (column + d) % GROUP
        source_copy(0, other).wait_send()
        for k in range(ITERS + 1):
            u_copy(k, other).wait_send()
        for k in range(ITERS):
            f_copy(k, 0, other).wait_send()

    @pl.when(odd == 0)
    def _():
        for f in range(GROUP):
            source_copy(1, f).wait_send()
            for k in range(ITERS):
                f_copy(k, 1, f).wait_send()

    @pl.when((odd == 1) & (plane < planes - 2))
    def _():
        for k in range(ITERS + 1):
            for ahead in (1, 2):
                edge_copy(k, ahead).wait_send()

    for k in range(ITERS):
        first_all(k).wait_send()
    for m in range(ITERS * (FINE_STEPS - 1)):
        share_all(m).wait_send()


def body(
    pressure0,
    storage,
    perm_base,
    leakoff,
    sources,
    export_cells,
    inter_local,
    trace_source,
    inter_trans,
    inter_count,
):
    planes = lax.axis_size("tm") // GROUP
    peers = lax.axis_size("frac")
    flat = lambda a: a.reshape(128, 128)
    vmem = pl.BlockSpec(memory_space=pltpu.VMEM)
    f32 = jnp.float32
    block = (4, 8, 128)
    whole = (GROUP,) + block
    packed = (GROUP // 2, 2) + block
    shares = ITERS * (FINE_STEPS - 1)
    slots = 2 * GROUP
    out = pl.pallas_call(
        functools.partial(kernel, planes, peers),
        out_shape=jax.ShapeDtypeStruct((128, 128), f32),
        in_specs=[pl.BlockSpec(memory_space=pltpu.SMEM)]
        + [pl.BlockSpec(memory_space=pl.ANY)] * 9,
        out_specs=vmem,
        scratch_shapes=[
            pltpu.VMEM((128, 128), f32),
            pltpu.VMEM((128, 128), f32),
            pltpu.VMEM((128, 128), f32),
            pltpu.VMEM((128, 128), f32),
            pltpu.VMEM((128, 128), f32),
            pltpu.VMEM((2, 128), jnp.int32),
            pltpu.VMEM((8, 128), jnp.int32),
            pltpu.VMEM((8, 128), jnp.int32),
            pltpu.VMEM((8, 128), f32),
            pltpu.VMEM(whole, f32),
            pltpu.VMEM(whole, f32),
            pltpu.VMEM(whole, f32),
            pltpu.VMEM(whole, f32),
            pltpu.VMEM(packed, f32),
            pltpu.VMEM(packed, f32),
            pltpu.VMEM(packed, f32),
            pltpu.VMEM(packed, f32),
            pltpu.VMEM(whole, f32),
            pltpu.VMEM((slots,) + block, f32),
            pltpu.VMEM((ITERS + 1,) + whole, f32),
            pltpu.VMEM((ITERS + 1,) + whole, f32),
            pltpu.VMEM((ITERS,) + whole, f32),
            pltpu.VMEM((ITERS, slots) + block, f32),
            pltpu.VMEM((ITERS + 1,) + block, f32),
            pltpu.VMEM((ITERS + 1,) + block, f32),
            pltpu.VMEM((slots,) + block, f32),
            pltpu.VMEM((ITERS, GROUP, 2, 128), f32),
            pltpu.VMEM((ITERS, GROUP * peers, 2, 128), f32),
            pltpu.VMEM((shares, peers, 2, 128), f32),
            pltpu.VMEM((peers, 2, 128), f32),
            pltpu.VMEM(packed, f32),
            pltpu.VMEM((64, 1024), jnp.bfloat16),
            pltpu.VMEM((1024, 256), jnp.bfloat16),
            pltpu.VMEM((2, 8, 128), jnp.int32),
            pltpu.VMEM((2, 8, 128), jnp.int32),
            pltpu.VMEM((2, 8, 128), jnp.int32),
            pltpu.VMEM((2, 8, 128), jnp.int32),
            pltpu.VMEM((8, 128), jnp.int32),
            pltpu.VMEM((8, 128), jnp.int32),
            pltpu.VMEM((8, 128), f32),
            pltpu.SemaphoreType.DMA((9,)),
            pltpu.SemaphoreType.DMA((2, GROUP)),
            pltpu.SemaphoreType.DMA((slots,)),
            pltpu.SemaphoreType.DMA((ITERS + 1, GROUP)),
            pltpu.SemaphoreType.DMA((ITERS + 1, GROUP)),
            pltpu.SemaphoreType.DMA((ITERS, 2, GROUP)),
            pltpu.SemaphoreType.DMA((ITERS, slots)),
            pltpu.SemaphoreType.DMA((ITERS + 1, 2)),
            pltpu.SemaphoreType.DMA((ITERS + 1,)),
            pltpu.SemaphoreType.DMA((ITERS,)),
            pltpu.SemaphoreType.DMA((ITERS,)),
            pltpu.SemaphoreType.DMA((shares,)),
            pltpu.SemaphoreType.DMA((shares,)),
        ],
        compiler_params=pltpu.CompilerParams(
            collective_id=0, has_side_effects=True
        ),
        name="parareal",
    )(
        inter_count,
        flat(pressure0),
        flat(storage),
        flat(perm_base),
        flat(leakoff),
        flat(sources),
        export_cells.reshape(2, 128),
        inter_local.reshape(8, 128),
        trace_source.reshape(8, 128),
        inter_trans.reshape(8, 128),
    )
    return out.reshape(sources.shape)


def solution(mesh):
    placed = (
        P("frac", None, None),
        P("frac", None, None),
        P("frac", None, None),
        P("frac", None, None),
        P("tm", "frac", None, None),
        P("frac"),
        P("frac"),
        P("frac"),
        P("frac"),
        P("frac"),
    )
    return jax.shard_map(
        body, mesh=mesh, in_specs=placed, out_specs=P("tm", "frac", None, None), check_vma=False
    )
```

```python
import functools

import jax
import jax.numpy as jnp
from jax import lax
from jax.experimental import pallas as pl
from jax.experimental.pallas import tpu as pltpu
from jax.sharding import PartitionSpec as P

FINE_STEPS = 4
SWEEPS = 8
COARSE_SWEEPS = 2
ITERS = 2
GROUP = 4

stress_factor = 0.15
fine_size = 0.25


def next_rows(v):
    return jnp.concatenate(
        [v[..., 1:, :, :], pltpu.roll(v[..., :1, :, :], 7, v.ndim - 2)], axis=v.ndim - 3
    )


def prev_rows(v):
    return jnp.concatenate(
        [pltpu.roll(v[..., 3:, :, :], 1, v.ndim - 2), v[..., :3, :, :]], axis=v.ndim - 3
    )


def next_cols(v):
    return pltpu.roll(v, 127, v.ndim - 1)


def prev_cols(v):
    return pltpu.roll(v, 1, v.ndim - 1)


def iota(shape, axis):
    return lax.broadcasted_iota(jnp.int32, shape, len(shape) + axis)


def row_halves(shape):
    block, sub = iota(shape, -3), iota(shape, -2)
    return (
        jnp.where((block == 3) & (sub == 7), 0.0, 0.5),
        jnp.where((block == 0) & (sub == 0), 0.0, 0.5),
    )


def packed_next(v):
    return jnp.concatenate([v[:, 1:], pltpu.roll(v[:, :1], 127, v.ndim - 1)], axis=1)


def packed_prev(v):
    return jnp.concatenate([pltpu.roll(v[:, 1:], 1, v.ndim - 1), v[:, :1]], axis=1)


def packed_faces(pressure, perm):
    conductivity = perm * jnp.exp(stress_factor * pressure)
    shape = pressure.shape
    parity, place = iota(shape, -4), iota(shape, -1) & 63
    down, up = row_halves(shape)
    right = jnp.where((parity == 1) & (place == 63), 0.0, 0.5)
    left = jnp.where((parity == 0) & (place == 0), 0.0, 0.5)
    return (
        down * (conductivity + next_rows(conductivity)),
        up * (conductivity + prev_rows(conductivity)),
        right * (conductivity + packed_next(conductivity)),
        left * (conductivity + packed_prev(conductivity)),
    )


def packed_sweep(v, base, weights):
    down, up, right, left = weights
    return base + (down * next_rows(v) + up * prev_rows(v)) + (
        right * packed_next(v) + left * packed_prev(v)
    )


def coarse(pressure, source, store, perm, leak):
    conductivity = perm * jnp.exp(stress_factor * pressure)
    shape = pressure.shape
    lane = iota(shape, -1)
    down_half, up_half = row_halves(shape)
    down = down_half * (conductivity + next_rows(conductivity))
    up = up_half * (conductivity + prev_rows(conductivity))
    right = jnp.where(lane == 127, 0.0, 0.5) * (conductivity + next_cols(conductivity))
    left = jnp.where(lane == 0, 0.0, 0.5) * (conductivity + prev_cols(conductivity))
    inverse = 1.0 / (store + leak + (down + up) + (right + left))
    base = (store * pressure + source) * inverse
    down, up, right, left = down * inverse, up * inverse, right * inverse, left * inverse
    v = pressure
    for _ in range(COARSE_SWEEPS):
        v = base + (down * next_rows(v) + up * prev_rows(v)) + (
            right * next_cols(v) + left * prev_cols(v)
        )
    return v


def pick(table, lanes):
    return jnp.take_along_axis(table, lanes, axis=1, mode="promise_in_bounds")


def pack(blocks):
    lane = lax.broadcasted_iota(jnp.int32, (8, 128), 1)
    places = 2 * (lane & 63)
    pairs = []
    for p in range(GROUP // 2):
        for e in range(2):
            for r in range(4):
                low, high = pick(blocks[2 * p, r], places + e), pick(blocks[2 * p + 1, r], places + e)
                pairs.append(jnp.where(lane < 64, low, high))
    return jnp.stack(pairs).reshape(GROUP // 2, 2, 4, 8, 128)


def unpack(packed):
    lane = lax.broadcasted_iota(jnp.int32, (8, 128), 1)
    places = lane >> 1
    blocks = []
    for f in range(GROUP):
        for r in range(4):
            even, odd = [pick(packed[f // 2, e, r], places + 64 * (f % 2)) for e in range(2)]
            blocks.append(jnp.where((lane & 1) == 0, even, odd))
    return jnp.stack(blocks).reshape(GROUP, 4, 8, 128)


def kernel(
    planes,
    peers,
    count_ref,
    pressure_hbm,
    storage_hbm,
    perm_hbm,
    leak_hbm,
    source_hbm,
    export_hbm,
    local_hbm,
    trace_hbm,
    trans_hbm,
    out_ref,
    pressure_ref,
    storage_ref,
    perm_ref,
    leak_ref,
    source_ref,
    export_ref,
    local_ref,
    trace_ref,
    trans_ref,
    start,
    store,
    perm,
    leak,
    fine_store,
    fine_perm,
    fine_leak,
    fine_source,
    own_source,
    source_in,
    u_out,
    u_in,
    f_out,
    f_in,
    edge_in,
    edge_out,
    coarse_old,
    first_out,
    first_in,
    shared,
    gathered,
    field,
    row_hot,
    lane_hot,
    export_lane,
    export_code,
    fine_lane,
    fine_code,
    trace_lane,
    trace_row,
    weight,
    fetched,
    source_send,
    source_recv,
    u_send,
    u_recv,
    f_send,
    f_recv,
    edge_send,
    edge_recv,
    first_send,
    first_recv,
    share_send,
    share_recv,
):
    slice_index = lax.axis_index("tm")
    me = lax.axis_index("frac")
    plane = slice_index // GROUP
    column = slice_index % GROUP
    odd = plane % 2
    handed = odd * ((plane < planes - 1).astype(jnp.int32) + (plane < planes - 2).astype(jnp.int32))
    others = sorted(range(1, peers), key=lambda d: -min(d, peers - d))

    barrier = pltpu.get_barrier_semaphore()
    for d in others:
        pl.semaphore_signal(
            barrier, inc=1, device_id={"tm": slice_index, "frac": (me + d) % peers}
        )
    for d in range(1, GROUP):
        pl.semaphore_signal(
            barrier,
            inc=1,
            device_id={"tm": plane * GROUP + (column + d) % GROUP, "frac": me},
        )

    @pl.when(odd == 1)
    def _():
        for x in range(GROUP):
            pl.semaphore_signal(
                barrier, inc=1, device_id={"tm": (plane - 1) * GROUP + x, "frac": me}
            )

    @pl.when(plane > 1)
    def _():
        pl.semaphore_signal(
            barrier, inc=1, device_id={"tm": slice_index - (1 + odd) * GROUP, "frac": me}
        )

    pairs = (
        (source_hbm, source_ref),
        (pressure_hbm, pressure_ref),
        (storage_hbm, storage_ref),
        (perm_hbm, perm_ref),
        (leak_hbm, leak_ref),
        (export_hbm, export_ref),
        (local_hbm, local_ref),
        (trace_hbm, trace_ref),
        (trans_hbm, trans_ref),
    )
    fetches = [
        pltpu.make_async_copy(origin, target, fetched.at[n])
        for n, (origin, target) in enumerate(pairs)
    ]
    for fetch in fetches:
        fetch.start()
    fetches[0].wait()
    for f in range(GROUP):
        for r in range(4):
            own_source[f, r] = source_ref[pl.ds(f * 32 + r, 8, stride=4), :]

    pl.semaphore_wait(barrier, peers - 1 + GROUP - 1 + (1 - odd) * GROUP + handed)

    def source_copy(ahead, target):
        slot = (1 - ahead) * GROUP + column
        return pltpu.make_async_remote_copy(
            src_ref=own_source.at[target],
            dst_ref=source_in.at[slot],
            send_sem=source_send.at[ahead, target],
            recv_sem=source_recv.at[slot],
            device_id={"tm": (plane + ahead) * GROUP + target, "frac": me},
        )

    def source_arrival(slot):
        return pltpu.make_async_remote_copy(
            src_ref=own_source.at[0],
            dst_ref=source_in.at[slot],
            send_sem=source_send.at[0, 0],
            recv_sem=source_recv.at[slot],
            device_id={"tm": plane * GROUP + (column + 1) % GROUP, "frac": me},
        )

    def u_copy(k, target):
        return pltpu.make_async_remote_copy(
            src_ref=u_out.at[k, target],
            dst_ref=u_in.at[k, column],
            send_sem=u_send.at[k, target],
            recv_sem=u_recv.at[k, column],
            device_id={"tm": plane * GROUP + target, "frac": me},
        )

    def u_arrival(k, origin):
        return pltpu.make_async_remote_copy(
            src_ref=u_out.at[k, origin],
            dst_ref=u_in.at[k, origin],
            send_sem=u_send.at[k, origin],
            recv_sem=u_recv.at[k, origin],
            device_id={"tm": plane * GROUP + origin, "frac": me},
        )

    def f_copy(k, ahead, target):
        slot = (1 - ahead) * GROUP + column
        return pltpu.make_async_remote_copy(
            src_ref=f_out.at[k, target],
            dst_ref=f_in.at[k, slot],
            send_sem=f_send.at[k, ahead, target],
            recv_sem=f_recv.at[k, slot],
            device_id={"tm": (plane + ahead) * GROUP + target, "frac": me},
        )

    def f_arrival(k, slot):
        return pltpu.make_async_remote_copy(
            src_ref=f_out.at[k, 0],
            dst_ref=f_in.at[k, slot],
            send_sem=f_send.at[k, 0, 0],
            recv_sem=f_recv.at[k, slot],
            device_id={"tm": plane * GROUP + (column + 1) % GROUP, "frac": me},
        )

    def edge_copy(k, ahead):
        return pltpu.make_async_remote_copy(
            src_ref=edge_out.at[k],
            dst_ref=edge_in.at[k],
            send_sem=edge_send.at[k, ahead - 1],
            recv_sem=edge_recv.at[k],
            device_id={"tm": slice_index + ahead * GROUP, "frac": me},
        )

    def edge_arrival(k):
        return pltpu.make_async_remote_copy(
            src_ref=edge_out.at[k],
            dst_ref=edge_in.at[k],
            send_sem=edge_send.at[k, 0],
            recv_sem=edge_recv.at[k],
            device_id={"tm": slice_index - GROUP, "frac": me},
        )

    def first_copy(k, target, peer):
        return pltpu.make_async_remote_copy(
            src_ref=first_out.at[k, target],
            dst_ref=first_in.at[k, column * peers + me],
            send_sem=first_send.at[k],
            recv_sem=first_recv.at[k],
            device_id={"tm": plane * GROUP + target, "frac": peer},
        )

    def first_all(k):
        return pltpu.make_async_remote_copy(
            src_ref=first_in.at[k, pl.ds(0, GROUP * peers - 1)],
            dst_ref=first_in.at[k, pl.ds(0, GROUP * peers - 1)],
            send_sem=first_send.at[k],
            recv_sem=first_recv.at[k],
            device_id={"tm": slice_index, "frac": (me + 1) % peers},
        )

    def share_copy(m, target):
        return pltpu.make_async_remote_copy(
            src_ref=shared.at[m, me],
            dst_ref=shared.at[m, me],
            send_sem=share_send.at[m],
            recv_sem=share_recv.at[m],
            device_id={"tm": slice_index, "frac": target},
        )

    def share_all(m):
        return pltpu.make_async_remote_copy(
            src_ref=shared.at[m, pl.ds(0, peers - 1)],
            dst_ref=shared.at[m, pl.ds(0, peers - 1)],
            send_sem=share_send.at[m],
            recv_sem=share_recv.at[m],
            device_id={"tm": slice_index, "frac": (me + 1) % peers},
        )

    @pl.when(odd == 0)
    def _():
        for d in (2, 1, 3, 0):
            source_copy(1, (column + d) % GROUP).start()

    for d in (2, 1, 3):
        source_copy(0, (column + d) % GROUP).start()
    source_in[GROUP + column] = own_source[column]

    for fetch in fetches[1:]:
        fetch.wait()

    for f in range(GROUP):
        for r in range(4):
            rows = pl.ds(f * 32 + r, 8, stride=4)
            start[f, r] = pressure_ref[rows, :]
            store[f, r] = storage_ref[rows, :]
            perm[f, r] = perm_ref[rows, :]
            leak[f, r] = leak_ref[rows, :]

    sub8 = lax.broadcasted_iota(jnp.int32, (8, 128), 0)
    lane8 = lax.broadcasted_iota(jnp.int32, (8, 128), 1)
    for g in range(2):
        cell = jnp.broadcast_to(export_ref[g : g + 1, :], (8, 128))
        row = (cell >> 7) & 31
        export_lane[g] = cell & 127
        export_code[g] = jnp.where((row >> 2) == sub8, (cell >> 12) * 4 + (row & 3), -1)
        fine_lane[g] = ((cell >> 12) & 1) * 64 + ((cell & 127) >> 1)
        number = (cell >> 13) * 8 + (cell & 1) * 4 + (row & 3)
        fine_code[g] = jnp.where((row >> 2) == sub8, number, -1)
    slot = trace_ref[...]
    trace_lane[...] = slot & 127
    trace_row[...] = slot >> 7
    live = (sub8 * 128 + lane8) < count_ref[0]
    weight[...] = jnp.where(live, trans_ref[...], 0.0)
    cell = local_ref[...]
    cell_row = (cell >> 7) & 31
    code = (cell & 1) * 32 + (cell_row & 3) * 8 + (cell_row >> 2)
    cell_column = (cell >> 13) * 128 + ((cell >> 12) & 1) * 64 + ((cell & 127) >> 1)
    number = lax.broadcasted_iota(jnp.int32, (64, 128), 0)
    column_number = lax.broadcasted_iota(jnp.int32, (256, 128), 0)
    for t in range(8):
        rows_t = jnp.broadcast_to(code[t : t + 1, :], (64, 128))
        row_hot[:, t * 128 : (t + 1) * 128] = jnp.where(rows_t == number, 1.0, 0.0).astype(
            jnp.bfloat16
        )
        columns_t = jnp.broadcast_to(cell_column[t : t + 1, :], (256, 128))
        hot = jnp.where(columns_t == column_number, 1.0, 0.0)
        lane_hot[t * 128 : (t + 1) * 128, :] = hot.T.astype(jnp.bfloat16)

    def scatter(parts):
        rows = []
        for part in parts:
            line = jnp.concatenate([part[t : t + 1, :] for t in range(8)], axis=1)
            line = jnp.broadcast_to(line, (16, 1024)).astype(jnp.bfloat16)
            rows.append((row_hot[...].reshape(4, 16, 1024) * line[None]).reshape(64, 1024))
        left = jnp.concatenate(rows, axis=0)
        total = jnp.dot(left, lane_hot[...], preferred_element_type=jnp.float32)
        result = total[:64]
        for n in range(1, len(parts)):
            result = result + total[n * 64 : (n + 1) * 64]
        halves = [result[:, h * 128 : (h + 1) * 128].reshape(1, 2, 4, 8, 128) for h in (0, 1)]
        return jnp.concatenate(halves, axis=0)

    def terms(value, number_of):
        parts = []
        for _ in range(number_of):
            part = value.astype(jnp.bfloat16).astype(jnp.float32)
            parts.append(part)
            value = value - part
        return parts

    rate = pack(store[...]) * (1.0 / fine_size)
    fine_store[...] = rate
    fine_perm[...] = pack(perm[...])
    fine_leak[...] = rate + pack(leak[...]) + scatter(terms(weight[...], 3))
    fine_source[...] = pack(own_source[...])


    def exports(tables, lanes, codes):
        found = jnp.zeros((8, 128), jnp.float32)
        for n, table in enumerate(tables):
            found = jnp.where(codes == n, pick(table, lanes), found)
        return jnp.sum(found, axis=0, keepdims=True)

    def announce(k):
        for j in range(GROUP):
            u = u_out[k, j]
            for g in range(2):
                first_out[k, j, g : g + 1, :] = exports(
                    [u[r] for r in range(4)], export_lane[g], export_code[g] - 4 * column
                )

        for d in others:
            for j in range(GROUP):
                first_copy(k, j, (me + d) % peers).start()
        for d in range(1, GROUP):
            first_copy(k, (column + d) % GROUP, me).start()
        first_in[k, column * peers + me] = first_out[k, column]

    def advance(k, first, slot, u):
        following = coarse(u, source_in[slot], store[column], perm[column], leak[column])
        if first:
            u = following
        else:
            u = following + (f_in[k - 1, slot] - coarse_old[slot])
        coarse_old[slot] = following
        return u

    def arrival(k, first, slot):
        if first:
            source_arrival(slot).wait_recv()
        else:
            f_arrival(k - 1, slot).wait_recv()

    def chain(k, first):
        @pl.when(plane > 1)
        def _():
            edge_arrival(k).wait_recv()

        @pl.when(plane <= 1)
        def _():
            edge_in[k] = start[column]

        @pl.when(odd == 1)
        def _():
            u = edge_in[k]
            for j in range(GROUP):
                arrival(k, first, j)
                u = advance(k, first, j, u)
            edge_in[k] = u

        u = edge_in[k]
        for j in range(GROUP):
            u_out[k, j] = u

            @pl.when(column != j)
            def _():
                u_copy(k, j).start()
                arrival(k, first, GROUP + j)

            u = advance(k, first, GROUP + j, u)
        edge_out[k] = u

        @pl.when((odd == 1) & (plane < planes - 2))
        def _():
            edge_copy(k, 2).start()
            edge_copy(k, 1).start()

        if first:
            announce(k)
        else:

            @pl.when(k < ITERS)
            def _():
                announce(k)

        u_in[k, column] = u_out[k, column]
        for d in range(1, GROUP):
            u_arrival(k, (column + d) % GROUP).wait_recv()

    def fine(k):
        field[...] = pack(u_in[k])

        def step(t, carry):
            m = k * (FINE_STEPS - 1) + t - 1
            q = field[...]

            @pl.when(t > 0)
            def _():
                for g in range(2):
                    tables = [q[n // 8, (n // 4) % 2, n % 4] for n in range(16)]
                    shared[m, me, g : g + 1, :] = exports(tables, fine_lane[g], fine_code[g])
                for d in others:
                    share_copy(m, (me + d) % peers).start()

            parts = packed_faces(q, fine_perm[...])
            total = fine_leak[...] + (parts[0] + parts[1]) + (parts[2] + parts[3])
            inverse = 1.0 / total
            base = (fine_store[...] * q + fine_source[...]) * inverse
            weights = [part * inverse for part in parts]

            @pl.when(t > 0)
            def _():
                share_all(m).wait_recv()
                gathered[...] = shared[m]

            @pl.when(t == 0)
            def _():
                first_all(k).wait_recv()
                total = first_in[k, 0:peers]
                for f in range(1, GROUP):
                    total = total + first_in[k, f * peers : (f + 1) * peers]
                gathered[...] = total

            rows = trace_row[...]
            lanes = trace_lane[...]
            value = jnp.zeros((8, 128), jnp.float32)
            for n in range(2 * peers):
                line = jnp.broadcast_to(gathered[n // 2, n % 2 : n % 2 + 1, :], (8, 128))
                value = jnp.where(rows == n, pick(line, lanes), value)
            base = base + scatter(terms(weight[...] * value, 2)) * inverse
            v = q
            for _ in range(SWEEPS):
                v = packed_sweep(v, base, weights)
            field[...] = v
            return carry

        lax.fori_loop(0, FINE_STEPS, step, 0)
        f_out[k] = unpack(field[...])

        @pl.when(odd == 0)
        def _():
            for d in (2, 1, 3, 0):
                f_copy(k, 1, (column + d) % GROUP).start()

        for d in (2, 1, 3):
            f_copy(k, 0, (column + d) % GROUP).start()
        f_in[k, GROUP + column] = f_out[k, column]

    chain(0, True)

    def iteration(k, carry):
        fine(k)
        chain(k + 1, False)
        return carry

    lax.fori_loop(0, ITERS, iteration, 0)

    for f in range(GROUP):
        for r in range(4):
            out_ref[pl.ds(f * 32 + r, 8, stride=4), :] = u_in[ITERS, f, r]

    for d in range(1, GROUP):
        other = (column + d) % GROUP
        source_copy(0, other).wait_send()
        for k in range(ITERS + 1):
            u_copy(k, other).wait_send()
        for k in range(ITERS):
            f_copy(k, 0, other).wait_send()

    @pl.when(odd == 0)
    def _():
        for f in range(GROUP):
            source_copy(1, f).wait_send()
            for k in range(ITERS):
                f_copy(k, 1, f).wait_send()

    @pl.when((odd == 1) & (plane < planes - 2))
    def _():
        for k in range(ITERS + 1):
            for ahead in (1, 2):
                edge_copy(k, ahead).wait_send()

    for k in range(ITERS):
        first_all(k).wait_send()
    for m in range(ITERS * (FINE_STEPS - 1)):
        share_all(m).wait_send()


def body(
    pressure0,
    storage,
    perm_base,
    leakoff,
    sources,
    export_cells,
    inter_local,
    trace_source,
    inter_trans,
    inter_count,
):
    planes = lax.axis_size("tm") // GROUP
    peers = lax.axis_size("frac")
    flat = lambda a: a.reshape(128, 128)
    vmem = pl.BlockSpec(memory_space=pltpu.VMEM)
    f32 = jnp.float32
    block = (4, 8, 128)
    whole = (GROUP,) + block
    packed = (GROUP // 2, 2) + block
    shares = ITERS * (FINE_STEPS - 1)
    slots = 2 * GROUP
    out = pl.pallas_call(
        functools.partial(kernel, planes, peers),
        out_shape=jax.ShapeDtypeStruct((128, 128), f32),
        in_specs=[pl.BlockSpec(memory_space=pltpu.SMEM)]
        + [pl.BlockSpec(memory_space=pl.ANY)] * 9,
        out_specs=vmem,
        scratch_shapes=[
            pltpu.VMEM((128, 128), f32),
            pltpu.VMEM((128, 128), f32),
            pltpu.VMEM((128, 128), f32),
            pltpu.VMEM((128, 128), f32),
            pltpu.VMEM((128, 128), f32),
            pltpu.VMEM((2, 128), jnp.int32),
            pltpu.VMEM((8, 128), jnp.int32),
            pltpu.VMEM((8, 128), jnp.int32),
            pltpu.VMEM((8, 128), f32),
            pltpu.VMEM(whole, f32),
            pltpu.VMEM(whole, f32),
            pltpu.VMEM(whole, f32),
            pltpu.VMEM(whole, f32),
            pltpu.VMEM(packed, f32),
            pltpu.VMEM(packed, f32),
            pltpu.VMEM(packed, f32),
            pltpu.VMEM(packed, f32),
            pltpu.VMEM(whole, f32),
            pltpu.VMEM((slots,) + block, f32),
            pltpu.VMEM((ITERS + 1,) + whole, f32),
            pltpu.VMEM((ITERS + 1,) + whole, f32),
            pltpu.VMEM((ITERS,) + whole, f32),
            pltpu.VMEM((ITERS, slots) + block, f32),
            pltpu.VMEM((ITERS + 1,) + block, f32),
            pltpu.VMEM((ITERS + 1,) + block, f32),
            pltpu.VMEM((slots,) + block, f32),
            pltpu.VMEM((ITERS, GROUP, 2, 128), f32),
            pltpu.VMEM((ITERS, GROUP * peers, 2, 128), f32),
            pltpu.VMEM((shares, peers, 2, 128), f32),
            pltpu.VMEM((peers, 2, 128), f32),
            pltpu.VMEM(packed, f32),
            pltpu.VMEM((64, 1024), jnp.bfloat16),
            pltpu.VMEM((1024, 256), jnp.bfloat16),
            pltpu.VMEM((2, 8, 128), jnp.int32),
            pltpu.VMEM((2, 8, 128), jnp.int32),
            pltpu.VMEM((2, 8, 128), jnp.int32),
            pltpu.VMEM((2, 8, 128), jnp.int32),
            pltpu.VMEM((8, 128), jnp.int32),
            pltpu.VMEM((8, 128), jnp.int32),
            pltpu.VMEM((8, 128), f32),
            pltpu.SemaphoreType.DMA((9,)),
            pltpu.SemaphoreType.DMA((2, GROUP)),
            pltpu.SemaphoreType.DMA((slots,)),
            pltpu.SemaphoreType.DMA((ITERS + 1, GROUP)),
            pltpu.SemaphoreType.DMA((ITERS + 1, GROUP)),
            pltpu.SemaphoreType.DMA((ITERS, 2, GROUP)),
            pltpu.SemaphoreType.DMA((ITERS, slots)),
            pltpu.SemaphoreType.DMA((ITERS + 1, 2)),
            pltpu.SemaphoreType.DMA((ITERS + 1,)),
            pltpu.SemaphoreType.DMA((ITERS,)),
            pltpu.SemaphoreType.DMA((ITERS,)),
            pltpu.SemaphoreType.DMA((shares,)),
            pltpu.SemaphoreType.DMA((shares,)),
        ],
        compiler_params=pltpu.CompilerParams(
            collective_id=0, has_side_effects=True
        ),
        name="parareal",
    )(
        inter_count,
        flat(pressure0),
        flat(storage),
        flat(perm_base),
        flat(leakoff),
        flat(sources),
        export_cells.reshape(2, 128),
        inter_local.reshape(8, 128),
        trace_source.reshape(8, 128),
        inter_trans.reshape(8, 128),
    )
    return out.reshape(sources.shape)


def solution(mesh):
    placed = (
        P("frac", None, None),
        P("frac", None, None),
        P("frac", None, None),
        P("frac", None, None),
        P("tm", "frac", None, None),
        P("frac"),
        P("frac"),
        P("frac"),
        P("frac"),
        P("frac"),
    )
    return jax.shard_map(
        body, mesh=mesh, in_specs=placed, out_specs=P("tm", "frac", None, None), check_vma=False
    )
```

```python
import functools

import jax
import jax.numpy as jnp
from jax import lax
from jax.experimental import pallas as pl
from jax.experimental.pallas import tpu as pltpu
from jax.sharding import PartitionSpec as P

FINE_STEPS = 4
SWEEPS = 8
COARSE_SWEEPS = 2
ITERS = 2
GROUP = 4

stress_factor = 0.15
fine_size = 0.25


def next_rows(v):
    return jnp.concatenate(
        [v[..., 1:, :, :], pltpu.roll(v[..., :1, :, :], 7, v.ndim - 2)], axis=v.ndim - 3
    )


def prev_rows(v):
    return jnp.concatenate(
        [pltpu.roll(v[..., 3:, :, :], 1, v.ndim - 2), v[..., :3, :, :]], axis=v.ndim - 3
    )


def next_cols(v):
    return pltpu.roll(v, 127, v.ndim - 1)


def prev_cols(v):
    return pltpu.roll(v, 1, v.ndim - 1)


def iota(shape, axis):
    return lax.broadcasted_iota(jnp.int32, shape, len(shape) + axis)


def row_halves(shape):
    block, sub = iota(shape, -3), iota(shape, -2)
    return (
        jnp.where((block == 3) & (sub == 7), 0.0, 0.5),
        jnp.where((block == 0) & (sub == 0), 0.0, 0.5),
    )


def packed_next(v):
    return jnp.concatenate([v[:, 1:], pltpu.roll(v[:, :1], 127, v.ndim - 1)], axis=1)


def packed_prev(v):
    return jnp.concatenate([pltpu.roll(v[:, 1:], 1, v.ndim - 1), v[:, :1]], axis=1)


def packed_faces(pressure, perm):
    conductivity = perm * jnp.exp(stress_factor * pressure)
    shape = pressure.shape
    parity, place = iota(shape, -4), iota(shape, -1) & 63
    down, up = row_halves(shape)
    right = jnp.where((parity == 1) & (place == 63), 0.0, 0.5)
    left = jnp.where((parity == 0) & (place == 0), 0.0, 0.5)
    return (
        down * (conductivity + next_rows(conductivity)),
        up * (conductivity + prev_rows(conductivity)),
        right * (conductivity + packed_next(conductivity)),
        left * (conductivity + packed_prev(conductivity)),
    )


def packed_sweep(v, base, weights):
    down, up, right, left = weights
    return base + (down * next_rows(v) + up * prev_rows(v)) + (
        right * packed_next(v) + left * packed_prev(v)
    )


def coarse(pressure, source, store, perm, leak):
    conductivity = perm * jnp.exp(stress_factor * pressure)
    shape = pressure.shape
    lane = iota(shape, -1)
    down_half, up_half = row_halves(shape)
    down = down_half * (conductivity + next_rows(conductivity))
    up = up_half * (conductivity + prev_rows(conductivity))
    right = jnp.where(lane == 127, 0.0, 0.5) * (conductivity + next_cols(conductivity))
    left = jnp.where(lane == 0, 0.0, 0.5) * (conductivity + prev_cols(conductivity))
    inverse = 1.0 / (store + leak + (down + up) + (right + left))
    base = (store * pressure + source) * inverse
    down, up, right, left = down * inverse, up * inverse, right * inverse, left * inverse
    v = pressure
    for _ in range(COARSE_SWEEPS):
        v = base + (down * next_rows(v) + up * prev_rows(v)) + (
            right * next_cols(v) + left * prev_cols(v)
        )
    return v


def pick(table, lanes):
    return jnp.take_along_axis(table, lanes, axis=1, mode="promise_in_bounds")


def pack(blocks):
    lane = lax.broadcasted_iota(jnp.int32, (8, 128), 1)
    places = 2 * (lane & 63)
    pairs = []
    for p in range(GROUP // 2):
        for e in range(2):
            for r in range(4):
                low, high = pick(blocks[2 * p, r], places + e), pick(blocks[2 * p + 1, r], places + e)
                pairs.append(jnp.where(lane < 64, low, high))
    return jnp.stack(pairs).reshape(GROUP // 2, 2, 4, 8, 128)


def unpack(packed):
    lane = lax.broadcasted_iota(jnp.int32, (8, 128), 1)
    places = lane >> 1
    blocks = []
    for f in range(GROUP):
        for r in range(4):
            even, odd = [pick(packed[f // 2, e, r], places + 64 * (f % 2)) for e in range(2)]
            blocks.append(jnp.where((lane & 1) == 0, even, odd))
    return jnp.stack(blocks).reshape(GROUP, 4, 8, 128)


def kernel(
    planes,
    peers,
    count_ref,
    pressure_hbm,
    storage_hbm,
    perm_hbm,
    leak_hbm,
    source_hbm,
    export_hbm,
    local_hbm,
    trace_hbm,
    trans_hbm,
    out_ref,
    pressure_ref,
    storage_ref,
    perm_ref,
    leak_ref,
    source_ref,
    export_ref,
    local_ref,
    trace_ref,
    trans_ref,
    start,
    store,
    perm,
    leak,
    fine_store,
    fine_perm,
    fine_leak,
    fine_source,
    own_source,
    source_in,
    u_out,
    u_in,
    f_out,
    f_in,
    edge_in,
    edge_out,
    coarse_old,
    first_out,
    first_in,
    shared,
    gathered,
    field,
    row_hot,
    lane_hot,
    export_lane,
    export_code,
    fine_lane,
    fine_code,
    trace_lane,
    trace_row,
    weight,
    fetched,
    source_send,
    source_recv,
    u_send,
    u_recv,
    f_send,
    f_recv,
    edge_send,
    edge_recv,
    first_send,
    first_recv,
    share_send,
    share_recv,
):
    slice_index = lax.axis_index("tm")
    me = lax.axis_index("frac")
    plane = slice_index // GROUP
    column = slice_index % GROUP
    odd = plane % 2
    handed = odd * ((plane < planes - 1).astype(jnp.int32) + (plane < planes - 2).astype(jnp.int32))
    others = sorted(range(1, peers), key=lambda d: -min(d, peers - d))

    barrier = pltpu.get_barrier_semaphore()
    for d in others:
        pl.semaphore_signal(
            barrier, inc=1, device_id={"tm": slice_index, "frac": (me + d) % peers}
        )
    for d in range(1, GROUP):
        pl.semaphore_signal(
            barrier,
            inc=1,
            device_id={"tm": plane * GROUP + (column + d) % GROUP, "frac": me},
        )

    @pl.when(odd == 1)
    def _():
        for x in range(GROUP):
            pl.semaphore_signal(
                barrier, inc=1, device_id={"tm": (plane - 1) * GROUP + x, "frac": me}
            )

    @pl.when(plane > 1)
    def _():
        pl.semaphore_signal(
            barrier, inc=1, device_id={"tm": slice_index - (1 + odd) * GROUP, "frac": me}
        )

    pairs = (
        (source_hbm, source_ref),
        (pressure_hbm, pressure_ref),
        (storage_hbm, storage_ref),
        (perm_hbm, perm_ref),
        (leak_hbm, leak_ref),
        (export_hbm, export_ref),
        (local_hbm, local_ref),
        (trace_hbm, trace_ref),
        (trans_hbm, trans_ref),
    )
    fetches = [
        pltpu.make_async_copy(origin, target, fetched.at[n])
        for n, (origin, target) in enumerate(pairs)
    ]
    for fetch in fetches:
        fetch.start()
    fetches[0].wait()
    for f in range(GROUP):
        for r in range(4):
            own_source[f, r] = source_ref[pl.ds(f * 32 + r, 8, stride=4), :]

    pl.semaphore_wait(barrier, peers - 1 + GROUP - 1 + (1 - odd) * GROUP + handed)

    def source_copy(ahead, target):
        slot = (1 - ahead) * GROUP + column
        return pltpu.make_async_remote_copy(
            src_ref=own_source.at[target],
            dst_ref=source_in.at[slot],
            send_sem=source_send.at[ahead, target],
            recv_sem=source_recv.at[slot],
            device_id={"tm": (plane + ahead) * GROUP + target, "frac": me},
        )

    def source_arrival(slot):
        return pltpu.make_async_remote_copy(
            src_ref=own_source.at[0],
            dst_ref=source_in.at[slot],
            send_sem=source_send.at[0, 0],
            recv_sem=source_recv.at[slot],
            device_id={"tm": plane * GROUP + (column + 1) % GROUP, "frac": me},
        )

    def u_copy(k, target):
        return pltpu.make_async_remote_copy(
            src_ref=u_out.at[k, target],
            dst_ref=u_in.at[k, column],
            send_sem=u_send.at[k, target],
            recv_sem=u_recv.at[k, column],
            device_id={"tm": plane * GROUP + target, "frac": me},
        )

    def u_arrival(k, origin):
        return pltpu.make_async_remote_copy(
            src_ref=u_out.at[k, origin],
            dst_ref=u_in.at[k, origin],
            send_sem=u_send.at[k, origin],
            recv_sem=u_recv.at[k, origin],
            device_id={"tm": plane * GROUP + origin, "frac": me},
        )

    def f_copy(k, ahead, target):
        slot = (1 - ahead) * GROUP + column
        return pltpu.make_async_remote_copy(
            src_ref=f_out.at[k, target],
            dst_ref=f_in.at[k, slot],
            send_sem=f_send.at[k, ahead, target],
            recv_sem=f_recv.at[k, slot],
            device_id={"tm": (plane + ahead) * GROUP + target, "frac": me},
        )

    def f_arrival(k, slot):
        return pltpu.make_async_remote_copy(
            src_ref=f_out.at[k, 0],
            dst_ref=f_in.at[k, slot],
            send_sem=f_send.at[k, 0, 0],
            recv_sem=f_recv.at[k, slot],
            device_id={"tm": plane * GROUP + (column + 1) % GROUP, "frac": me},
        )

    def edge_copy(k, ahead):
        return pltpu.make_async_remote_copy(
            src_ref=edge_out.at[k],
            dst_ref=edge_in.at[k],
            send_sem=edge_send.at[k, ahead - 1],
            recv_sem=edge_recv.at[k],
            device_id={"tm": slice_index + ahead * GROUP, "frac": me},
        )

    def edge_arrival(k):
        return pltpu.make_async_remote_copy(
            src_ref=edge_out.at[k],
            dst_ref=edge_in.at[k],
            send_sem=edge_send.at[k, 0],
            recv_sem=edge_recv.at[k],
            device_id={"tm": slice_index - GROUP, "frac": me},
        )

    def first_copy(k, target, peer):
        return pltpu.make_async_remote_copy(
            src_ref=first_out.at[k, target],
            dst_ref=first_in.at[k, column * peers + me],
            send_sem=first_send.at[k],
            recv_sem=first_recv.at[k],
            device_id={"tm": plane * GROUP + target, "frac": peer},
        )

    def first_all(k):
        return pltpu.make_async_remote_copy(
            src_ref=first_in.at[k, pl.ds(0, GROUP * peers - 1)],
            dst_ref=first_in.at[k, pl.ds(0, GROUP * peers - 1)],
            send_sem=first_send.at[k],
            recv_sem=first_recv.at[k],
            device_id={"tm": slice_index, "frac": (me + 1) % peers},
        )

    def share_copy(m, target):
        return pltpu.make_async_remote_copy(
            src_ref=shared.at[m, me],
            dst_ref=shared.at[m, me],
            send_sem=share_send.at[m],
            recv_sem=share_recv.at[m],
            device_id={"tm": slice_index, "frac": target},
        )

    def share_all(m):
        return pltpu.make_async_remote_copy(
            src_ref=shared.at[m, pl.ds(0, peers - 1)],
            dst_ref=shared.at[m, pl.ds(0, peers - 1)],
            send_sem=share_send.at[m],
            recv_sem=share_recv.at[m],
            device_id={"tm": slice_index, "frac": (me + 1) % peers},
        )

    @pl.when(odd == 0)
    def _():
        for d in (2, 1, 3, 0):
            source_copy(1, (column + d) % GROUP).start()

    for d in (2, 1, 3):
        source_copy(0, (column + d) % GROUP).start()
    source_in[GROUP + column] = own_source[column]

    for fetch in fetches[1:]:
        fetch.wait()

    for f in range(GROUP):
        for r in range(4):
            rows = pl.ds(f * 32 + r, 8, stride=4)
            start[f, r] = pressure_ref[rows, :]
            store[f, r] = storage_ref[rows, :]
            perm[f, r] = perm_ref[rows, :]
            leak[f, r] = leak_ref[rows, :]

    sub8 = lax.broadcasted_iota(jnp.int32, (8, 128), 0)
    lane8 = lax.broadcasted_iota(jnp.int32, (8, 128), 1)
    for g in range(2):
        cell = jnp.broadcast_to(export_ref[g : g + 1, :], (8, 128))
        row = (cell >> 7) & 31
        export_lane[g] = cell & 127
        export_code[g] = jnp.where((row >> 2) == sub8, (cell >> 12) * 4 + (row & 3), -1)
        fine_lane[g] = ((cell >> 12) & 1) * 64 + ((cell & 127) >> 1)
        number = (cell >> 13) * 8 + (cell & 1) * 4 + (row & 3)
        fine_code[g] = jnp.where((row >> 2) == sub8, number, -1)
    slot = trace_ref[...]
    trace_lane[...] = slot & 127
    trace_row[...] = slot >> 7
    live = (sub8 * 128 + lane8) < count_ref[0]
    weight[...] = jnp.where(live, trans_ref[...], 0.0)
    cell = local_ref[...]
    cell_row = (cell >> 7) & 31
    code = (cell & 1) * 32 + (cell_row & 3) * 8 + (cell_row >> 2)
    cell_column = (cell >> 13) * 128 + ((cell >> 12) & 1) * 64 + ((cell & 127) >> 1)
    number = lax.broadcasted_iota(jnp.int32, (64, 128), 0)
    column_number = lax.broadcasted_iota(jnp.int32, (256, 128), 0)
    for t in range(8):
        rows_t = jnp.broadcast_to(code[t : t + 1, :], (64, 128))
        row_hot[:, t * 128 : (t + 1) * 128] = jnp.where(rows_t == number, 1.0, 0.0).astype(
            jnp.bfloat16
        )
        columns_t = jnp.broadcast_to(cell_column[t : t + 1, :], (256, 128))
        hot = jnp.where(columns_t == column_number, 1.0, 0.0)
        lane_hot[t * 128 : (t + 1) * 128, :] = hot.T.astype(jnp.bfloat16)

    def scatter(parts):
        rows = []
        for part in parts:
            line = jnp.concatenate([part[t : t + 1, :] for t in range(8)], axis=1)
            line = jnp.broadcast_to(line, (16, 1024)).astype(jnp.bfloat16)
            rows.append((row_hot[...].reshape(4, 16, 1024) * line[None]).reshape(64, 1024))
        left = jnp.concatenate(rows, axis=0)
        total = jnp.dot(left, lane_hot[...], preferred_element_type=jnp.float32)
        result = total[:64]
        for n in range(1, len(parts)):
            result = result + total[n * 64 : (n + 1) * 64]
        halves = [result[:, h * 128 : (h + 1) * 128].reshape(1, 2, 4, 8, 128) for h in (0, 1)]
        return jnp.concatenate(halves, axis=0)

    def terms(value, number_of):
        parts = []
        for _ in range(number_of):
            part = value.astype(jnp.bfloat16).astype(jnp.float32)
            parts.append(part)
            value = value - part
        return parts

    rate = pack(store[...]) * (1.0 / fine_size)
    fine_store[...] = rate
    fine_perm[...] = pack(perm[...])
    fine_leak[...] = rate + pack(leak[...]) + scatter(terms(weight[...], 3))
    fine_source[...] = pack(own_source[...])


    def exports(tables, lanes, codes):
        found = jnp.zeros((8, 128), jnp.float32)
        for n, table in enumerate(tables):
            found = jnp.where(codes == n, pick(table, lanes), found)
        return jnp.sum(found, axis=0, keepdims=True)

    def announce(k):
        for j in range(GROUP):
            u = u_out[k, j]
            for g in range(2):
                first_out[k, j, g : g + 1, :] = exports(
                    [u[r] for r in range(4)], export_lane[g], export_code[g] - 4 * column
                )

        for d in others:
            for j in range(GROUP):
                first_copy(k, j, (me + d) % peers).start()
        for d in range(1, GROUP):
            first_copy(k, (column + d) % GROUP, me).start()
        first_in[k, column * peers + me] = first_out[k, column]

    def advance(k, first, slot, u):
        following = coarse(u, source_in[slot], store[column], perm[column], leak[column])
        if first:
            u = following
        else:
            u = following + (f_in[k - 1, slot] - coarse_old[slot])
        coarse_old[slot] = following
        return u

    def arrival(k, first, slot):
        if first:
            source_arrival(slot).wait_recv()
        else:
            f_arrival(k - 1, slot).wait_recv()

    def chain(k, first):
        @pl.when(plane > 1)
        def _():
            edge_arrival(k).wait_recv()

        @pl.when(plane <= 1)
        def _():
            edge_in[k] = start[column]

        @pl.when(odd == 1)
        def _():
            u = edge_in[k]
            for j in range(GROUP):
                arrival(k, first, j)
                u = advance(k, first, j, u)
            edge_in[k] = u

        u = edge_in[k]
        for j in range(GROUP):
            u_out[k, j] = u

            @pl.when(column != j)
            def _():
                u_copy(k, j).start()
                arrival(k, first, GROUP + j)

            u = advance(k, first, GROUP + j, u)
        edge_out[k] = u

        @pl.when((odd == 1) & (plane < planes - 2))
        def _():
            edge_copy(k, 2).start()
            edge_copy(k, 1).start()

        if first:
            announce(k)
        else:

            @pl.when(k < ITERS)
            def _():
                announce(k)

        u_in[k, column] = u_out[k, column]
        for d in range(1, GROUP):
            u_arrival(k, (column + d) % GROUP).wait_recv()

    def fine(k):
        field[...] = pack(u_in[k])

        def step(t, carry):
            m = k * (FINE_STEPS - 1) + t - 1
            q = field[...]

            @pl.when(t > 0)
            def _():
                for g in range(2):
                    tables = [q[n // 8, (n // 4) % 2, n % 4] for n in range(16)]
                    shared[m, me, g : g + 1, :] = exports(tables, fine_lane[g], fine_code[g])
                for d in others:
                    share_copy(m, (me + d) % peers).start()

            parts = packed_faces(q, fine_perm[...])
            total = fine_leak[...] + (parts[0] + parts[1]) + (parts[2] + parts[3])
            inverse = 1.0 / total
            base = (fine_store[...] * q + fine_source[...]) * inverse
            weights = [part * inverse for part in parts]
            first_sweep = packed_sweep(q, base, weights)

            @pl.when(t > 0)
            def _():
                share_all(m).wait_recv()
                gathered[...] = shared[m]

            @pl.when(t == 0)
            def _():
                first_all(k).wait_recv()
                total = first_in[k, 0:peers]
                for f in range(1, GROUP):
                    total = total + first_in[k, f * peers : (f + 1) * peers]
                gathered[...] = total

            rows = trace_row[...]
            lanes = trace_lane[...]
            value = jnp.zeros((8, 128), jnp.float32)
            for n in range(2 * peers):
                line = jnp.broadcast_to(gathered[n // 2, n % 2 : n % 2 + 1, :], (8, 128))
                value = jnp.where(rows == n, pick(line, lanes), value)
            coupled = scatter(terms(weight[...] * value, 2)) * inverse
            base = base + coupled
            v = first_sweep + coupled
            for _ in range(SWEEPS - 1):
                v = packed_sweep(v, base, weights)
            field[...] = v
            return carry

        lax.fori_loop(0, FINE_STEPS, step, 0)
        f_out[k] = unpack(field[...])

        @pl.when(odd == 0)
        def _():
            for d in (2, 1, 3, 0):
                f_copy(k, 1, (column + d) % GROUP).start()

        for d in (2, 1, 3):
            f_copy(k, 0, (column + d) % GROUP).start()
        f_in[k, GROUP + column] = f_out[k, column]

    chain(0, True)

    def iteration(k, carry):
        fine(k)
        chain(k + 1, False)
        return carry

    lax.fori_loop(0, ITERS, iteration, 0)

    for f in range(GROUP):
        for r in range(4):
            out_ref[pl.ds(f * 32 + r, 8, stride=4), :] = u_in[ITERS, f, r]

    for d in range(1, GROUP):
        other = (column + d) % GROUP
        source_copy(0, other).wait_send()
        for k in range(ITERS + 1):
            u_copy(k, other).wait_send()
        for k in range(ITERS):
            f_copy(k, 0, other).wait_send()

    @pl.when(odd == 0)
    def _():
        for f in range(GROUP):
            source_copy(1, f).wait_send()
            for k in range(ITERS):
                f_copy(k, 1, f).wait_send()

    @pl.when((odd == 1) & (plane < planes - 2))
    def _():
        for k in range(ITERS + 1):
            for ahead in (1, 2):
                edge_copy(k, ahead).wait_send()

    for k in range(ITERS):
        first_all(k).wait_send()
    for m in range(ITERS * (FINE_STEPS - 1)):
        share_all(m).wait_send()


def body(
    pressure0,
    storage,
    perm_base,
    leakoff,
    sources,
    export_cells,
    inter_local,
    trace_source,
    inter_trans,
    inter_count,
):
    planes = lax.axis_size("tm") // GROUP
    peers = lax.axis_size("frac")
    flat = lambda a: a.reshape(128, 128)
    vmem = pl.BlockSpec(memory_space=pltpu.VMEM)
    f32 = jnp.float32
    block = (4, 8, 128)
    whole = (GROUP,) + block
    packed = (GROUP // 2, 2) + block
    shares = ITERS * (FINE_STEPS - 1)
    slots = 2 * GROUP
    out = pl.pallas_call(
        functools.partial(kernel, planes, peers),
        out_shape=jax.ShapeDtypeStruct((128, 128), f32),
        in_specs=[pl.BlockSpec(memory_space=pltpu.SMEM)]
        + [pl.BlockSpec(memory_space=pl.ANY)] * 9,
        out_specs=vmem,
        scratch_shapes=[
            pltpu.VMEM((128, 128), f32),
            pltpu.VMEM((128, 128), f32),
            pltpu.VMEM((128, 128), f32),
            pltpu.VMEM((128, 128), f32),
            pltpu.VMEM((128, 128), f32),
            pltpu.VMEM((2, 128), jnp.int32),
            pltpu.VMEM((8, 128), jnp.int32),
            pltpu.VMEM((8, 128), jnp.int32),
            pltpu.VMEM((8, 128), f32),
            pltpu.VMEM(whole, f32),
            pltpu.VMEM(whole, f32),
            pltpu.VMEM(whole, f32),
            pltpu.VMEM(whole, f32),
            pltpu.VMEM(packed, f32),
            pltpu.VMEM(packed, f32),
            pltpu.VMEM(packed, f32),
            pltpu.VMEM(packed, f32),
            pltpu.VMEM(whole, f32),
            pltpu.VMEM((slots,) + block, f32),
            pltpu.VMEM((ITERS + 1,) + whole, f32),
            pltpu.VMEM((ITERS + 1,) + whole, f32),
            pltpu.VMEM((ITERS,) + whole, f32),
            pltpu.VMEM((ITERS, slots) + block, f32),
            pltpu.VMEM((ITERS + 1,) + block, f32),
            pltpu.VMEM((ITERS + 1,) + block, f32),
            pltpu.VMEM((slots,) + block, f32),
            pltpu.VMEM((ITERS, GROUP, 2, 128), f32),
            pltpu.VMEM((ITERS, GROUP * peers, 2, 128), f32),
            pltpu.VMEM((shares, peers, 2, 128), f32),
            pltpu.VMEM((peers, 2, 128), f32),
            pltpu.VMEM(packed, f32),
            pltpu.VMEM((64, 1024), jnp.bfloat16),
            pltpu.VMEM((1024, 256), jnp.bfloat16),
            pltpu.VMEM((2, 8, 128), jnp.int32),
            pltpu.VMEM((2, 8, 128), jnp.int32),
            pltpu.VMEM((2, 8, 128), jnp.int32),
            pltpu.VMEM((2, 8, 128), jnp.int32),
            pltpu.VMEM((8, 128), jnp.int32),
            pltpu.VMEM((8, 128), jnp.int32),
            pltpu.VMEM((8, 128), f32),
            pltpu.SemaphoreType.DMA((9,)),
            pltpu.SemaphoreType.DMA((2, GROUP)),
            pltpu.SemaphoreType.DMA((slots,)),
            pltpu.SemaphoreType.DMA((ITERS + 1, GROUP)),
            pltpu.SemaphoreType.DMA((ITERS + 1, GROUP)),
            pltpu.SemaphoreType.DMA((ITERS, 2, GROUP)),
            pltpu.SemaphoreType.DMA((ITERS, slots)),
            pltpu.SemaphoreType.DMA((ITERS + 1, 2)),
            pltpu.SemaphoreType.DMA((ITERS + 1,)),
            pltpu.SemaphoreType.DMA((ITERS,)),
            pltpu.SemaphoreType.DMA((ITERS,)),
            pltpu.SemaphoreType.DMA((shares,)),
            pltpu.SemaphoreType.DMA((shares,)),
        ],
        compiler_params=pltpu.CompilerParams(
            collective_id=0, has_side_effects=True
        ),
        name="parareal",
    )(
        inter_count,
        flat(pressure0),
        flat(storage),
        flat(perm_base),
        flat(leakoff),
        flat(sources),
        export_cells.reshape(2, 128),
        inter_local.reshape(8, 128),
        trace_source.reshape(8, 128),
        inter_trans.reshape(8, 128),
    )
    return out.reshape(sources.shape)


def solution(mesh):
    placed = (
        P("frac", None, None),
        P("frac", None, None),
        P("frac", None, None),
        P("frac", None, None),
        P("tm", "frac", None, None),
        P("frac"),
        P("frac"),
        P("frac"),
        P("frac"),
        P("frac"),
    )
    return jax.shard_map(
        body, mesh=mesh, in_specs=placed, out_specs=P("tm", "frac", None, None), check_vma=False
    )
```

```python
import functools

import jax
import jax.numpy as jnp
from jax import lax
from jax.experimental import pallas as pl
from jax.experimental.pallas import tpu as pltpu
from jax.sharding import PartitionSpec as P

FINE_STEPS = 4
SWEEPS = 8
COARSE_SWEEPS = 2
ITERS = 2
GROUP = 4

stress_factor = 0.15
fine_size = 0.25


def next_rows(v):
    return jnp.concatenate(
        [v[..., 1:, :, :], pltpu.roll(v[..., :1, :, :], 7, v.ndim - 2)], axis=v.ndim - 3
    )


def prev_rows(v):
    return jnp.concatenate(
        [pltpu.roll(v[..., 3:, :, :], 1, v.ndim - 2), v[..., :3, :, :]], axis=v.ndim - 3
    )


def next_cols(v):
    return pltpu.roll(v, 127, v.ndim - 1)


def prev_cols(v):
    return pltpu.roll(v, 1, v.ndim - 1)


def iota(shape, axis):
    return lax.broadcasted_iota(jnp.int32, shape, len(shape) + axis)


def row_halves(shape):
    block, sub = iota(shape, -3), iota(shape, -2)
    return (
        jnp.where((block == 3) & (sub == 7), 0.0, 0.5),
        jnp.where((block == 0) & (sub == 0), 0.0, 0.5),
    )


def packed_next(v):
    return jnp.concatenate([v[:, 1:], pltpu.roll(v[:, :1], 127, v.ndim - 1)], axis=1)


def packed_prev(v):
    return jnp.concatenate([pltpu.roll(v[:, 1:], 1, v.ndim - 1), v[:, :1]], axis=1)


def packed_faces(pressure, perm):
    conductivity = perm * jnp.exp(stress_factor * pressure)
    shape = pressure.shape
    parity, place = iota(shape, -4), iota(shape, -1) & 63
    down, up = row_halves(shape)
    right = jnp.where((parity == 1) & (place == 63), 0.0, 0.5)
    left = jnp.where((parity == 0) & (place == 0), 0.0, 0.5)
    return (
        down * (conductivity + next_rows(conductivity)),
        up * (conductivity + prev_rows(conductivity)),
        right * (conductivity + packed_next(conductivity)),
        left * (conductivity + packed_prev(conductivity)),
    )


def packed_sweep(v, base, weights):
    down, up, right, left = weights
    return base + (down * next_rows(v) + up * prev_rows(v)) + (
        right * packed_next(v) + left * packed_prev(v)
    )


def coarse(pressure, source, store, perm, leak):
    conductivity = perm * jnp.exp(stress_factor * pressure)
    shape = pressure.shape
    lane = iota(shape, -1)
    down_half, up_half = row_halves(shape)
    down = down_half * (conductivity + next_rows(conductivity))
    up = up_half * (conductivity + prev_rows(conductivity))
    right = jnp.where(lane == 127, 0.0, 0.5) * (conductivity + next_cols(conductivity))
    left = jnp.where(lane == 0, 0.0, 0.5) * (conductivity + prev_cols(conductivity))
    inverse = 1.0 / (store + leak + (down + up) + (right + left))
    base = (store * pressure + source) * inverse
    down, up, right, left = down * inverse, up * inverse, right * inverse, left * inverse
    v = pressure
    for _ in range(COARSE_SWEEPS):
        v = base + (down * next_rows(v) + up * prev_rows(v)) + (
            right * next_cols(v) + left * prev_cols(v)
        )
    return v


def pick(table, lanes):
    return jnp.take_along_axis(table, lanes, axis=1, mode="promise_in_bounds")


def pack(blocks):
    lane = lax.broadcasted_iota(jnp.int32, (8, 128), 1)
    places = 2 * (lane & 63)
    pairs = []
    for p in range(GROUP // 2):
        for e in range(2):
            for r in range(4):
                low, high = pick(blocks[2 * p, r], places + e), pick(blocks[2 * p + 1, r], places + e)
                pairs.append(jnp.where(lane < 64, low, high))
    return jnp.stack(pairs).reshape(GROUP // 2, 2, 4, 8, 128)


def unpack(packed):
    lane = lax.broadcasted_iota(jnp.int32, (8, 128), 1)
    places = lane >> 1
    blocks = []
    for f in range(GROUP):
        for r in range(4):
            even, odd = [pick(packed[f // 2, e, r], places + 64 * (f % 2)) for e in range(2)]
            blocks.append(jnp.where((lane & 1) == 0, even, odd))
    return jnp.stack(blocks).reshape(GROUP, 4, 8, 128)


def kernel(
    planes,
    peers,
    count_hbm,
    pressure_hbm,
    storage_hbm,
    perm_hbm,
    leak_hbm,
    source_hbm,
    export_hbm,
    local_hbm,
    trace_hbm,
    trans_hbm,
    out_ref,
    count_ref,
    pressure_ref,
    storage_ref,
    perm_ref,
    leak_ref,
    source_ref,
    export_ref,
    local_ref,
    trace_ref,
    trans_ref,
    start,
    store,
    perm,
    leak,
    fine_store,
    fine_perm,
    fine_leak,
    fine_source,
    own_source,
    source_in,
    u_out,
    u_in,
    f_out,
    f_in,
    edge_in,
    edge_out,
    coarse_old,
    first_out,
    first_in,
    shared,
    gathered,
    field,
    row_hot,
    lane_hot,
    export_lane,
    export_code,
    fine_lane,
    fine_code,
    trace_lane,
    trace_row,
    weight,
    fetched,
    source_send,
    source_recv,
    u_send,
    u_recv,
    f_send,
    f_recv,
    edge_send,
    edge_recv,
    first_send,
    first_recv,
    share_send,
    share_recv,
):
    slice_index = lax.axis_index("tm")
    me = lax.axis_index("frac")
    plane = slice_index // GROUP
    column = slice_index % GROUP
    odd = plane % 2
    handed = odd * ((plane < planes - 1).astype(jnp.int32) + (plane < planes - 2).astype(jnp.int32))
    others = sorted(range(1, peers), key=lambda d: -min(d, peers - d))

    pairs = (
        (source_hbm, source_ref),
        (pressure_hbm, pressure_ref),
        (storage_hbm, storage_ref),
        (perm_hbm, perm_ref),
        (leak_hbm, leak_ref),
        (export_hbm, export_ref),
        (local_hbm, local_ref),
        (trace_hbm, trace_ref),
        (trans_hbm, trans_ref),
        (count_hbm, count_ref),
    )
    fetches = [
        pltpu.make_async_copy(origin, target, fetched.at[n])
        for n, (origin, target) in enumerate(pairs)
    ]
    for fetch in fetches:
        fetch.start()

    barrier = pltpu.get_barrier_semaphore()
    for d in others:
        pl.semaphore_signal(
            barrier, inc=1, device_id={"tm": slice_index, "frac": (me + d) % peers}
        )
    for d in range(1, GROUP):
        pl.semaphore_signal(
            barrier,
            inc=1,
            device_id={"tm": plane * GROUP + (column + d) % GROUP, "frac": me},
        )

    @pl.when(odd == 1)
    def _():
        for x in range(GROUP):
            pl.semaphore_signal(
                barrier, inc=1, device_id={"tm": (plane - 1) * GROUP + x, "frac": me}
            )

    @pl.when(plane > 1)
    def _():
        pl.semaphore_signal(
            barrier, inc=1, device_id={"tm": slice_index - (1 + odd) * GROUP, "frac": me}
        )

    fetches[0].wait()
    for f in range(GROUP):
        for r in range(4):
            own_source[f, r] = source_ref[pl.ds(f * 32 + r, 8, stride=4), :]

    pl.semaphore_wait(barrier, peers - 1 + GROUP - 1 + (1 - odd) * GROUP + handed)

    def source_copy(ahead, target):
        slot = (1 - ahead) * GROUP + column
        return pltpu.make_async_remote_copy(
            src_ref=own_source.at[target],
            dst_ref=source_in.at[slot],
            send_sem=source_send.at[ahead, target],
            recv_sem=source_recv.at[slot],
            device_id={"tm": (plane + ahead) * GROUP + target, "frac": me},
        )

    def source_arrival(slot):
        return pltpu.make_async_remote_copy(
            src_ref=own_source.at[0],
            dst_ref=source_in.at[slot],
            send_sem=source_send.at[0, 0],
            recv_sem=source_recv.at[slot],
            device_id={"tm": plane * GROUP + (column + 1) % GROUP, "frac": me},
        )

    def u_copy(k, target):
        return pltpu.make_async_remote_copy(
            src_ref=u_out.at[k, target],
            dst_ref=u_in.at[k, column],
            send_sem=u_send.at[k, target],
            recv_sem=u_recv.at[k, column],
            device_id={"tm": plane * GROUP + target, "frac": me},
        )

    def u_arrival(k, origin):
        return pltpu.make_async_remote_copy(
            src_ref=u_out.at[k, origin],
            dst_ref=u_in.at[k, origin],
            send_sem=u_send.at[k, origin],
            recv_sem=u_recv.at[k, origin],
            device_id={"tm": plane * GROUP + origin, "frac": me},
        )

    def f_copy(k, ahead, target):
        slot = (1 - ahead) * GROUP + column
        return pltpu.make_async_remote_copy(
            src_ref=f_out.at[k, target],
            dst_ref=f_in.at[k, slot],
            send_sem=f_send.at[k, ahead, target],
            recv_sem=f_recv.at[k, slot],
            device_id={"tm": (plane + ahead) * GROUP + target, "frac": me},
        )

    def f_arrival(k, slot):
        return pltpu.make_async_remote_copy(
            src_ref=f_out.at[k, 0],
            dst_ref=f_in.at[k, slot],
            send_sem=f_send.at[k, 0, 0],
            recv_sem=f_recv.at[k, slot],
            device_id={"tm": plane * GROUP + (column + 1) % GROUP, "frac": me},
        )

    def edge_copy(k, ahead):
        return pltpu.make_async_remote_copy(
            src_ref=edge_out.at[k],
            dst_ref=edge_in.at[k],
            send_sem=edge_send.at[k, ahead - 1],
            recv_sem=edge_recv.at[k],
            device_id={"tm": slice_index + ahead * GROUP, "frac": me},
        )

    def edge_arrival(k):
        return pltpu.make_async_remote_copy(
            src_ref=edge_out.at[k],
            dst_ref=edge_in.at[k],
            send_sem=edge_send.at[k, 0],
            recv_sem=edge_recv.at[k],
            device_id={"tm": slice_index - GROUP, "frac": me},
        )

    def first_copy(k, target, peer):
        return pltpu.make_async_remote_copy(
            src_ref=first_out.at[k, target],
            dst_ref=first_in.at[k, column * peers + me],
            send_sem=first_send.at[k],
            recv_sem=first_recv.at[k],
            device_id={"tm": plane * GROUP + target, "frac": peer},
        )

    def first_all(k):
        return pltpu.make_async_remote_copy(
            src_ref=first_in.at[k, pl.ds(0, GROUP * peers - 1)],
            dst_ref=first_in.at[k, pl.ds(0, GROUP * peers - 1)],
            send_sem=first_send.at[k],
            recv_sem=first_recv.at[k],
            device_id={"tm": slice_index, "frac": (me + 1) % peers},
        )

    def share_copy(m, target):
        return pltpu.make_async_remote_copy(
            src_ref=shared.at[m, me],
            dst_ref=shared.at[m, me],
            send_sem=share_send.at[m],
            recv_sem=share_recv.at[m],
            device_id={"tm": slice_index, "frac": target},
        )

    def share_all(m):
        return pltpu.make_async_remote_copy(
            src_ref=shared.at[m, pl.ds(0, peers - 1)],
            dst_ref=shared.at[m, pl.ds(0, peers - 1)],
            send_sem=share_send.at[m],
            recv_sem=share_recv.at[m],
            device_id={"tm": slice_index, "frac": (me + 1) % peers},
        )

    @pl.when(odd == 0)
    def _():
        for d in (2, 1, 3, 0):
            source_copy(1, (column + d) % GROUP).start()

    for d in (2, 1, 3):
        source_copy(0, (column + d) % GROUP).start()
    source_in[GROUP + column] = own_source[column]

    for fetch in fetches[1:]:
        fetch.wait()

    for f in range(GROUP):
        for r in range(4):
            rows = pl.ds(f * 32 + r, 8, stride=4)
            start[f, r] = pressure_ref[rows, :]
            store[f, r] = storage_ref[rows, :]
            perm[f, r] = perm_ref[rows, :]
            leak[f, r] = leak_ref[rows, :]

    sub8 = lax.broadcasted_iota(jnp.int32, (8, 128), 0)
    lane8 = lax.broadcasted_iota(jnp.int32, (8, 128), 1)
    for g in range(2):
        cell = jnp.broadcast_to(export_ref[g : g + 1, :], (8, 128))
        row = (cell >> 7) & 31
        export_lane[g] = cell & 127
        export_code[g] = jnp.where((row >> 2) == sub8, (cell >> 12) * 4 + (row & 3), -1)
        fine_lane[g] = ((cell >> 12) & 1) * 64 + ((cell & 127) >> 1)
        number = (cell >> 13) * 8 + (cell & 1) * 4 + (row & 3)
        fine_code[g] = jnp.where((row >> 2) == sub8, number, -1)
    slot = trace_ref[...]
    trace_lane[...] = slot & 127
    trace_row[...] = slot >> 7
    live = (sub8 * 128 + lane8) < count_ref[0]
    weight[...] = jnp.where(live, trans_ref[...], 0.0)
    cell = local_ref[...]
    cell_row = (cell >> 7) & 31
    code = (cell & 1) * 32 + (cell_row & 3) * 8 + (cell_row >> 2)
    cell_column = (cell >> 13) * 128 + ((cell >> 12) & 1) * 64 + ((cell & 127) >> 1)
    number = lax.broadcasted_iota(jnp.int32, (64, 128), 0)
    column_number = lax.broadcasted_iota(jnp.int32, (256, 128), 0)
    for t in range(8):
        rows_t = jnp.broadcast_to(code[t : t + 1, :], (64, 128))
        row_hot[:, t * 128 : (t + 1) * 128] = jnp.where(rows_t == number, 1.0, 0.0).astype(
            jnp.bfloat16
        )
        columns_t = jnp.broadcast_to(cell_column[t : t + 1, :], (256, 128))
        hot = jnp.where(columns_t == column_number, 1.0, 0.0)
        lane_hot[t * 128 : (t + 1) * 128, :] = hot.T.astype(jnp.bfloat16)

    def scatter(parts):
        rows = []
        for part in parts:
            line = jnp.concatenate([part[t : t + 1, :] for t in range(8)], axis=1)
            line = jnp.broadcast_to(line, (16, 1024)).astype(jnp.bfloat16)
            rows.append((row_hot[...].reshape(4, 16, 1024) * line[None]).reshape(64, 1024))
        left = jnp.concatenate(rows, axis=0)
        total = jnp.dot(left, lane_hot[...], preferred_element_type=jnp.float32)
        result = total[:64]
        for n in range(1, len(parts)):
            result = result + total[n * 64 : (n + 1) * 64]
        halves = [result[:, h * 128 : (h + 1) * 128].reshape(1, 2, 4, 8, 128) for h in (0, 1)]
        return jnp.concatenate(halves, axis=0)

    def terms(value, number_of):
        parts = []
        for _ in range(number_of):
            part = value.astype(jnp.bfloat16).astype(jnp.float32)
            parts.append(part)
            value = value - part
        return parts

    rate = pack(store[...]) * (1.0 / fine_size)
    fine_store[...] = rate
    fine_perm[...] = pack(perm[...])
    fine_leak[...] = rate + pack(leak[...]) + scatter(terms(weight[...], 3))
    fine_source[...] = pack(own_source[...])


    def exports(tables, lanes, codes):
        found = jnp.zeros((8, 128), jnp.float32)
        for n, table in enumerate(tables):
            found = jnp.where(codes == n, pick(table, lanes), found)
        return jnp.sum(found, axis=0, keepdims=True)

    def announce(k):
        for j in range(GROUP):
            u = u_out[k, j]
            for g in range(2):
                first_out[k, j, g : g + 1, :] = exports(
                    [u[r] for r in range(4)], export_lane[g], export_code[g] - 4 * column
                )

        for d in others:
            for j in range(GROUP):
                first_copy(k, j, (me + d) % peers).start()
        for d in range(1, GROUP):
            first_copy(k, (column + d) % GROUP, me).start()
        first_in[k, column * peers + me] = first_out[k, column]

    def advance(k, first, slot, u):
        following = coarse(u, source_in[slot], store[column], perm[column], leak[column])
        if first:
            u = following
        else:
            u = following + (f_in[k - 1, slot] - coarse_old[slot])
        coarse_old[slot] = following
        return u

    def arrival(k, first, slot):
        if first:
            source_arrival(slot).wait_recv()
        else:
            f_arrival(k - 1, slot).wait_recv()

    def chain(k, first):
        @pl.when(plane > 1)
        def _():
            edge_arrival(k).wait_recv()

        @pl.when(plane <= 1)
        def _():
            edge_in[k] = start[column]

        @pl.when(odd == 1)
        def _():
            u = edge_in[k]
            for j in range(GROUP):
                arrival(k, first, j)
                u = advance(k, first, j, u)
            edge_in[k] = u

        u = edge_in[k]
        for j in range(GROUP):
            u_out[k, j] = u

            @pl.when(column != j)
            def _():
                u_copy(k, j).start()
                arrival(k, first, GROUP + j)

            u = advance(k, first, GROUP + j, u)
        edge_out[k] = u

        @pl.when((odd == 1) & (plane < planes - 2))
        def _():
            edge_copy(k, 2).start()
            edge_copy(k, 1).start()

        if first:
            announce(k)
        else:

            @pl.when(k < ITERS)
            def _():
                announce(k)

        u_in[k, column] = u_out[k, column]
        for d in range(1, GROUP):
            u_arrival(k, (column + d) % GROUP).wait_recv()

    def fine(k):
        field[...] = pack(u_in[k])

        def step(t, carry):
            m = k * (FINE_STEPS - 1) + t - 1
            q = field[...]

            @pl.when(t > 0)
            def _():
                for g in range(2):
                    tables = [q[n // 8, (n // 4) % 2, n % 4] for n in range(16)]
                    shared[m, me, g : g + 1, :] = exports(tables, fine_lane[g], fine_code[g])
                for d in others:
                    share_copy(m, (me + d) % peers).start()

            parts = packed_faces(q, fine_perm[...])
            total = fine_leak[...] + (parts[0] + parts[1]) + (parts[2] + parts[3])
            inverse = 1.0 / total
            base = (fine_store[...] * q + fine_source[...]) * inverse
            weights = [part * inverse for part in parts]

            @pl.when(t > 0)
            def _():
                share_all(m).wait_recv()
                gathered[...] = shared[m]

            @pl.when(t == 0)
            def _():
                first_all(k).wait_recv()
                total = first_in[k, 0:peers]
                for f in range(1, GROUP):
                    total = total + first_in[k, f * peers : (f + 1) * peers]
                gathered[...] = total

            rows = trace_row[...]
            lanes = trace_lane[...]
            value = jnp.zeros((8, 128), jnp.float32)
            for n in range(2 * peers):
                line = jnp.broadcast_to(gathered[n // 2, n % 2 : n % 2 + 1, :], (8, 128))
                value = jnp.where(rows == n, pick(line, lanes), value)
            base = base + scatter(terms(weight[...] * value, 2)) * inverse
            v = q
            for _ in range(SWEEPS):
                v = packed_sweep(v, base, weights)
            field[...] = v
            return carry

        lax.fori_loop(0, FINE_STEPS, step, 0)
        f_out[k] = unpack(field[...])

        @pl.when(odd == 0)
        def _():
            for d in (2, 1, 3, 0):
                f_copy(k, 1, (column + d) % GROUP).start()

        for d in (2, 1, 3):
            f_copy(k, 0, (column + d) % GROUP).start()
        f_in[k, GROUP + column] = f_out[k, column]

    chain(0, True)

    def iteration(k, carry):
        fine(k)
        chain(k + 1, False)
        return carry

    lax.fori_loop(0, ITERS, iteration, 0)

    for f in range(GROUP):
        for r in range(4):
            out_ref[pl.ds(f * 32 + r, 8, stride=4), :] = u_in[ITERS, f, r]

    for d in range(1, GROUP):
        other = (column + d) % GROUP
        source_copy(0, other).wait_send()
        for k in range(ITERS + 1):
            u_copy(k, other).wait_send()
        for k in range(ITERS):
            f_copy(k, 0, other).wait_send()

    @pl.when(odd == 0)
    def _():
        for f in range(GROUP):
            source_copy(1, f).wait_send()
            for k in range(ITERS):
                f_copy(k, 1, f).wait_send()

    @pl.when((odd == 1) & (plane < planes - 2))
    def _():
        for k in range(ITERS + 1):
            for ahead in (1, 2):
                edge_copy(k, ahead).wait_send()

    for k in range(ITERS):
        first_all(k).wait_send()
    for m in range(ITERS * (FINE_STEPS - 1)):
        share_all(m).wait_send()


def body(
    pressure0,
    storage,
    perm_base,
    leakoff,
    sources,
    export_cells,
    inter_local,
    trace_source,
    inter_trans,
    inter_count,
):
    planes = lax.axis_size("tm") // GROUP
    peers = lax.axis_size("frac")
    flat = lambda a: a.reshape(128, 128)
    vmem = pl.BlockSpec(memory_space=pltpu.VMEM)
    f32 = jnp.float32
    block = (4, 8, 128)
    whole = (GROUP,) + block
    packed = (GROUP // 2, 2) + block
    shares = ITERS * (FINE_STEPS - 1)
    slots = 2 * GROUP
    out = pl.pallas_call(
        functools.partial(kernel, planes, peers),
        out_shape=jax.ShapeDtypeStruct((128, 128), f32),
        in_specs=[pl.BlockSpec(memory_space=pl.ANY)] * 10,
        out_specs=vmem,
        scratch_shapes=[
            pltpu.SMEM((1,), jnp.int32),
            pltpu.VMEM((128, 128), f32),
            pltpu.VMEM((128, 128), f32),
            pltpu.VMEM((128, 128), f32),
            pltpu.VMEM((128, 128), f32),
            pltpu.VMEM((128, 128), f32),
            pltpu.VMEM((2, 128), jnp.int32),
            pltpu.VMEM((8, 128), jnp.int32),
            pltpu.VMEM((8, 128), jnp.int32),
            pltpu.VMEM((8, 128), f32),
            pltpu.VMEM(whole, f32),
            pltpu.VMEM(whole, f32),
            pltpu.VMEM(whole, f32),
            pltpu.VMEM(whole, f32),
            pltpu.VMEM(packed, f32),
            pltpu.VMEM(packed, f32),
            pltpu.VMEM(packed, f32),
            pltpu.VMEM(packed, f32),
            pltpu.VMEM(whole, f32),
            pltpu.VMEM((slots,) + block, f32),
            pltpu.VMEM((ITERS + 1,) + whole, f32),
            pltpu.VMEM((ITERS + 1,) + whole, f32),
            pltpu.VMEM((ITERS,) + whole, f32),
            pltpu.VMEM((ITERS, slots) + block, f32),
            pltpu.VMEM((ITERS + 1,) + block, f32),
            pltpu.VMEM((ITERS + 1,) + block, f32),
            pltpu.VMEM((slots,) + block, f32),
            pltpu.VMEM((ITERS, GROUP, 2, 128), f32),
            pltpu.VMEM((ITERS, GROUP * peers, 2, 128), f32),
            pltpu.VMEM((shares, peers, 2, 128), f32),
            pltpu.VMEM((peers, 2, 128), f32),
            pltpu.VMEM(packed, f32),
            pltpu.VMEM((64, 1024), jnp.bfloat16),
            pltpu.VMEM((1024, 256), jnp.bfloat16),
            pltpu.VMEM((2, 8, 128), jnp.int32),
            pltpu.VMEM((2, 8, 128), jnp.int32),
            pltpu.VMEM((2, 8, 128), jnp.int32),
            pltpu.VMEM((2, 8, 128), jnp.int32),
            pltpu.VMEM((8, 128), jnp.int32),
            pltpu.VMEM((8, 128), jnp.int32),
            pltpu.VMEM((8, 128), f32),
            pltpu.SemaphoreType.DMA((10,)),
            pltpu.SemaphoreType.DMA((2, GROUP)),
            pltpu.SemaphoreType.DMA((slots,)),
            pltpu.SemaphoreType.DMA((ITERS + 1, GROUP)),
            pltpu.SemaphoreType.DMA((ITERS + 1, GROUP)),
            pltpu.SemaphoreType.DMA((ITERS, 2, GROUP)),
            pltpu.SemaphoreType.DMA((ITERS, slots)),
            pltpu.SemaphoreType.DMA((ITERS + 1, 2)),
            pltpu.SemaphoreType.DMA((ITERS + 1,)),
            pltpu.SemaphoreType.DMA((ITERS,)),
            pltpu.SemaphoreType.DMA((ITERS,)),
            pltpu.SemaphoreType.DMA((shares,)),
            pltpu.SemaphoreType.DMA((shares,)),
        ],
        compiler_params=pltpu.CompilerParams(
            collective_id=0, has_side_effects=True
        ),
        name="parareal",
    )(
        inter_count,
        flat(pressure0),
        flat(storage),
        flat(perm_base),
        flat(leakoff),
        flat(sources),
        export_cells.reshape(2, 128),
        inter_local.reshape(8, 128),
        trace_source.reshape(8, 128),
        inter_trans.reshape(8, 128),
    )
    return out.reshape(sources.shape)


def solution(mesh):
    placed = (
        P("frac", None, None),
        P("frac", None, None),
        P("frac", None, None),
        P("frac", None, None),
        P("tm", "frac", None, None),
        P("frac"),
        P("frac"),
        P("frac"),
        P("frac"),
        P("frac"),
    )
    return jax.shard_map(
        body, mesh=mesh, in_specs=placed, out_specs=P("tm", "frac", None, None), check_vma=False
    )
```
